32 devices in a mesh: grp: 2 (over y), pool: 4 (over z), tp: 2 (over x), sub: 2 (over core).
Axes of the slice: x: 2, y: 2, z: 4, core: 2. Of those that a mesh axis runs over, the one named last changes fastest.
Arguments:
- queries: bfloat16 [128, 4096], P(('grp', 'pool', 'tp', 'sub')), parts along dimension 0, may hold values from -48 to 48
- keys_cache: bfloat16 [128, 512, 256], P(('grp', 'pool', 'tp', 'sub')), parts along dimension 0, may hold values from -6 to 6
- values_cache: bfloat16 [128, 512, 256], P(('grp', 'pool', 'tp', 'sub')), parts along dimension 0, may hold values from -6 to 6
- lengths: int32 [128], P(('grp', 'pool', 'tp', 'sub')), parts along dimension 0, may hold values from 2 to 512
- out_weight: bfloat16 [4096, 2048], P(('tp', 'sub')), may hold values from -0.75 to 0.75
- routes: int32 [128, 8], P(('grp', 'pool')), parts along dimension 0, may hold values from 0 to 63, all different within a row; in each aligned block of 16 rows (0 to 15, 16 to 31, ...) at most 14 rows name the same one
- route_weight: float32 [128, 8], P(('grp', 'pool')), parts along dimension 0, may hold values from 0.1 to 0.5
- expert_table: int32 [64], replicated, may hold values from 0 to 63, each once
- w_gate: bfloat16 [64, 768, 2048], P('pool', 'sub', 'tp'), may hold values from -0.125 to 0.125
- w_up: bfloat16 [64, 768, 2048], P('pool', 'sub', 'tp'), may hold values from -0.125 to 0.125
- w_down: bfloat16 [64, 768, 2048], P('pool', 'sub', 'tp'), may hold values from -0.875 to 0.875
Outputs:
- attended: bfloat16 [128, 2048], P(('grp', 'pool', 'tp', 'sub')), parts along dimension 0
- expert_out: bfloat16 [128, 2048], P(('grp', 'pool'), ('tp', 'sub')), parts along dimension 0
The draws below stay inside these ranges and needn't reach their ends.
There are 2 independent parts, one for each index of `grp`. The reference program is written for one: setup_inputs(seed, part) draws one part's arguments, and reference() takes and returns one part's arrays. A program takes and returns all parts, laid end to end along the dimension named above; an argument that names none is the same for every part. Nothing has to cross between parts.
Inputs may be any that keep to these rules, and one draw needn't show every extreme that they name: `routes`: in each aligned block of 16 rows (the rows of one pool index) no expert is named by more than 14 rows, and in some block one expert is named by exactly 14 rows; each row names 8 different experts. `expert_table`: a permutation of the experts.
All inputs are finite; a program needn't handle non-finite values.
Results may differ from the reference program's by a relative error of at most 0.0086.
Values may be sent and summed in bfloat16 or wider, within the bound.
No kernel may reach another device: no remote copies, remote signals or barrier semaphores. Data moves between devices by JAX's collectives and lax.ppermute only.
A program may use at most 128 MiB of HBM per device.

```python
import math
import jax
import jax.numpy as jnp
import numpy as np
from jax import lax

D = 2048
HEADS = 32
KV_HEADS = 2
HEAD_DIM = 128
EXPERTS = 64
EXPERT_FF = 768
TOP_K = 8
CACHE_LEN = 512
CAPACITY = 14
ROWS_POOL = 16
ROWS = 64
N_POOL = 4


def draw_keys_cache(key, part):
    extent = (ROWS, CACHE_LEN, KV_HEADS * HEAD_DIM)
    drawn = jnp.clip(jax.random.normal(jax.random.fold_in(key, 11), extent, jnp.float32), -6.0, 6.0)
    return drawn.astype(jnp.bfloat16)


def draw_queries(key, part):
    extent = (ROWS, HEADS * HEAD_DIM)
    drawn = jnp.clip(jax.random.normal(jax.random.fold_in(key, 23), extent, jnp.float32), -6.0, 6.0)
    return drawn.astype(jnp.bfloat16)


def draw_lengths(key, part):
    drawn = jax.random.randint(jax.random.fold_in(key, 31), (ROWS,), 2, CACHE_LEN + 1, jnp.int32)
    return drawn.at[0].set(CACHE_LEN)


def shard_levels(rng, shape, cuts, smallest, largest):
    def one(axis_at, parts):
        draws = jax.random.uniform(jax.random.fold_in(jax.random.fold_in(rng, 6), axis_at), (parts,), jnp.float32, smallest / len(cuts), largest / len(cuts))
        return jnp.repeat(jnp.exp(draws), shape[axis_at] // parts).reshape((-1,) + (1,) * (len(shape) - axis_at - 1))

    gain = one(*cuts[0])
    for cut in cuts[1:]:
        gain = gain * one(*cut)
    return gain


def routed_block(stream_key, own, number, rows, count, top, limit, slope):
    ranking = jax.random.permutation(stream_key, count)
    packed, usual = portions_of(count, rows * top, limit, slope, True), portions_of(count, rows * top, limit, slope, False)
    places = jnp.arange(count)

    def named(sizes, rotation):
        used = int((sizes > 0).sum())
        fixed = max(1, used // 4)
        passed = fixed + (places - fixed + rotation * (used - fixed)) % max(1, count - fixed)
        return jnp.zeros((count,), jnp.int32).at[ranking[jnp.where(places < fixed, places, passed)]].set(jnp.asarray(sizes, jnp.int32))

    sizes = jnp.where(number % 4 == 0, named(packed, number // 4), named(usual, number - number // 4 - 1))
    mixed = jax.random.permutation(jax.random.fold_in(own, 3), count)
    donor, receiver = mixed[0:count // 2 * 2:2], mixed[1:count // 2 * 2:2]
    slack = jnp.minimum(sizes[donor] - 1, limit - sizes[receiver]) // 2
    slack = jnp.where((donor == ranking[0]) | (receiver == ranking[0]) | (sizes[receiver] == 0), 0, jnp.maximum(slack, 0))
    passed = jax.random.randint(jax.random.fold_in(own, 4), (count // 2,), 0, 1 << 20) % (slack + 1)
    sizes = sizes.at[donor].add(-passed).at[receiver].add(passed)
    members = jnp.searchsorted(jnp.cumsum(sizes), jnp.arange(rows * top), side="right").astype(jnp.int32)
    grid = members.reshape(top, rows).T
    grid = grid[jax.random.permutation(jax.random.fold_in(own, 1), rows)]
    rotation = jax.random.randint(jax.random.fold_in(own, 2), (rows, 1), 0, top)
    return jnp.take_along_axis(grid, (jnp.arange(top)[None, :] + rotation) % top, axis=1)


def portions_of(number_of, total, bound, skew, full):
    portions = [(1 << 20) // math.isqrt(grade ** skew) + 1 for grade in range(1, number_of + 1)]
    largest = bound if full else min(bound, max(-(-total // number_of), total * portions[0] // sum(portions)))
    least = 1 if total - largest >= number_of - 1 else 0
    counts, rest = [largest] + [least] * (number_of - 1), total - largest - least * (number_of - 1)
    while rest > 0:
        movable = [i for i in range(1, number_of) if counts[i] < largest] or [i for i in range(1, number_of) if counts[i] < bound]
        pool, budget = sum([portions[i] for i in movable]), rest
        for i in movable:
            more = min(bound - counts[i], max(1, budget * portions[i] // pool), rest)
            counts[i] = counts[i] + more
            rest = rest - more
    return np.array(counts)


def normal_values(stream_key, shape, deviation, bound, pieces=(), dtype=jnp.bfloat16):
    factor_of = shard_levels(stream_key, shape, pieces, -0.22, 0.18) if pieces else 1.0
    entries = jax.random.normal(stream_key, shape, jnp.float32) * deviation * factor_of
    return jnp.minimum(jnp.maximum(entries, -bound), bound).astype(dtype)


def setup_inputs(seed: int = 0, part: int = 0) -> dict:
    arg_keys = jax.random.split(jax.random.key(seed), 12)
    part_splits = jax.random.split(jax.random.fold_in(arg_keys[11], part), 12)
    queries = draw_queries(jax.random.fold_in(jax.random.fold_in(arg_keys[11], part), 71), part)
    keys_cache = draw_keys_cache(jax.random.fold_in(jax.random.fold_in(arg_keys[11], part), 71), part)
    values_cache = normal_values(part_splits[2], (ROWS, CACHE_LEN, KV_HEADS * HEAD_DIM), 1.0, 6.0, ((0, 16),))
    lengths = draw_lengths(jax.random.fold_in(jax.random.fold_in(arg_keys[11], part), 71), part)
    out_weight = normal_values(arg_keys[4], (HEADS * HEAD_DIM, D), 64 ** -0.5, 0.75, ((0, 4),))
    routes_keys = jax.random.split(jax.random.fold_in(part_splits[5], 1), ROWS // ROWS_POOL)
    routes_turns = jax.random.permutation(jax.random.fold_in(part_splits[5], 3), ROWS // ROWS_POOL)
    routes = jax.vmap(lambda own, number: routed_block(jax.random.fold_in(part_splits[5], 2), own, number, ROWS_POOL, EXPERTS, TOP_K, CAPACITY, 2))(routes_keys, routes_turns).reshape((ROWS, TOP_K))
    route_weight = jnp.clip(0.1 + 0.4 * jax.random.uniform(part_splits[6], (ROWS, TOP_K), jnp.float32) ** shard_levels(part_splits[6], (ROWS, TOP_K), ((0, 4),), -0.2, 0.2), 0.1, 0.5)
    expert_table = jax.random.permutation(arg_keys[7], EXPERTS).astype(jnp.int32)
    w_gate = normal_values(arg_keys[8], (EXPERTS, EXPERT_FF, D), D ** -0.5, 0.125, ((0, 4), (1, 2), (2, 2)))
    w_up = normal_values(arg_keys[9], (EXPERTS, EXPERT_FF, D), D ** -0.5, 0.125, ((0, 4), (1, 2), (2, 2)))
    w_down = normal_values(arg_keys[10], (EXPERTS, EXPERT_FF, D), (EXPERT_FF // 16) ** -0.5, 0.875, ((0, 4), (1, 2), (2, 2)))
    return {"queries": queries, "keys_cache": keys_cache, "values_cache": values_cache, "lengths": lengths, "out_weight": out_weight, "routes": routes, "route_weight": route_weight, "expert_table": expert_table, "w_gate": w_gate, "w_up": w_up, "w_down": w_down}


def reference(queries, keys_cache, values_cache, lengths, out_weight, routes, route_weight, expert_table, w_gate, w_up, w_down):
    row_count = queries.shape[0]
    group_size = HEADS // KV_HEADS
    query_four = queries.astype(jnp.float32).reshape(row_count, KV_HEADS, group_size, HEAD_DIM)
    key_four = keys_cache.astype(jnp.float32).reshape(row_count, CACHE_LEN, KV_HEADS, HEAD_DIM)
    value_four = values_cache.astype(jnp.float32).reshape(row_count, CACHE_LEN, KV_HEADS, HEAD_DIM)
    scores = jnp.einsum('rkgd,rlkd->rkgl', query_four, key_four, precision=lax.Precision.HIGHEST) * (1.0 / math.sqrt(HEAD_DIM))
    in_range = (lax.iota(jnp.int32, CACHE_LEN)[None, :] < lengths[:, None])[:, None, None, :]
    masked = jnp.where(in_range, scores, -jnp.inf)
    row_max = lax.optimization_barrier(jnp.max(masked, axis=3, keepdims=True))
    exp_terms = jnp.where(in_range, jnp.exp(masked - row_max), 0.0)
    exp_sum = lax.optimization_barrier(jnp.sum(exp_terms, axis=3))
    weights = exp_terms.astype(jnp.bfloat16).astype(jnp.float32)
    weighted = jnp.einsum('rkgl,rlkd->rkgd', weights, value_four, precision=lax.Precision.HIGHEST)
    attention = (weighted / exp_sum[..., None]).reshape(row_count, HEADS * HEAD_DIM).astype(jnp.bfloat16)
    attended = jnp.dot(attention, out_weight, preferred_element_type=jnp.float32).astype(jnp.bfloat16)
    pair_count = row_count * TOP_K
    flat_routes = routes.reshape(pair_count)
    entry_index = expert_table[flat_routes].astype(jnp.int32)
    entry_hot = (entry_index[:, None] == lax.iota(jnp.int32, EXPERTS)[None, :]).astype(jnp.int32)
    slot_rank = lax.optimization_barrier(jnp.sum((jnp.cumsum(entry_hot, axis=0) - entry_hot) * entry_hot, axis=1)).astype(jnp.int32)
    per_expert = N_POOL * CAPACITY
    slot_index = (entry_index * per_expert + slot_rank).astype(jnp.int32)
    sources = jnp.repeat(attended, TOP_K, axis=0)
    buffer_rows = jnp.zeros((EXPERTS * per_expert, D), jnp.bfloat16).at[slot_index].set(sources)

    def run_expert(operands):
        inputs, gate_rows, up_rows, down_rows = operands
        gate_value = jnp.dot(inputs, gate_rows.T, preferred_element_type=jnp.float32)
        up_value = jnp.dot(inputs, up_rows.T, preferred_element_type=jnp.float32)
        hidden = (jax.nn.silu(gate_value) * up_value).astype(jnp.bfloat16)
        return jnp.dot(hidden, down_rows, preferred_element_type=jnp.float32).astype(jnp.bfloat16)
    outputs = lax.map(run_expert, (buffer_rows.reshape(EXPERTS, per_expert, D), w_gate, w_up, w_down))
    picked = outputs.reshape(EXPERTS * per_expert, D)[slot_index].astype(jnp.float32)
    scaled = picked * route_weight.reshape(pair_count)[:, None]
    expert_out = lax.optimization_barrier(jnp.sum(scaled.reshape(row_count, TOP_K, D), axis=1)).astype(jnp.bfloat16)
    return (attended, expert_out)
```

```python
import functools
import math

import jax
import jax.numpy as jnp
from jax import lax
from jax.experimental import pallas as pl
from jax.experimental.pallas import tpu as pltpu
from jax.sharding import PartitionSpec as P

HEAD_DIM = 128
KV_HEADS = 2
CHUNK = 128
VMEM_LIMIT = 56 << 20

F32 = jnp.float32
BF16 = jnp.bfloat16


def dot_nt(a, b):
    return lax.dot_general(a, b, (((1,), (1,)), ((), ())), preferred_element_type=F32)


def dot_tn(a, b):
    return lax.dot_general(a, b, (((0,), (0,)), ((), ())), preferred_element_type=F32)


def dot_nn(a, b):
    return jnp.dot(a, b, preferred_element_type=F32)


def whole_spec(shape):
    return pl.BlockSpec(shape, lambda *_: (0,) * len(shape))


def attention_kernel(lengths, where, q_ref, k_ref, v_ref, *refs, rows, step_rows, heads, pieces):
    outs, (gathered, flat) = refs[:pieces], refs[pieces:]
    step = pl.program_id(0)
    group = heads // KV_HEADS
    positions = k_ref.shape[1]
    column = lax.broadcasted_iota(jnp.int32, (group, positions), 1)
    for r in range(step_rows):
        row = step * step_rows + r
        valid = column < lengths[row]
        for j in range(KV_HEADS):
            lanes = slice(j * HEAD_DIM, (j + 1) * HEAD_DIM)
            scores = dot_nt(q_ref[r, j * group : (j + 1) * group, :], k_ref[r, :, lanes])
            scores = jnp.where(valid, scores * (1.0 / math.sqrt(HEAD_DIM)), -1e30)
            top = jnp.max(scores, axis=1, keepdims=True)
            terms = jnp.where(valid, jnp.exp(scores - top), 0.0)
            total = jnp.sum(terms, axis=1, keepdims=True)
            value = dot_nn(terms.astype(BF16), v_ref[r, :, lanes]) / total
            gathered[row, j * group : (j + 1) * group, :] = value

    @pl.when(step == pl.num_programs(0) - 1)
    def _():
        for h in range(heads):
            flat[:, h * HEAD_DIM : (h + 1) * HEAD_DIM] = gathered[:, h, :]
        width = heads * HEAD_DIM // pieces
        for k in range(pieces):
            start = pl.multiple_of((where[0] ^ k) * width, width)
            outs[k][...] = flat[:, pl.ds(start, width)].astype(BF16)


def attend(queries, keys_cache, values_cache, lengths, where, pieces):
    rows, columns = queries.shape
    heads = columns // HEAD_DIM
    positions, kv_width = keys_cache.shape[1:]
    step_rows = 2
    width = columns // pieces
    cache = pl.BlockSpec((step_rows, positions, kv_width), lambda i, *_: (i, 0, 0))
    return pl.pallas_call(
        functools.partial(
            attention_kernel, rows=rows, step_rows=step_rows, heads=heads, pieces=pieces
        ),
        grid_spec=pltpu.PrefetchScalarGridSpec(
            num_scalar_prefetch=2,
            grid=(rows // step_rows,),
            in_specs=[
                pl.BlockSpec((step_rows, heads, HEAD_DIM), lambda i, *_: (i, 0, 0)),
                cache,
                cache,
            ],
            out_specs=[whole_spec((rows, width))] * pieces,
            scratch_shapes=[
                pltpu.VMEM((rows, heads, HEAD_DIM), F32),
                pltpu.VMEM((rows, columns), F32),
            ],
        ),
        out_shape=[jax.ShapeDtypeStruct((rows, width), BF16)] * pieces,
        compiler_params=pltpu.CompilerParams(vmem_limit_bytes=VMEM_LIMIT),
        name="attention",
    )(lengths, where, queries.reshape(rows, heads, HEAD_DIM), keys_cache, values_cache)


def project_kernel(where, *refs, sources, pieces):
    inputs, w_ref = refs[:sources], refs[sources]
    outs, (x,) = refs[sources + 1 : sources + 1 + pieces], refs[sources + 1 + pieces :]
    step = pl.program_id(0)

    @pl.when(step == 0)
    def _():
        own_rows = inputs[0].shape[0]
        count = sources * own_rows
        stacked = jnp.concatenate([ref[...].astype(F32) for ref in inputs], axis=0).astype(BF16)
        target = lax.broadcasted_iota(jnp.int32, (count, count), 0)
        origin = lax.broadcasted_iota(jnp.int32, (count, count), 1)
        order = (target ^ (where[1] * own_rows)) == origin
        x[...] = dot_nn(jnp.where(order, 1.0, 0.0).astype(BF16), stacked).astype(BF16)

    value = dot_nn(x[...], w_ref[...])
    for k in range(pieces):

        @pl.when(step == k)
        def _(k=k):
            outs[k][...] = value.astype(outs[k].dtype)


def project(inputs, out_weight, where, pieces):
    sources = len(inputs)
    own_rows, depth = inputs[0].shape
    width = out_weight.shape[1] // pieces
    count = sources * own_rows
    return pl.pallas_call(
        functools.partial(project_kernel, sources=sources, pieces=pieces),
        grid_spec=pltpu.PrefetchScalarGridSpec(
            num_scalar_prefetch=1,
            grid=(pieces,),
            in_specs=[whole_spec((own_rows, depth))] * sources
            + [pl.BlockSpec((depth, width), lambda i, where: (0, where[0] ^ i))],
            out_specs=[whole_spec((count, width))] * pieces,
            scratch_shapes=[pltpu.VMEM((count, depth), BF16)],
        ),
        out_shape=[
            jax.ShapeDtypeStruct((count, width), F32 if k == 0 else BF16) for k in range(pieces)
        ],
        compiler_params=pltpu.CompilerParams(vmem_limit_bytes=VMEM_LIMIT),
        name="project",
    )(where, *inputs, out_weight)


def gate_up_kernel(where, own_ref, other_ref, slot_ref, g_ref, u_ref, out_ref, x, total):
    step = pl.program_id(0)
    half = own_ref.shape[1]
    rows = own_ref.shape[0]
    experts, chunk, depth = g_ref.shape
    capacity = out_ref.shape[0]

    @pl.when(step == 0)
    def _():
        x[:, pl.ds(pl.multiple_of(where[2] * half, half), half)] = own_ref[...]
        x[:, pl.ds(pl.multiple_of((1 - where[2]) * half, half), half)] = other_ref[...]
        total[...] = jnp.zeros_like(total)

    gate = dot_nt(x[...], g_ref[...].reshape(experts * chunk, depth)).astype(BF16)
    up = dot_nt(x[...], u_ref[...].reshape(experts * chunk, depth)).astype(BF16)
    blocks = []
    for e in range(experts):
        lanes = slice(e * chunk, (e + 1) * chunk)
        blocks.append(jnp.concatenate([gate[:, lanes], up[:, lanes]], axis=1))
    both = jnp.concatenate(blocks, axis=0)
    place = lax.broadcasted_iota(jnp.int32, (capacity, experts * rows), 0)
    pick = jnp.where(place == slot_ref[0], 1.0, 0.0).astype(BF16)
    total[...] += dot_nn(pick, both)

    @pl.when(step == pl.num_programs(0) - 1)
    def _():
        out_ref[...] = total[...].astype(BF16)


def gate_up(own, other, slots, w_gate, w_up, where, index, group, capacity):
    rows, half = own.shape
    experts, _, depth = w_gate.shape
    weight = pl.BlockSpec((group, CHUNK, depth), lambda i, *_: (i, index, 0))
    return pl.pallas_call(
        gate_up_kernel,
        grid_spec=pltpu.PrefetchScalarGridSpec(
            num_scalar_prefetch=1,
            grid=(experts // group,),
            in_specs=[
                whole_spec((rows, half)),
                whole_spec((rows, half)),
                pl.BlockSpec((1, 1, group * rows), lambda i, *_: (i, 0, 0)),
                weight,
                weight,
            ],
            out_specs=whole_spec((capacity, 2 * CHUNK)),
            scratch_shapes=[
                pltpu.VMEM((rows, 2 * half), BF16),
                pltpu.VMEM((capacity, 2 * CHUNK), F32),
            ],
        ),
        out_shape=jax.ShapeDtypeStruct((capacity, 2 * CHUNK), BF16),
        compiler_params=pltpu.CompilerParams(vmem_limit_bytes=VMEM_LIMIT),
        name=f"gate_up_{index}",
    )(where, own, other, slots, w_gate, w_up)


def down_kernel(where, own_ref, other_ref, weight_ref, slot_ref, d_ref, *refs, pieces, carried):
    before, refs = refs[:carried], refs[carried:]
    outs, (hidden, total) = refs[:-2], refs[-2:]
    step = pl.program_id(0)
    experts, chunk, depth = d_ref.shape
    capacity = own_ref.shape[0]
    rows = total.shape[0]

    @pl.when(step == 0)
    def _():
        both = own_ref[...].astype(F32) + other_ref[...].astype(F32)
        gate, up = both[:, :chunk], both[:, chunk:]
        value = gate / (1.0 + jnp.exp(-gate)) * up * weight_ref[...]
        hidden[...] = value.astype(BF16)
        if carried:
            total[...] = before[0][...]
        else:
            total[...] = jnp.zeros_like(total)

    place = lax.broadcasted_iota(jnp.int32, (capacity, experts * rows), 0)
    pick = jnp.where(place == slot_ref[0], 1.0, 0.0).astype(BF16)
    spread = dot_tn(pick, hidden[...]).astype(BF16)
    left = jnp.concatenate([spread[e * rows : (e + 1) * rows] for e in range(experts)], axis=1)
    total[...] += dot_nn(left, d_ref[...].reshape(experts * chunk, depth))

    @pl.when(step == pl.num_programs(0) - 1)
    def _():
        if pieces == 1:
            outs[0][...] = total[...]
        else:
            count, width = outs[0].shape
            for k in range(pieces):
                row = pl.multiple_of((where[3] ^ (k >> 1)) * count, count)
                lane = pl.multiple_of((where[2] ^ (k & 1)) * width, width)
                outs[k][...] = total[pl.ds(row, count), pl.ds(lane, width)].astype(outs[k].dtype)


def down(own, other, slot_weight, slots, w_down, before, where, index, group, rows, pieces):
    experts, _, depth = w_down.shape
    capacity = own.shape[0]
    if pieces == 1:
        out_shape = [jax.ShapeDtypeStruct((rows, depth), F32)]
    else:
        shape = (rows * 2 // pieces, depth // 2)
        out_shape = [jax.ShapeDtypeStruct(shape, F32 if k == 0 else BF16) for k in range(pieces)]
    carried = [] if before is None else [before]
    return pl.pallas_call(
        functools.partial(down_kernel, pieces=pieces, carried=len(carried)),
        grid_spec=pltpu.PrefetchScalarGridSpec(
            num_scalar_prefetch=1,
            grid=(experts // group,),
            in_specs=[
                whole_spec((capacity, 2 * CHUNK)),
                whole_spec((capacity, 2 * CHUNK)),
                whole_spec((capacity, 1)),
                pl.BlockSpec((1, 1, group * rows), lambda i, *_: (i, 0, 0)),
                pl.BlockSpec((group, CHUNK, depth), lambda i, *_: (i, index, 0)),
            ]
            + [whole_spec((rows, depth))] * len(carried),
            out_specs=[whole_spec(leaf.shape) for leaf in out_shape],
            scratch_shapes=[
                pltpu.VMEM((capacity, CHUNK), BF16),
                pltpu.VMEM((rows, depth), F32),
            ],
        ),
        out_shape=out_shape,
        compiler_params=pltpu.CompilerParams(vmem_limit_bytes=VMEM_LIMIT),
        name=f"down_{index}",
    )(where, own, other, slot_weight, slots, w_down, *carried)


def xor_permute(value, axes, count, k):
    return lax.ppermute(value, axes, [(i, i ^ k) for i in range(count)])


def body(
    queries,
    keys_cache,
    values_cache,
    lengths,
    out_weight,
    routes,
    route_weight,
    expert_table,
    w_gate,
    w_up,
    w_down,
):
    pools, tps, subs = lax.axis_size("pool"), lax.axis_size("tp"), lax.axis_size("sub")
    pool, tp, sub = lax.axis_index("pool"), lax.axis_index("tp"), lax.axis_index("sub")
    shards = tps * subs
    shard = tp * subs + sub
    direct = tps == 2 and subs == 2 and pools == 4
    own_rows = queries.shape[0]
    pool_rows = own_rows * shards
    rows = pool_rows * pools
    experts, hidden_units, half_width = w_gate.shape
    quarter = half_width // subs
    top = routes.shape[1]
    where = jnp.stack([shard, pool * shards + shard, sub, pool]).astype(jnp.int32)

    facts = jnp.concatenate([routes.astype(F32), route_weight], axis=1)
    if direct:
        blocks = [facts] + [xor_permute(facts, "pool", pools, k) for k in range(1, pools)]
        stacked = jnp.stack(blocks)
        order = lax.iota(jnp.int32, pools) ^ pool
        hot = order[:, None] == lax.iota(jnp.int32, pools)[None, :]
        facts = jnp.sum(jnp.where(hot[:, :, None, None], stacked[None], 0.0), axis=1)
        facts = facts.reshape(rows, 2 * top)
    else:
        facts = lax.all_gather(facts, "pool", axis=0, tiled=True)
    all_routes = facts[:, :top].astype(jnp.int32)
    all_weights = facts[:, top:]
    total_experts = expert_table.shape[0]
    ids = lax.iota(jnp.int32, total_experts)
    entry = jnp.sum(
        jnp.where(all_routes[:, :, None] == ids[None, None, :], expert_table[None, None, :], 0),
        axis=2,
    )
    loads = jnp.sum(
        (entry // experts)[:, :, None] == lax.iota(jnp.int32, pools)[None, None, :],
        axis=(0, 1),
        dtype=jnp.int32,
    )
    largest = jnp.max(loads)
    capacity = -(-rows * top * 13 // (8 * pools * 16)) * 16
    group = max(1, min(experts, 256 // rows))
    groups = experts // group
    local = entry - pool * experts
    expert_of = lax.iota(jnp.int32, experts)
    chosen = local.T[:, None, :] == expert_of[None, :, None]
    mask = jnp.any(chosen, axis=0).reshape(groups, group * rows)
    pair_weight = jnp.sum(jnp.where(chosen, all_weights.T[:, None, :], 0.0), axis=0)
    pair_weight = pair_weight.reshape(1, experts * rows)
    lane = lax.iota(jnp.int32, group * rows)
    before = (lane[:, None] < lane[None, :]).astype(BF16)
    rank = jnp.dot(mask.astype(BF16), before, preferred_element_type=F32).astype(jnp.int32)
    counts = jnp.sum(mask, axis=1, dtype=jnp.int32)
    base = jnp.cumsum(counts) - counts
    slots = jnp.where(mask, rank + base[:, None], -1).reshape(groups, 1, group * rows)

    if direct:
        pieces = attend(queries, keys_cache, values_cache, lengths, where, shards)
        part = pools * shards
        axes = ("pool", "tp", "sub")
        inputs = [
            pieces[k % shards] if k == 0 else xor_permute(pieces[k % shards], axes, part, k)
            for k in range(part)
        ]
        sums = project(inputs, out_weight, where, shards)
        x_sum = sums[0]
        for k in range(1, shards):
            x_sum = x_sum + xor_permute(sums[k], ("tp", "sub"), shards, k).astype(F32)
        own_x = x_sum.astype(BF16)
    else:
        attention = attend(queries, keys_cache, values_cache, lengths, where * 0, 1)[0]
        head_rows = lax.all_to_all(
            attention, ("tp", "sub"), split_axis=1, concat_axis=0, tiled=True
        )
        partial = jnp.dot(head_rows, out_weight, preferred_element_type=F32)
        x_sum = lax.psum_scatter(partial, ("tp", "sub"), scatter_dimension=1, tiled=True)
        own_x = lax.all_gather(x_sum.astype(BF16), "pool", axis=0, tiled=True)
    other_x = xor_permute(own_x, "sub", subs, 1)

    if direct:
        first = jnp.where(sub == 0, own_x, other_x)
        second = jnp.where(sub == 0, other_x, own_x)
        x_half = jnp.concatenate([first, second], axis=1)
        start = pool * pool_rows + (shard ^ subs) * own_rows
        theirs = lax.ppermute(
            lax.dynamic_slice_in_dim(x_half, start, own_rows, 0), "tp", [(0, 1), (1, 0)]
        )
        start = pool * pool_rows + shard * own_rows
        mine = lax.dynamic_slice_in_dim(x_half, start, own_rows, 0)
        attended = jnp.where(
            tp == 0,
            jnp.concatenate([mine, theirs], axis=1),
            jnp.concatenate([theirs, mine], axis=1),
        )
    else:
        pool_x = lax.dynamic_slice_in_dim(own_x, pool * pool_rows, pool_rows, 0)
        attended = lax.all_to_all(pool_x, ("tp", "sub"), split_axis=0, concat_axis=1, tiled=True)

    def weights_of(shifted):
        place = lax.iota(jnp.int32, capacity)[:, None]
        hit = place == shifted.reshape(1, experts * rows)
        return jnp.sum(jnp.where(hit, pair_weight, 0.0), axis=1, keepdims=True)

    def run_experts(shifted, pieces):
        slot_weight = weights_of(shifted)
        chunks = hidden_units // CHUNK
        sent = [
            gate_up(own_x, other_x, shifted, w_gate, w_up, where, c, group, capacity)
            for c in range(chunks)
        ]
        if tps == 2:
            both = [(value, lax.ppermute(value, "tp", [(0, 1), (1, 0)])) for value in sent]
        else:
            both = [
                (lax.psum(value.astype(F32), "tp").astype(BF16), jnp.zeros_like(value))
                for value in sent
            ]
        result = [None]
        for c in range(chunks):
            own, other = both[c]
            last = pieces if c == chunks - 1 else 1
            result = down(
                own,
                other,
                slot_weight,
                shifted,
                w_down,
                result[0],
                where,
                c,
                group,
                rows,
                last,
            )
        return result

    def reduce_rows(values):
        total = values[0]
        for k in range(1, len(values)):
            moved = xor_permute(values[k], ("pool", "sub"), pools * subs, k)
            total = total + moved.astype(F32)
        return total

    def finish(shifted):
        if direct:
            return reduce_rows(run_experts(shifted, pools * subs))
        value = run_experts(shifted, 1)[0]
        value = lax.psum_scatter(value, "pool", scatter_dimension=0, tiled=True)
        return lax.psum_scatter(value, "sub", scatter_dimension=1, tiled=True)

    def more(state):
        k, total = state
        return k + 1, total + finish(slots - k * capacity)

    expert_sum = finish(slots)
    _, extra = lax.while_loop(
        lambda state: state[0] * capacity < largest,
        more,
        (jnp.int32(1), jnp.zeros((pool_rows, quarter), F32)),
    )
    return attended, (expert_sum + extra).astype(BF16)


def solution(mesh):
    in_specs = (
        P(("grp", "pool", "tp", "sub"), None),
        P(("grp", "pool", "tp", "sub"), None, None),
        P(("grp", "pool", "tp", "sub"), None, None),
        P(("grp", "pool", "tp", "sub")),
        P(("tp", "sub"), None),
        P(("grp", "pool"), None),
        P(("grp", "pool"), None),
        P(),
        P("pool", "sub", "tp"),
        P("pool", "sub", "tp"),
        P("pool", "sub", "tp"),
    )
    out_specs = (P(("grp", "pool", "tp", "sub"), None), P(("grp", "pool"), ("tp", "sub")))
    return jax.shard_map(body, mesh=mesh, in_specs=in_specs, out_specs=out_specs, check_vma=False)
```

```python
import functools
import math

import jax
import jax.numpy as jnp
from jax import lax
from jax.experimental import pallas as pl
from jax.experimental.pallas import tpu as pltpu
from jax.sharding import PartitionSpec as P

HEAD_DIM = 128
KV_HEADS = 2
CHUNK = 128
VMEM_LIMIT = 16 << 20

F32 = jnp.float32
BF16 = jnp.bfloat16


def dot_nt(a, b):
    return lax.dot_general(a, b, (((1,), (1,)), ((), ())), preferred_element_type=F32)


def dot_tn(a, b):
    return lax.dot_general(a, b, (((0,), (0,)), ((), ())), preferred_element_type=F32)


def dot_nn(a, b):
    return jnp.dot(a, b, preferred_element_type=F32)


def cost(microseconds):
    return pl.CostEstimate(
        flops=0, transcendentals=0, bytes_accessed=int(microseconds * 3_000_000)
    )


VMEM = pl.BlockSpec(memory_space=pltpu.VMEM)
SMEM = pl.BlockSpec(memory_space=pltpu.SMEM)
HBM = pl.BlockSpec(memory_space=pltpu.HBM)
ANY = pl.BlockSpec(memory_space=pl.ANY)


def in_hbm(value):
    return pltpu.with_memory_space_constraint(value, pltpu.HBM)


def call(kernel, name, inputs, specs, outs, out_specs=None, scratch=(), loads=(), anchors=(), us=2):
    count_in, count_out, count_load = len(inputs), len(outs), len(loads)

    def source(ref, first):
        return ref if first is None else ref.at[:, first : first + CHUNK, :]

    def run(*refs):
        refs = list(refs)
        given = [refs.pop(0) for _ in range(count_in)]
        sources = [refs.pop(0) for _ in range(count_load)]
        del refs[: len(anchors)]
        results = [refs.pop(0) for _ in range(count_out)]
        targets = [refs.pop(0) for _ in range(count_load)]
        copies = []
        if loads:
            sems = refs.pop()
            for i, (_, first) in enumerate(loads):
                copies.append(
                    pltpu.make_async_copy(source(sources[i], first), targets[i], sems.at[i])
                )
                copies[-1].start()
        kernel(*given, *results, *refs)
        for copy in copies:
            copy.wait()

    def loaded(array, first):
        shape = array.shape if first is None else (array.shape[0], CHUNK, array.shape[2])
        return pltpu.VMEM(shape, array.dtype)

    scratch = list(scratch) + ([pltpu.SemaphoreType.DMA((count_load,))] if loads else [])
    results = pl.pallas_call(
        run,
        in_specs=list(specs) + [HBM] * count_load + [ANY] * len(anchors),
        out_specs=list(out_specs or [VMEM] * count_out) + [VMEM] * count_load,
        out_shape=list(outs) + [loaded(*leaf) for leaf in loads],
        scratch_shapes=scratch,
        compiler_params=pltpu.CompilerParams(vmem_limit_bytes=VMEM_LIMIT),
        cost_estimate=cost(us),
        name=name,
    )(*inputs, *[in_hbm(leaf[0]) for leaf in loads], *anchors)
    return list(results[:count_out]), list(results[count_out:])


def attention_kernel(lengths, where, q_ref, k_hbm, v_hbm, *refs, pieces):
    outs, (k_ref, v_ref, sems, gathered, flat) = refs[:pieces], refs[pieces:]
    rows, heads, _ = q_ref.shape
    positions = k_ref.shape[1]
    group = heads // KV_HEADS
    copies = []
    for row in range(rows):
        pair = [
            pltpu.make_async_copy(k_hbm.at[row], k_ref.at[row], sems.at[row, 0]),
            pltpu.make_async_copy(v_hbm.at[row], v_ref.at[row], sems.at[row, 1]),
        ]
        pair[0].start()
        pair[1].start()
        copies.append(pair)
    column = lax.broadcasted_iota(jnp.int32, (group, positions), 1)
    for row in range(rows):
        valid = column < lengths[row]
        copies[row][0].wait()
        copies[row][1].wait()
        for j in range(KV_HEADS):
            lanes = slice(j * HEAD_DIM, (j + 1) * HEAD_DIM)
            scores = dot_nt(q_ref[row, j * group : (j + 1) * group, :], k_ref[row, :, lanes])
            scores = jnp.where(valid, scores * (1.0 / math.sqrt(HEAD_DIM)), -1e30)
            top = jnp.max(scores, axis=1, keepdims=True)
            terms = jnp.where(valid, jnp.exp(scores - top), 0.0)
            total = jnp.sum(terms, axis=1, keepdims=True)
            value = dot_nn(terms.astype(BF16), v_ref[row, :, lanes]) / total
            gathered[row, j * group : (j + 1) * group, :] = value
    for h in range(heads):
        flat[:, h * HEAD_DIM : (h + 1) * HEAD_DIM] = gathered[:, h, :]
    width = heads * HEAD_DIM // pieces
    for k in range(pieces):
        start = pl.multiple_of((where[0] ^ k) * width, width)
        outs[k][...] = flat[:, pl.ds(start, width)].astype(BF16)


def attend(queries, keys_cache, values_cache, lengths, where, pieces, loads):
    rows, columns = queries.shape
    heads = columns // HEAD_DIM
    return call(
        functools.partial(attention_kernel, pieces=pieces),
        "attention",
        [lengths, where, queries.reshape(rows, heads, HEAD_DIM), in_hbm(keys_cache), in_hbm(values_cache)],
        [SMEM, SMEM, VMEM, HBM, HBM],
        [jax.ShapeDtypeStruct((rows, columns // pieces), BF16)] * pieces,
        scratch=[
            pltpu.VMEM(keys_cache.shape, BF16),
            pltpu.VMEM(values_cache.shape, BF16),
            pltpu.SemaphoreType.DMA((rows, 2)),
            pltpu.VMEM((rows, heads, HEAD_DIM), F32),
            pltpu.VMEM((rows, columns), F32),
        ],
        loads=loads,
        us=4,
    )


def route_kernel(where, table_ref, facts_ref, slot_ref, weight_ref, largest_ref, *, experts, swapped):
    pools, double, pool_rows = facts_ref.shape
    top = double // 2
    rows = pools * pool_rows
    total = table_ref.shape[1]
    groups, _, lanes = slot_ref.shape
    group = lanes // rows
    own = where[3] if swapped else 0
    facts = jnp.concatenate([facts_ref[own ^ p] for p in range(pools)], axis=1)
    routes = jnp.concatenate([facts[i : i + 1] for i in range(top)], axis=1).astype(jnp.int32)
    ids = lax.broadcasted_iota(jnp.int32, (total, top * rows), 0)
    hot = jnp.where(ids == routes, 1.0, 0.0).astype(BF16)
    table = jnp.broadcast_to(table_ref[...].astype(F32), (8, total)).astype(BF16)
    entry = dot_nn(table, hot)[0:1].astype(jnp.int32)

    largest = jnp.int32(0)
    for p in range(pools):
        inside = (entry >= p * experts) & (entry < (p + 1) * experts)
        largest = jnp.maximum(largest, jnp.sum(jnp.where(inside, 1.0, 0.0)).astype(jnp.int32))
    largest_ref[0] = largest

    lane = lax.broadcasted_iota(jnp.int32, (groups, lanes), 1)
    block = lax.broadcasted_iota(jnp.int32, (groups, lanes), 0)
    wanted = where[3] * experts + block * group + lane // rows
    weight = jnp.zeros((groups, lanes), F32)
    mask = jnp.zeros((groups, lanes), F32)
    for i in range(top):
        named = jnp.concatenate([entry[:, i * rows : (i + 1) * rows]] * group, axis=1)
        value = jnp.concatenate([facts[top + i : top + i + 1]] * group, axis=1)
        match = wanted == named
        mask = mask + jnp.where(match, 1.0, 0.0)
        weight = weight + jnp.where(match, value, 0.0)
    earlier = lax.broadcasted_iota(jnp.int32, (lanes, lanes), 0)
    later = lax.broadcasted_iota(jnp.int32, (lanes, lanes), 1)
    before = jnp.where(earlier < later, 1.0, 0.0).astype(BF16)
    rank = dot_nn(mask.astype(BF16), before)
    base = jnp.zeros((1, 1), F32)
    for g in range(groups):
        slot = jnp.where(mask[g : g + 1] > 0.0, rank[g : g + 1] + base, -1.0)
        slot_ref[g] = slot.astype(jnp.int32)
        weight_ref[g] = weight[g : g + 1]
        base = base + jnp.sum(mask[g : g + 1], axis=1, keepdims=True)


def route(facts, expert_table, where, experts, rows, swapped, loads):
    group = max(1, min(experts, 256 // rows))
    shape = (experts // group, 1, group * rows)
    return call(
        functools.partial(route_kernel, experts=experts, swapped=swapped),
        "route",
        [where, expert_table.reshape(1, -1), facts],
        [SMEM, VMEM, VMEM],
        [
            jax.ShapeDtypeStruct(shape, jnp.int32),
            jax.ShapeDtypeStruct(shape, F32),
            jax.ShapeDtypeStruct((1,), jnp.int32),
        ],
        out_specs=[VMEM, VMEM, SMEM],
        loads=loads,
    )


def pick_kernel(shift, slot_ref, weight_ref, pick_ref, spread_ref, slot_weight_ref):
    groups, _, lanes = slot_ref.shape
    capacity = pick_ref.shape[0]
    total = jnp.zeros((capacity, 1), F32)
    place = lax.broadcasted_iota(jnp.int32, (capacity, lanes), 0)
    for g in range(groups):
        hit = place == slot_ref[g] - shift[0]
        one = jnp.where(hit, 1.0, 0.0)
        part = slice(g * lanes, (g + 1) * lanes)
        pick_ref[:, part] = one.astype(BF16)
        spread_ref[part, :] = one.T.astype(BF16)
        total = total + jnp.sum(jnp.where(hit, weight_ref[g], 0.0), axis=1, keepdims=True)
    slot_weight_ref[...] = total


def pick_slots(shift, slots, weights, capacity, loads=()):
    pairs = slots.shape[0] * slots.shape[2]
    return call(
        pick_kernel,
        "pick",
        [shift.reshape(1), slots, weights],
        [SMEM, VMEM, VMEM],
        [
            jax.ShapeDtypeStruct((capacity, pairs), BF16),
            jax.ShapeDtypeStruct((pairs, capacity), BF16),
            jax.ShapeDtypeStruct((capacity, 1), F32),
        ],
        loads=loads,
    )


def project_kernel(where, *refs, sources):
    inputs, w_ref = refs[:sources], refs[sources]
    outs = refs[sources + 1 :]
    own_rows = inputs[0].shape[0]
    count = sources * own_rows
    half = outs[0].shape[1]
    stacked = jnp.concatenate([ref[...].astype(F32) for ref in inputs], axis=0).astype(BF16)
    target = lax.broadcasted_iota(jnp.int32, (count, count), 0)
    origin = lax.broadcasted_iota(jnp.int32, (count, count), 1)
    order = (target ^ (where[0] * own_rows)) == origin
    x = dot_nn(jnp.where(order, 1.0, 0.0).astype(BF16), stacked).astype(BF16)
    for k in range(2):
        start = pl.multiple_of((where[1] ^ k) * half, half)
        value = dot_nn(x, w_ref[:, pl.ds(start, half)])
        if k == 0:
            outs[0][...] = value
            outs[1][...] = value.astype(BF16)
        else:
            outs[2][...] = value.astype(BF16)


def project(inputs, out_weight, where, loads, anchors):
    sources = len(inputs)
    shape = (sources * inputs[0].shape[0], out_weight.shape[1] // 2)
    return call(
        functools.partial(project_kernel, sources=sources),
        "project",
        [where, *inputs, out_weight],
        [SMEM] + [VMEM] * (sources + 1),
        [
            jax.ShapeDtypeStruct(shape, F32),
            jax.ShapeDtypeStruct(shape, BF16),
            jax.ShapeDtypeStruct(shape, BF16),
        ],
        loads=loads,
        anchors=anchors,
    )


def gate_up_kernel(where, *refs, sources, group):
    inputs = refs[:sources]
    pick_ref, g_ref, u_ref, out_ref, x, both = refs[sources:]
    count = inputs[0].shape[0]
    rows = x.shape[0]
    experts, _, depth = g_ref.shape
    if sources == 1:
        x[...] = inputs[0][...]
    else:
        for k in range(sources):
            start = pl.multiple_of((where[3] ^ k) * count, count)
            x[pl.ds(start, count), :] = inputs[k][...]
    for i in range(experts // group):
        part = slice(i * group, (i + 1) * group)
        gate = dot_nt(x[...], g_ref[part].reshape(group * CHUNK, depth)).astype(BF16)
        up = dot_nt(x[...], u_ref[part].reshape(group * CHUNK, depth)).astype(BF16)
        for e in range(group):
            first = (i * group + e) * rows
            lanes = slice(e * CHUNK, (e + 1) * CHUNK)
            both[first : first + rows, :CHUNK] = gate[:, lanes]
            both[first : first + rows, CHUNK:] = up[:, lanes]
    out_ref[...] = dot_nn(pick_ref[...], both[...]).astype(BF16)


def gate_up(xs, pick, w_gate, w_up, where, index, group, loads):
    sources = len(xs)
    rows = xs[0].shape[0] * sources
    experts, _, depth = w_gate.shape
    (sent,), held = call(
        functools.partial(gate_up_kernel, sources=sources, group=group),
        f"gate_up_{index}",
        [where, *xs, pick, w_gate, w_up],
        [SMEM] + [VMEM] * (sources + 3),
        [jax.ShapeDtypeStruct((pick.shape[0], 2 * CHUNK), BF16)],
        scratch=[
            pltpu.VMEM((rows, depth), BF16),
            pltpu.VMEM((experts * rows, 2 * CHUNK), BF16),
        ],
        loads=loads,
        us=4,
    )
    return sent, held


def down_kernel(own_ref, other_ref, weight_ref, spread_ref, d_ref, *refs, carried):
    before, outs = refs[:carried], refs[carried:]
    experts, _, depth = d_ref.shape
    rows = spread_ref.shape[0] // experts
    both = own_ref[...].astype(F32) + other_ref[...].astype(F32)
    gate, up = both[:, :CHUNK], both[:, CHUNK:]
    hidden = (gate / (1.0 + jnp.exp(-gate)) * up * weight_ref[...]).astype(BF16)
    spread = dot_nn(spread_ref[...], hidden).astype(BF16)
    left = jnp.concatenate([spread[e * rows : (e + 1) * rows] for e in range(experts)], axis=1)
    total = dot_nn(left, d_ref[...].reshape(experts * CHUNK, depth))
    if carried:
        total = total + before[0][...]
    outs[0][...] = total


def down(own, other, slot_weight, spread, w_down, before, index):
    experts, _, depth = w_down.shape
    rows = spread.shape[0] // experts
    carried = [] if before is None else [before]
    (total,), _ = call(
        functools.partial(down_kernel, carried=len(carried)),
        f"down_{index}",
        [own, other, slot_weight, spread, w_down, *carried],
        [VMEM] * (5 + len(carried)),
        [jax.ShapeDtypeStruct((rows, depth), F32)],
        us=3,
    )
    return total


def load(loads, anchors, name):
    return call(lambda: None, name, [], [], [], loads=loads, anchors=anchors, us=2 * len(loads))[1]


def halves_kernel(where, value_ref, own_ref, other_ref):
    width = own_ref.shape[1]
    own_ref[...] = value_ref[:, pl.ds(pl.multiple_of(where[2] * width, width), width)]
    other_ref[...] = value_ref[:, pl.ds(pl.multiple_of((1 - where[2]) * width, width), width)]


def halves(value, where):
    rows, depth = value.shape
    vmem = pl.BlockSpec(memory_space=pltpu.VMEM)
    return pl.pallas_call(
        halves_kernel,
        in_specs=[pl.BlockSpec(memory_space=pltpu.SMEM), vmem],
        out_specs=[vmem] * 2,
        out_shape=[jax.ShapeDtypeStruct((rows, depth // 2), F32)] * 2,
        name="halves",
    )(where, value)


def split_kernel(where, own_ref, other_ref, *outs):
    count = outs[0].shape[0]
    for k in range(len(outs)):
        row = pl.ds(pl.multiple_of((where[3] ^ k) * count, count), count)
        outs[k][...] = (own_ref[row, :] + other_ref[row, :]).astype(outs[k].dtype)


def split(own, other, where, pieces):
    rows, width = own.shape
    vmem = pl.BlockSpec(memory_space=pltpu.VMEM)
    return pl.pallas_call(
        split_kernel,
        in_specs=[pl.BlockSpec(memory_space=pltpu.SMEM), vmem, vmem],
        out_specs=[vmem] * pieces,
        out_shape=[
            jax.ShapeDtypeStruct((rows // pieces, width), F32 if k == 0 else BF16)
            for k in range(pieces)
        ],
        name="split",
    )(where, own, other)


def xor_permute(value, axes, count, k):
    return lax.ppermute(value, axes, [(i, i ^ k) for i in range(count)])


def body(
    queries,
    keys_cache,
    values_cache,
    lengths,
    out_weight,
    routes,
    route_weight,
    expert_table,
    w_gate,
    w_up,
    w_down,
):
    pools, tps, subs = lax.axis_size("pool"), lax.axis_size("tp"), lax.axis_size("sub")
    pool, tp, sub = lax.axis_index("pool"), lax.axis_index("tp"), lax.axis_index("sub")
    shards = tps * subs
    shard = tp * subs + sub
    direct = tps == 2 and subs == 2 and pools == 4
    own_rows = queries.shape[0]
    pool_rows = own_rows * shards
    rows = pool_rows * pools
    experts, hidden_units, half_width = w_gate.shape
    top = routes.shape[1]
    where = jnp.stack([shard, tp, sub, pool]).astype(jnp.int32)

    facts = jnp.concatenate([routes.astype(F32), route_weight], axis=1).T
    capacity = -(-rows * top * 13 // (8 * pools * 16)) * 16
    group = max(1, min(experts, 256 // rows))
    gates, ups, downs = [[(w, c) for c in range(0, hidden_units, CHUNK)] for w in (w_gate, w_up, w_down)]
    chunks = len(gates)

    if direct:
        axes = ("tp", "sub")
        pieces, (out_held, gate_0) = attend(
            queries,
            keys_cache,
            values_cache,
            lengths,
            where,
            shards,
            [(out_weight, None), gates[0]],
        )
        facts, pieces = lax.optimization_barrier((facts, pieces))
        inputs = [pieces[0]] + [xor_permute(pieces[k], axes, shards, k) for k in range(1, shards)]
        blocks = [facts] + [xor_permute(facts, "pool", pools, k) for k in range(1, pools)]
        (up_0,) = load([ups[0]], [pieces[0]], "load_a")
        (kept, near, far), (gate_1,) = project(inputs, out_held, where, [gates[1]], [up_0])
        (up_1,) = load([ups[1]], [near], "load_b")
        x_sum = kept
        for k in range(1, shards):
            value = near if k < subs else far
            x_sum = x_sum + xor_permute(value, axes, shards, k).astype(F32)
        x_half, up_1 = lax.optimization_barrier((x_sum.astype(BF16), up_1))
        xs = [x_half] + [xor_permute(x_half, "pool", pools, k) for k in range(1, pools)]
        blocks, _ = lax.optimization_barrier((blocks, x_half))
        (slots, weights, largest), (gate_2,) = route(
            jnp.stack(blocks), expert_table, where, experts, rows, True, [gates[2]]
        )
        (pick, spread, slot_weight), (up_2,) = pick_slots(
            jnp.int32(0), slots, weights, capacity, [ups[2]]
        )
        (down_0,) = load([downs[0]], [pick], "load_c")
        held = [(gate_0, up_0), (gate_1, up_1), (gate_2, up_2)]
        theirs = lax.ppermute(
            lax.dynamic_slice_in_dim(x_half, (shard ^ subs) * own_rows, own_rows, 0),
            "tp",
            [(0, 1), (1, 0)],
        )
        mine = lax.dynamic_slice_in_dim(x_half, shard * own_rows, own_rows, 0)
        attended = jnp.where(
            tp == 0,
            jnp.concatenate([mine, theirs], axis=1),
            jnp.concatenate([theirs, mine], axis=1),
        )
        held_down, sent = [down_0], []
        for c in range(chunks):
            value, more_held = gate_up(
                xs, pick, *held[c], where, c, group, downs[c + 1 : c + 2]
            )
            sent.append(value)
            held_down += more_held
    else:
        blocks = lax.all_gather(facts, "pool", axis=0)
        (slots, weights, largest), _ = route(blocks, expert_table, where, experts, rows, False, [])
        (pick, spread, slot_weight), _ = pick_slots(jnp.int32(0), slots, weights, capacity)
        (attention,), _ = attend(queries, keys_cache, values_cache, lengths, where * 0, 1, [])
        head_rows = lax.all_to_all(
            attention, ("tp", "sub"), split_axis=1, concat_axis=0, tiled=True
        )
        partial = jnp.dot(head_rows, out_weight, preferred_element_type=F32)
        x_sum = lax.psum_scatter(partial, ("tp", "sub"), scatter_dimension=1, tiled=True)
        x_pool = x_sum.astype(BF16)
        attended = lax.all_to_all(x_pool, ("tp", "sub"), split_axis=0, concat_axis=1, tiled=True)
        x_part = lax.all_gather(x_pool, "pool", axis=0, tiled=True)
        xs = [lax.all_gather(x_part, "sub", axis=1, tiled=True)]
        held = load(gates + ups + downs, [], "load")
        held_down = held[2 * chunks :]
        sent = [
            gate_up(xs, pick, held[c], held[chunks + c], where, c, group, [])[0]
            for c in range(chunks)
        ]

    def exchange(value):
        if tps == 2:
            return value, lax.ppermute(value, "tp", [(0, 1), (1, 0)])
        return lax.psum(value.astype(F32), "tp").astype(BF16), jnp.zeros_like(value)

    result = None
    both = [exchange(value) for value in sent]
    for c in range(chunks):
        result = down(*both[c], slot_weight, spread, held_down[c], result, c)

    def combine(value):
        if not direct:
            value = lax.psum_scatter(value, "pool", scatter_dimension=0, tiled=True)
            return lax.psum_scatter(value, "sub", scatter_dimension=1, tiled=True)
        own, other = halves(value, where)
        pieces = split(own, xor_permute(other, "sub", subs, 1), where, pools)
        total = pieces[0]
        for k in range(1, pools):
            total = total + xor_permute(pieces[k], "pool", pools, k).astype(F32)
        return total

    def more(state):
        k, total = state
        k, *held = lax.optimization_barrier((k, *xs))
        order = lax.iota(jnp.int32, len(held)) ^ (pool if direct else 0)
        x = jnp.take(jnp.stack(held), order, axis=0).reshape(rows, half_width)
        (pick, spread, slot_weight), _ = pick_slots(k * capacity, slots, weights, capacity)
        gate = jnp.einsum("rd,efd->erf", x, w_gate, preferred_element_type=F32)
        up = jnp.einsum("rd,efd->erf", x, w_up, preferred_element_type=F32)
        both = jnp.concatenate([gate, up], axis=2).astype(BF16)
        both = both.reshape(experts * rows, 2 * hidden_units)
        sent = jnp.dot(pick, both, preferred_element_type=F32).astype(BF16)
        if tps == 2:
            both = sent.astype(F32) + lax.ppermute(sent, "tp", [(0, 1), (1, 0)]).astype(F32)
        else:
            both = lax.psum(sent.astype(F32), "tp")
        hidden = jax.nn.silu(both[:, :hidden_units]) * both[:, hidden_units:] * slot_weight
        spread = jnp.dot(spread, hidden.astype(BF16), preferred_element_type=F32).astype(BF16)
        spread = spread.reshape(experts, rows, hidden_units)
        value = jnp.einsum("erf,efd->rd", spread, w_down, preferred_element_type=F32)
        return k + 1, total + combine(value)

    expert_sum = combine(result)
    _, extra = lax.while_loop(
        lambda state: state[0] * capacity < largest[0],
        more,
        (jnp.int32(1), jnp.zeros((pool_rows, half_width // subs), F32)),
    )
    return attended, (expert_sum + extra).astype(BF16)


def solution(mesh):
    in_specs = (
        P(("grp", "pool", "tp", "sub"), None),
        P(("grp", "pool", "tp", "sub"), None, None),
        P(("grp", "pool", "tp", "sub"), None, None),
        P(("grp", "pool", "tp", "sub")),
        P(("tp", "sub"), None),
        P(("grp", "pool"), None),
        P(("grp", "pool"), None),
        P(),
        P("pool", "sub", "tp"),
        P("pool", "sub", "tp"),
        P("pool", "sub", "tp"),
    )
    out_specs = (P(("grp", "pool", "tp", "sub"), None), P(("grp", "pool"), ("tp", "sub")))
    return jax.shard_map(body, mesh=mesh, in_specs=in_specs, out_specs=out_specs, check_vma=False)
```

```python
import functools
import math

import jax
import jax.numpy as jnp
from jax import lax
from jax.experimental import pallas as pl
from jax.experimental.pallas import tpu as pltpu
from jax.sharding import PartitionSpec as P

HEAD_DIM = 128
KV_HEADS = 2
CHUNK = 128
FACT_LANES = 128

F32 = jnp.float32
BF16 = jnp.bfloat16


def dot_nt(a, b):
    return lax.dot_general(a, b, (((1,), (1,)), ((), ())), preferred_element_type=F32)


def dot_tn(a, b):
    return lax.dot_general(a, b, (((0,), (0,)), ((), ())), preferred_element_type=F32)


def dot_nn(a, b):
    return jnp.dot(a, b, preferred_element_type=F32)


def cost(microseconds):
    return pl.CostEstimate(
        flops=0, transcendentals=0, bytes_accessed=int(microseconds * 3_000_000)
    )


VMEM = pl.BlockSpec(memory_space=pltpu.VMEM)
SMEM = pl.BlockSpec(memory_space=pltpu.SMEM)
HBM = pl.BlockSpec(memory_space=pltpu.HBM)
ANY = pl.BlockSpec(memory_space=pl.ANY)


def in_hbm(value):
    return pltpu.with_memory_space_constraint(value, pltpu.HBM)


def position():
    tp, sub = lax.axis_index("tp"), lax.axis_index("sub")
    subs = lax.axis_size("sub")
    return tp * subs + sub, tp, sub, lax.axis_index("pool"), subs


def call(kernel, name, inputs, specs, outs, out_specs=None, scratch=(), loads=(), anchors=(), us=2, roomy=False, begins=False):
    count_in, count_out, count_load = len(inputs), len(outs), len(loads)

    def source(ref, first):
        return ref if first is None else ref.at[:, first : first + CHUNK, :]

    def run(*refs):
        refs = list(refs)
        given = [refs.pop(0) for _ in range(count_in)]
        sources = [refs.pop(0) for _ in range(count_load)]
        del refs[: len(anchors)]
        results = [refs.pop(0) for _ in range(count_out)]
        targets = [refs.pop(0) for _ in range(count_load)]
        copies = []
        if loads:
            sems = refs.pop()
            for i, (_, first) in enumerate(loads):
                copies.append(
                    pltpu.make_async_copy(source(sources[i], first), targets[i], sems.at[i])
                )

        def begin():
            if copies:

                @pl.when(lax.axis_index("tp") >= 0)
                def _():
                    for copy in copies:
                        copy.start()

        if begins:
            kernel(begin, *given, *results, *refs)
        else:
            begin()
            kernel(*given, *results, *refs)
        for copy in copies:
            copy.wait()

    def loaded(array, first):
        shape = array.shape if first is None else (array.shape[0], CHUNK, array.shape[2])
        return pltpu.VMEM(shape, array.dtype)

    if not roomy:
        outs = [
            leaf if spec is HBM else pltpu.VMEM(leaf.shape, leaf.dtype)
            for leaf, spec in zip(outs, out_specs or [VMEM] * count_out)
        ]
    scratch = list(scratch) + ([pltpu.SemaphoreType.DMA((count_load,))] if loads else [])
    results = pl.pallas_call(
        run,
        in_specs=list(specs) + [HBM] * count_load + [ANY] * len(anchors),
        out_specs=list(out_specs or [VMEM] * count_out) + [VMEM] * count_load,
        out_shape=list(outs) + [loaded(*leaf) for leaf in loads],
        scratch_shapes=scratch,
        compiler_params=pltpu.CompilerParams(vmem_limit_bytes=(48 if roomy else 12) << 20),
        cost_estimate=cost(us),
        name=name,
    )(*inputs, *[in_hbm(leaf[0]) for leaf in loads], *anchors)
    return list(results[:count_out]), list(results[count_out:])


def attention_kernel(
    begin, q_hbm, lengths_hbm, route_hbm, share_hbm, k_hbm, v_hbm, *refs, pieces
):
    where = position()
    outs, facts_ref = refs[:pieces], refs[pieces]
    lengths, q_ref, route_ref, share_ref, k_ref, v_ref, sems, spread, gathered, flat = refs[
        pieces + 1 :
    ]
    rows, heads, _ = gathered.shape
    positions = k_ref.shape[1]
    group = heads // KV_HEADS
    small = [
        pltpu.make_async_copy(q_hbm, q_ref, sems.at[rows, 0]),
        pltpu.make_async_copy(lengths_hbm, lengths, sems.at[rows, 1]),
        pltpu.make_async_copy(route_hbm, route_ref, sems.at[rows + 1, 0]),
        pltpu.make_async_copy(share_hbm, share_ref, sems.at[rows + 1, 1]),
    ]
    for copy in small:
        copy.start()
    copies = []
    for row in range(rows):
        pair = [
            pltpu.make_async_copy(k_hbm.at[row], k_ref.at[row], sems.at[row, 0]),
            pltpu.make_async_copy(v_hbm.at[row], v_ref.at[row], sems.at[row, 1]),
        ]
        pair[0].start()
        pair[1].start()
        copies.append(pair)
    begin()
    for copy in small:
        copy.wait()
    share = share_ref[...]
    high = share.astype(BF16).astype(F32)
    middle = (share - high).astype(BF16).astype(F32)
    block = jnp.concatenate([route_ref[...].astype(F32), high, middle, share - high - middle], axis=0)
    count, lanes = block.shape[1], facts_ref.shape[1]
    block = jnp.concatenate([block, jnp.zeros((block.shape[0], -count % 128), F32)], axis=1).T
    blank = jnp.zeros((count, lanes - block.shape[1]), F32)
    facts_ref[...] = jnp.concatenate([block[:count], blank], axis=1).astype(BF16)
    queries = q_ref[...].astype(F32)
    for h in range(heads):
        spread[:, h, :] = queries[:, h * HEAD_DIM : (h + 1) * HEAD_DIM]
    column = lax.broadcasted_iota(jnp.int32, (group, positions), 1)
    for row in range(rows):
        valid = column < lengths[row]
        copies[row][0].wait()
        copies[row][1].wait()
        for j in range(KV_HEADS):
            lanes = slice(j * HEAD_DIM, (j + 1) * HEAD_DIM)
            own = spread[row, j * group : (j + 1) * group, :].astype(BF16)
            scores = dot_nt(own, k_ref[row, :, lanes])
            scores = jnp.where(valid, scores * (1.0 / math.sqrt(HEAD_DIM)), -1e30)
            top = jnp.max(scores, axis=1, keepdims=True)
            terms = jnp.where(valid, jnp.exp(scores - top), 0.0)
            total = jnp.sum(terms, axis=1, keepdims=True)
            value = dot_nn(terms.astype(BF16), v_ref[row, :, lanes]) / total
            gathered[row, j * group : (j + 1) * group, :] = value
    for h in range(heads):
        flat[:, h * HEAD_DIM : (h + 1) * HEAD_DIM] = gathered[:, h, :]
    width = heads * HEAD_DIM // pieces
    for k in range(pieces):
        start = pl.multiple_of(((where[0] ^ k) if pieces > 1 else 0) * width, width)
        outs[k][...] = flat[:, pl.ds(start, width)].astype(BF16)


def attend(queries, keys_cache, values_cache, lengths, facts, pieces, loads, roomy):
    rows, columns = queries.shape
    heads = columns // HEAD_DIM
    return call(
        functools.partial(attention_kernel, pieces=pieces),
        "attention",
        [in_hbm(a) for a in (queries, lengths, *facts, keys_cache, values_cache)],
        [HBM] * 6,
        [jax.ShapeDtypeStruct((rows, columns // pieces), BF16)] * pieces
        + [jax.ShapeDtypeStruct((facts[0].shape[1], FACT_LANES), BF16)],
        scratch=[
            pltpu.SMEM((rows,), jnp.int32),
            pltpu.VMEM(queries.shape, BF16),
            pltpu.VMEM(facts[0].shape, jnp.int32),
            pltpu.VMEM(facts[1].shape, F32),
            pltpu.VMEM(keys_cache.shape, BF16),
            pltpu.VMEM(values_cache.shape, BF16),
            pltpu.SemaphoreType.DMA((rows + 2, 2)),
            pltpu.VMEM((rows, heads, HEAD_DIM), F32),
            pltpu.VMEM((rows, heads, HEAD_DIM), F32),
            pltpu.VMEM((rows, columns), F32),
        ],
        loads=loads,
        us=4,
        roomy=roomy,
        begins=True,
    )


def route_kernel(table_ref, *refs, sources, experts, top):
    where = position()
    given, (slot_ref, weight_ref, largest_ref, *picks, held) = refs[:sources], refs[sources:]
    pools, pool_rows, lanes = held.shape
    if sources == 1:
        held[...] = given[0][...].astype(F32)
    else:
        for k in range(sources):
            width = given[k].shape[1]
            held[where[3] ^ where[0] ^ k] = given[k][:, width - lanes :].astype(F32)
    rows = pools * pool_rows
    total = table_ref.shape[1]
    groups, _, lanes = slot_ref.shape
    group = lanes // rows
    facts = held[...].reshape(rows, held.shape[2]).T
    shares = facts[top : 2 * top] + facts[2 * top : 3 * top] + facts[3 * top : 4 * top]
    routes = jnp.concatenate([facts[i : i + 1] for i in range(top)], axis=1).astype(jnp.int32)
    ids = lax.broadcasted_iota(jnp.int32, (total, top * rows), 0)
    hot = jnp.where(ids == routes, 1.0, 0.0).astype(BF16)
    table = jnp.broadcast_to(table_ref[...].astype(F32), (8, total)).astype(BF16)
    entry = dot_nn(table, hot)[0:1].astype(jnp.int32)

    first = lax.broadcasted_iota(jnp.int32, (pools, top * rows), 0) * experts
    inside = jnp.where((entry >= first) & (entry < first + experts), 1.0, 0.0)
    loads = jnp.sum(inside, axis=1, keepdims=True)
    largest_ref[...] = jnp.max(loads, axis=0, keepdims=True).astype(jnp.int32)

    lane = lax.broadcasted_iota(jnp.int32, (groups, lanes), 1)
    block = lax.broadcasted_iota(jnp.int32, (groups, lanes), 0)
    wanted = where[3] * experts + block * group + lane // rows
    weight = jnp.zeros((groups, lanes), F32)
    mask = jnp.zeros((groups, lanes), F32)
    for i in range(top):
        named = jnp.concatenate([entry[:, i * rows : (i + 1) * rows]] * group, axis=1)
        value = jnp.concatenate([shares[i : i + 1]] * group, axis=1)
        match = wanted == named
        mask = mask + jnp.where(match, 1.0, 0.0)
        weight = weight + jnp.where(match, value, 0.0)
    earlier = lax.broadcasted_iota(jnp.int32, (lanes, lanes), 0)
    later = lax.broadcasted_iota(jnp.int32, (lanes, lanes), 1)
    before = jnp.where(earlier < later, 1.0, 0.0).astype(BF16)
    rank = dot_nn(mask.astype(BF16), before)
    base = jnp.zeros((1, 1), F32)
    counts = jnp.sum(mask, axis=1, keepdims=True)
    slots = []
    for g in range(groups):
        slots.append(jnp.where(mask[g : g + 1] > 0.0, rank[g : g + 1] + base, -1.0))
        slot_ref[g] = slots[g].astype(jnp.int32)
        weight_ref[g] = weight[g : g + 1]
        base = base + counts[g : g + 1]
    fill_picks(slots, [weight[g : g + 1] for g in range(groups)], *picks)


def fill_picks(slots, weights, pick_ref, spread_ref, slot_weight_ref):
    groups, lanes = len(slots), slots[0].shape[1]
    capacity = pick_ref.shape[0]
    rows = jnp.concatenate(slots + [slots[0]] * (-groups % 8), axis=0).T
    place = lax.broadcasted_iota(jnp.int32, (capacity, lanes), 0).astype(F32)
    along = lax.broadcasted_iota(jnp.int32, (lanes, capacity), 1).astype(F32)
    total = jnp.zeros((capacity, lanes), F32)
    for g in range(groups):
        hit = place == slots[g]
        part = slice(g * lanes, (g + 1) * lanes)
        pick_ref[:, part] = jnp.where(hit, 1.0, 0.0).astype(BF16)
        spread_ref[part, :] = jnp.where(along == rows[:, g : g + 1], 1.0, 0.0).astype(BF16)
        total = total + jnp.where(hit, weights[g], 0.0)
    slot_weight_ref[...] = jnp.sum(total, axis=1, keepdims=True)


def pick_shapes(capacity, pairs):
    return [
        jax.ShapeDtypeStruct((capacity, pairs), BF16),
        jax.ShapeDtypeStruct((pairs, capacity), BF16),
        jax.ShapeDtypeStruct((capacity, 1), F32),
    ]


def route(blocks, expert_table, experts, rows, top, capacity, pools, loads, roomy):
    group = max(1, min(experts, 256 // rows))
    shape = (experts // group, 1, group * rows)
    results, held = call(
        functools.partial(route_kernel, sources=len(blocks), experts=experts, top=top),
        "route",
        [expert_table.reshape(1, -1), *blocks],
        [VMEM] + [VMEM] * len(blocks),
        [
            jax.ShapeDtypeStruct(shape, jnp.int32),
            jax.ShapeDtypeStruct(shape, F32),
            jax.ShapeDtypeStruct((1, 1), jnp.int32),
            *pick_shapes(capacity, experts * rows),
        ],
        scratch=[pltpu.VMEM((pools, rows // pools, FACT_LANES), F32)],
        loads=loads,
        us=6,
        roomy=roomy,
    )
    return results[:3], results[3:], held


def pick_slots(shift, slots, weights, capacity):
    def kernel(shift_ref, *refs):
        slot_ref, weight_ref, *picks = refs
        groups = range(slot_ref.shape[0])
        shifted = [(slot_ref[g] - shift_ref[0]).astype(F32) for g in groups]
        fill_picks(shifted, [weight_ref[g] for g in groups], *picks)

    return call(
        kernel,
        "pick",
        [shift.reshape(1), slots, weights],
        [SMEM, VMEM, VMEM],
        pick_shapes(capacity, slots.shape[0] * slots.shape[2]),
        roomy=True,
    )[0]


def project_kernel(*refs, sources):
    where = position()
    inputs, (own_ref, sent_ref, w_ref) = refs[:sources], refs[sources : sources + 3]
    kept, near, far, held = refs[sources + 3 :]
    own_rows = inputs[0].shape[0]
    count = sources * own_rows
    half = kept.shape[1]
    facts = jnp.where(where[0] == 0, own_ref[...].astype(F32), sent_ref[...].astype(F32))
    facts = facts.astype(BF16)
    held[...] = facts
    stacked = jnp.concatenate([ref[...].astype(F32) for ref in inputs], axis=0).astype(BF16)
    target = lax.broadcasted_iota(jnp.int32, (count, count), 0)
    origin = lax.broadcasted_iota(jnp.int32, (count, count), 1)
    order = (target ^ (where[0] * own_rows)) == origin
    x = dot_nn(jnp.where(order, 1.0, 0.0).astype(BF16), stacked).astype(BF16)
    for k, out in ((1, far), (0, near)):
        start = pl.multiple_of((where[1] ^ k) * half, half)
        value = dot_nn(x, w_ref[:, pl.ds(start, half)])
        out[:, :half] = value.astype(BF16)
        out[:, half:] = facts
        if k == 0:
            kept[...] = value


def project(inputs, facts, out_weight, loads, anchors):
    sources = len(inputs)
    count, half = sources * inputs[0].shape[0], out_weight.shape[1] // 2
    sent = jax.ShapeDtypeStruct((count, half + FACT_LANES), BF16)
    return call(
        functools.partial(project_kernel, sources=sources),
        "project",
        [*inputs, *facts, out_weight],
        [VMEM] * (sources + 3),
        [
            jax.ShapeDtypeStruct((count, half), F32),
            sent,
            sent,
            jax.ShapeDtypeStruct((count, FACT_LANES), BF16),
        ],
        loads=loads,
        anchors=anchors,
    )


def gate_up_kernel(*refs, sources, first):
    where = position()
    inputs, refs = refs[:sources], refs[sources:]
    pick_ref, g_ref, u_ref, out_ref = refs[:4]
    if first:
        columns_ref, mine_ref, theirs_ref, x, both = refs[4:]
        count = inputs[0].shape[0]
        own_rows = mine_ref.shape[0]
        row = lax.broadcasted_iota(jnp.int32, (own_rows, count), 0)
        place = lax.broadcasted_iota(jnp.int32, (own_rows, count), 1)
        for out, shard in ((mine_ref, where[0]), (theirs_ref, where[0] ^ where[4])):
            chosen = jnp.where(place == row + shard * own_rows, 1.0, 0.0).astype(BF16)
            out[...] = dot_nn(chosen, inputs[0][...]).astype(BF16)
        for k in range(sources):
            start = pl.multiple_of((where[3] ^ k) * count, count) if sources > 1 else 0
            x[pl.ds(start, count), :] = inputs[k][...].astype(F32)
        columns_ref[...] = x[...].T.astype(BF16)
    else:
        (columns_ref,), (both,) = inputs, refs[4:]
    experts, _, depth = g_ref.shape
    rows = columns_ref.shape[1]
    for base, w_ref in ((0, g_ref), (CHUNK, u_ref)):
        value = dot_nn(w_ref[...].reshape(experts * CHUNK, depth), columns_ref[...]).astype(BF16)
        for e in range(experts):
            both[base : base + CHUNK, e * rows : (e + 1) * rows] = value[
                e * CHUNK : (e + 1) * CHUNK
            ]
    out_ref[...] = dot_nt(pick_ref[...], both[...]).astype(BF16)


def gate_up(xs, pick, w_gate, w_up, index, own_rows, loads, roomy, anchors=()):
    first = index == 0
    experts, _, depth = w_gate.shape
    rows = pick.shape[1] // experts
    outs = [jax.ShapeDtypeStruct((pick.shape[0], 2 * CHUNK), BF16)]
    scratch = [pltpu.VMEM((2 * CHUNK, experts * rows), BF16)]
    if first:
        outs.append(jax.ShapeDtypeStruct((depth, rows), BF16))
        outs += [jax.ShapeDtypeStruct((own_rows, depth), BF16)] * 2
        scratch.insert(0, pltpu.VMEM((rows, depth), F32))
    results, held = call(
        functools.partial(gate_up_kernel, sources=len(xs), first=first),
        f"gate_up_{index}",
        [*xs, pick, w_gate, w_up],
        [VMEM] * (len(xs) + 3),
        outs,
        scratch=scratch,
        loads=loads,
        anchors=anchors,
        us=4,
        roomy=roomy,
    )
    return results[0], results[1:2] if first else xs, results[2:], held


def down_kernel(own_ref, other_ref, weight_ref, spread_ref, d_ref, *refs, carried):
    before, outs = refs[:carried], refs[carried:]
    experts, _, depth = d_ref.shape
    rows = spread_ref.shape[0] // experts
    both = own_ref[...].astype(F32) + other_ref[...].astype(F32)
    gate, up = both[:, :CHUNK], both[:, CHUNK:]
    hidden = (gate / (1.0 + jnp.exp(-gate)) * up * weight_ref[...]).astype(BF16)
    spread = dot_nn(spread_ref[...], hidden).astype(BF16)
    left = jnp.concatenate([spread[e * rows : (e + 1) * rows] for e in range(experts)], axis=1)
    total = dot_nn(left, d_ref[...].reshape(experts * CHUNK, depth))
    if carried:
        total = total + before[0][...]
    if len(outs) == 1:
        outs[0][...] = total
    else:
        half = depth // 2
        low, high = total[:, :half], total[:, half:]
        mine = lax.axis_index("sub") == 0
        outs[0][...] = jnp.where(mine, low, high)
        outs[1][...] = jnp.where(mine, high, low)


def down(own, other, slot_weight, spread, w_down, before, index, halved, roomy):
    experts, _, depth = w_down.shape
    rows = spread.shape[0] // experts
    carried = [] if before is None else [before]
    parts = 2 if halved else 1
    return call(
        functools.partial(down_kernel, carried=len(carried)),
        f"down_{index}",
        [own, other, slot_weight, spread, w_down, *carried],
        [VMEM] * (5 + len(carried)),
        [jax.ShapeDtypeStruct((rows, depth // parts), F32)] * parts,
        us=3,
        roomy=roomy,
    )[0]


def load(loads, anchors, name, roomy=False):
    return call(
        lambda: None, name, [], [], [], loads=loads, anchors=anchors, us=2 * len(loads), roomy=roomy
    )[1]


def arrange_kernel(*refs):
    inputs, out_ref = refs[:-1], refs[-1]
    count = inputs[0].shape[0]
    for k, ref in enumerate(inputs):
        start = pl.multiple_of((lax.axis_index("pool") ^ k) * count, count)
        out_ref[pl.ds(start, count), :] = ref[...]


def arrange(blocks):
    shape = (len(blocks) * blocks[0].shape[0], blocks[0].shape[1])
    outs = [jax.ShapeDtypeStruct(shape, BF16)]
    return call(arrange_kernel, "arrange", blocks, [VMEM] * len(blocks), outs, roomy=True)[0][0]


def halves_kernel(value_ref, own_ref, other_ref):
    half = own_ref.shape[1]
    low, high = value_ref[:, :half], value_ref[:, half:]
    mine = lax.axis_index("sub") == 0
    own_ref[...] = jnp.where(mine, low, high)
    other_ref[...] = jnp.where(mine, high, low)


def halves(value):
    outs = [jax.ShapeDtypeStruct((value.shape[0], value.shape[1] // 2), F32)] * 2
    return call(halves_kernel, "halves", [value], [VMEM], outs, roomy=True)[0]


def join_kernel(mine_ref, theirs_ref, out_hbm, out_ref, sem):
    half = mine_ref.shape[1]
    low = lax.axis_index("tp") == 0
    mine, theirs = mine_ref[...].astype(F32), theirs_ref[...].astype(F32)
    out_ref[:, :half] = jnp.where(low, mine, theirs).astype(BF16)
    out_ref[:, half:] = jnp.where(low, theirs, mine).astype(BF16)
    copy = pltpu.make_async_copy(out_ref, out_hbm, sem)
    copy.start()
    copy.wait()


def join(mine, theirs):
    shape = (mine.shape[0], 2 * mine.shape[1])
    return call(
        join_kernel,
        "join",
        [mine, theirs],
        [VMEM, VMEM],
        [jax.ShapeDtypeStruct(shape, BF16)],
        out_specs=[HBM],
        scratch=[pltpu.VMEM(shape, BF16), pltpu.SemaphoreType.DMA],
    )[0][0]


def split_kernel(own_ref, other_ref, *outs):
    count = outs[0].shape[0]
    pool = lax.axis_index("pool")
    for k in range(len(outs)):
        row = pl.ds(pl.multiple_of((pool ^ k) * count, count), count)
        outs[k][...] = (own_ref[row, :] + other_ref[row, :]).astype(outs[k].dtype)


def split(own, other, pieces):
    shape = (own.shape[0] // pieces, own.shape[1])
    return call(
        split_kernel,
        "split",
        [own, other],
        [VMEM, VMEM],
        [jax.ShapeDtypeStruct(shape, F32 if k == 0 else BF16) for k in range(pieces)],
    )[0]


def xor_permute(value, axes, count, k):
    return lax.ppermute(value, axes, [(i, i ^ k) for i in range(count)])


def body(
    queries,
    keys_cache,
    values_cache,
    lengths,
    out_weight,
    routes,
    route_weight,
    expert_table,
    w_gate,
    w_up,
    w_down,
):
    pools, tps, subs = lax.axis_size("pool"), lax.axis_size("tp"), lax.axis_size("sub")
    pool, tp, sub = lax.axis_index("pool"), lax.axis_index("tp"), lax.axis_index("sub")
    shards = tps * subs
    shard = tp * subs + sub
    direct = tps == 2 and subs == 2 and pools == 4
    own_rows = queries.shape[0]
    pool_rows = own_rows * shards
    rows = pool_rows * pools
    experts, hidden_units, half_width = w_gate.shape
    top = routes.shape[1]

    capacity = -(-rows * top * 13 // (8 * pools * 16)) * 16
    gates, ups, downs = [
        [(w, c) for c in range(0, hidden_units, CHUNK)] for w in (w_gate, w_up, w_down)
    ]
    chunks = len(gates)

    if direct:
        axes = ("tp", "sub")
        (*pieces, facts), (out_held, gate_0, up_0) = attend(
            queries,
            keys_cache,
            values_cache,
            lengths,
            (routes.T, route_weight.T),
            shards,
            [(out_weight, None), gates[0], ups[0]],
            False,
        )
        inputs = [pieces[0]] + [xor_permute(pieces[k], axes, shards, k) for k in range(1, shards)]
        pairs = [(i, i ^ (shards * (i % shards))) for i in range(pools * shards) if i % shards]
        other_facts = lax.ppermute(facts, ("pool", "tp", "sub"), pairs)
        gate_1, up_1 = load([gates[1], ups[1]], [pieces[0]], "load_a")
        (kept, near, far, block), (gate_2,) = project(
            inputs, [facts, other_facts], out_held, [gates[2]], [gate_1]
        )
        up_2, down_0 = load([ups[2], downs[0]], [near], "load_b")
        x_sum, blocks = kept, [block]
        for k in range(1, shards):
            blocks.append(xor_permute(near if k < subs else far, axes, shards, k))
            x_sum = x_sum + blocks[k][:, :half_width].astype(F32)
        x_half, up_2 = lax.optimization_barrier((x_sum.astype(BF16), up_2))
        xs = [x_half] + [xor_permute(x_half, "pool", pools, k) for k in range(1, pools)]
        blocks, _ = lax.optimization_barrier((blocks, x_half))
        (slots, weights, largest), (pick, spread, slot_weight), (down_1, down_2) = route(
            blocks,
            expert_table,
            experts,
            rows,
            top,
            capacity,
            pools,
            downs[1:3],
            False,
        )
        held = [(gate_0, up_0), (gate_1, up_1), (gate_2, up_2)]
        held_down, sent, given = [down_0, down_1, down_2], [], xs
        for c in range(chunks):
            value, given, rest, _ = gate_up(
                given, pick, *held[c], c, own_rows, [], False, sent[-1:]
            )
            if c == 0:
                mine, theirs = rest
            sent.append(value)
        theirs, _ = lax.optimization_barrier((theirs, sent[-1]))
        theirs = lax.ppermute(theirs, "tp", [(0, 1), (1, 0)])
    else:
        (attention, facts), _ = attend(
            queries,
            keys_cache,
            values_cache,
            lengths,
            (routes.T, route_weight.T),
            1,
            [],
            True,
        )
        blocks = lax.all_gather(facts, "pool", axis=0)
        (slots, weights, largest), (pick, spread, slot_weight), _ = route(
            [blocks], expert_table, experts, rows, top, capacity, pools, [], True
        )
        head_rows = lax.all_to_all(
            attention, ("tp", "sub"), split_axis=1, concat_axis=0, tiled=True
        )
        partial = jnp.dot(head_rows, out_weight, preferred_element_type=F32)
        x_sum = lax.psum_scatter(partial, ("tp", "sub"), scatter_dimension=1, tiled=True)
        x_pool = x_sum.astype(BF16)
        attended = lax.all_to_all(x_pool, ("tp", "sub"), split_axis=0, concat_axis=1, tiled=True)
        x_part = lax.all_gather(x_pool, "pool", axis=0, tiled=True)
        xs = [lax.all_gather(x_part, "sub", axis=1, tiled=True)]
        held = load(gates + ups + downs, [], "load")
        held_down, sent, given = held[2 * chunks :], [], xs
        for c in range(chunks):
            value, given, *_ = gate_up(
                given, pick, held[c], held[chunks + c], c, own_rows, [], True
            )
            sent.append(value)

    def exchange(value):
        if tps == 2:
            return value, lax.ppermute(value, "tp", [(0, 1), (1, 0)])
        return lax.psum(value.astype(F32), "tp").astype(BF16), jnp.zeros_like(value)

    def combine(halved, extra=None):
        if not direct:
            value = lax.psum_scatter(halved[0], "pool", scatter_dimension=0, tiled=True)
            return lax.psum_scatter(value, "sub", scatter_dimension=1, tiled=True)
        own, other = halved
        received = xor_permute(other, "sub", subs, 1)
        if extra is not None:
            received, extra = lax.optimization_barrier((received, extra))
        pieces = split(own, received, pools)
        total = pieces[0]
        for k in range(1, pools):
            total = total + xor_permute(pieces[k], "pool", pools, k).astype(F32)
        return total if extra is None else total + extra

    def more(state):
        k, total = state
        k, *held_x = lax.optimization_barrier((k, *xs))
        x = arrange(held_x) if direct else held_x[0]
        pick, spread, slot_weight = pick_slots(k * capacity, slots, weights, capacity)
        gate = jnp.einsum("rd,efd->erf", x, w_gate, preferred_element_type=F32)
        up = jnp.einsum("rd,efd->erf", x, w_up, preferred_element_type=F32)
        both = jnp.concatenate([gate, up], axis=2).astype(BF16)
        both = both.reshape(experts * rows, 2 * hidden_units)
        sent = jnp.dot(pick, both, preferred_element_type=F32).astype(BF16)
        if tps == 2:
            both = sent.astype(F32) + lax.ppermute(sent, "tp", [(0, 1), (1, 0)]).astype(F32)
        else:
            both = lax.psum(sent.astype(F32), "tp")
        hidden = jax.nn.silu(both[:, :hidden_units]) * both[:, hidden_units:] * slot_weight
        spread = jnp.dot(spread, hidden.astype(BF16), preferred_element_type=F32).astype(BF16)
        spread = spread.reshape(experts, rows, hidden_units)
        value = jnp.einsum("erf,efd->rd", spread, w_down, preferred_element_type=F32)
        value = halves(value) if direct else [value]
        return k + 1, total + combine(value)

    both = [exchange(value) for value in sent]
    result = [None]
    for c in range(chunks):
        last = direct and c == chunks - 1
        result = down(
            *both[c], slot_weight, spread, held_down[c], result[0], c, last, not direct
        )
    if direct:
        theirs, largest, *result = lax.optimization_barrier((theirs, largest, *result))
        attended = join(mine, theirs)
    _, extra = lax.while_loop(
        lambda state: state[0] * capacity < largest[0, 0],
        more,
        (jnp.minimum(largest[0, 0], 1), jnp.zeros((pool_rows, half_width // subs), F32)),
    )
    if direct:
        return attended, combine(result, extra).astype(BF16)
    return attended, (combine(result) + extra).astype(BF16)


def solution(mesh):
    in_specs = (
        P(("grp", "pool", "tp", "sub"), None),
        P(("grp", "pool", "tp", "sub"), None, None),
        P(("grp", "pool", "tp", "sub"), None, None),
        P(("grp", "pool", "tp", "sub")),
        P(("tp", "sub"), None),
        P(("grp", "pool"), None),
        P(("grp", "pool"), None),
        P(),
        P("pool", "sub", "tp"),
        P("pool", "sub", "tp"),
        P("pool", "sub", "tp"),
    )
    out_specs = (P(("grp", "pool", "tp", "sub"), None), P(("grp", "pool"), ("tp", "sub")))
    return jax.shard_map(body, mesh=mesh, in_specs=in_specs, out_specs=out_specs, check_vma=False)
```

```python
import functools
import math

import jax
import jax.numpy as jnp
from jax import lax
from jax.experimental import pallas as pl
from jax.experimental.pallas import tpu as pltpu
from jax.sharding import PartitionSpec as P

HEAD_DIM = 128
KV_HEADS = 2
CHUNK = 128
FACT_LANES = 128

F32 = jnp.float32
BF16 = jnp.bfloat16


def dot_nt(a, b):
    return lax.dot_general(a, b, (((1,), (1,)), ((), ())), preferred_element_type=F32)


def dot_tn(a, b):
    return lax.dot_general(a, b, (((0,), (0,)), ((), ())), preferred_element_type=F32)


def dot_nn(a, b):
    return jnp.dot(a, b, preferred_element_type=F32)


def cost(microseconds):
    return pl.CostEstimate(
        flops=0, transcendentals=0, bytes_accessed=int(microseconds * 3_000_000)
    )


VMEM = pl.BlockSpec(memory_space=pltpu.VMEM)
SMEM = pl.BlockSpec(memory_space=pltpu.SMEM)
HBM = pl.BlockSpec(memory_space=pltpu.HBM)
ANY = pl.BlockSpec(memory_space=pl.ANY)


def in_vmem(value):
    return pltpu.with_memory_space_constraint(value, pltpu.VMEM)


def in_hbm(value):
    return pltpu.with_memory_space_constraint(value, pltpu.HBM)


def position():
    tp, sub = lax.axis_index("tp"), lax.axis_index("sub")
    subs = lax.axis_size("sub")
    return tp * subs + sub, tp, sub, lax.axis_index("pool"), subs


def call(kernel, name, inputs, specs, outs, out_specs=None, scratch=(), loads=(), anchors=(), us=2, roomy=False, begins=False):
    count_in, count_out, count_load = len(inputs), len(outs), len(loads)

    def source(ref, first):
        return ref if first is None else ref.at[:, first : first + CHUNK, :]

    def run(*refs):
        refs = list(refs)
        given = [refs.pop(0) for _ in range(count_in)]
        sources = [refs.pop(0) for _ in range(count_load)]
        del refs[: len(anchors)]
        results = [refs.pop(0) for _ in range(count_out)]
        targets = [refs.pop(0) for _ in range(count_load)]
        copies = []
        if loads:
            sems = refs.pop()
            for i, (_, first) in enumerate(loads):
                copies.append(
                    pltpu.make_async_copy(source(sources[i], first), targets[i], sems.at[i])
                )

        def begin():
            if copies:

                @pl.when(lax.axis_index("tp") >= 0)
                def _():
                    for copy in copies:
                        copy.start()

        if begins:
            kernel(begin, *given, *results, *refs)
        else:
            begin()
            kernel(*given, *results, *refs)
        for copy in copies:
            copy.wait()

    def loaded(array, first):
        shape = array.shape if first is None else (array.shape[0], CHUNK, array.shape[2])
        return pltpu.VMEM(shape, array.dtype)

    if not roomy:
        outs = [
            leaf if spec is HBM else pltpu.VMEM(leaf.shape, leaf.dtype)
            for leaf, spec in zip(outs, out_specs or [VMEM] * count_out)
        ]
    scratch = list(scratch) + ([pltpu.SemaphoreType.DMA((count_load,))] if loads else [])
    results = pl.pallas_call(
        run,
        in_specs=list(specs) + [HBM] * count_load + [ANY] * len(anchors),
        out_specs=list(out_specs or [VMEM] * count_out) + [VMEM] * count_load,
        out_shape=list(outs) + [loaded(*leaf) for leaf in loads],
        scratch_shapes=scratch,
        compiler_params=pltpu.CompilerParams(vmem_limit_bytes=(48 if roomy else 12) << 20),
        cost_estimate=cost(us),
        name=name,
    )(*inputs, *[in_hbm(leaf[0]) for leaf in loads], *anchors)
    return list(results[:count_out]), list(results[count_out:])


def attention_kernel(
    begin, q_hbm, lengths_hbm, route_hbm, share_hbm, k_hbm, v_hbm, *refs, pieces
):
    where = position()
    outs, facts_ref = refs[:pieces], refs[pieces]
    lengths, q_ref, route_ref, share_ref, k_ref, v_ref, sems, spread, gathered, flat = refs[
        pieces + 1 :
    ]
    rows, heads, _ = gathered.shape
    positions = k_ref.shape[1]
    group = heads // KV_HEADS
    small = [
        pltpu.make_async_copy(q_hbm, q_ref, sems.at[rows, 0]),
        pltpu.make_async_copy(lengths_hbm, lengths, sems.at[rows, 1]),
        pltpu.make_async_copy(route_hbm, route_ref, sems.at[rows + 1, 0]),
        pltpu.make_async_copy(share_hbm, share_ref, sems.at[rows + 1, 1]),
    ]
    for copy in small:
        copy.start()
    copies = []
    for row in range(rows):
        pair = [
            pltpu.make_async_copy(k_hbm.at[row], k_ref.at[row], sems.at[row, 0]),
            pltpu.make_async_copy(v_hbm.at[row], v_ref.at[row], sems.at[row, 1]),
        ]
        pair[0].start()
        pair[1].start()
        copies.append(pair)
    begin()
    for copy in small:
        copy.wait()
    share = share_ref[...]
    high = share.astype(BF16).astype(F32)
    middle = (share - high).astype(BF16).astype(F32)
    block = jnp.concatenate([route_ref[...].astype(F32), high, middle, share - high - middle], axis=0)
    count, lanes = block.shape[1], facts_ref.shape[1]
    block = jnp.concatenate([block, jnp.zeros((block.shape[0], -count % 128), F32)], axis=1).T
    blank = jnp.zeros((count, lanes - block.shape[1]), F32)
    facts_ref[...] = jnp.concatenate([block[:count], blank], axis=1).astype(BF16)
    queries = q_ref[...].astype(F32)
    for h in range(heads):
        spread[:, h, :] = queries[:, h * HEAD_DIM : (h + 1) * HEAD_DIM]
    column = lax.broadcasted_iota(jnp.int32, (group, positions), 1)
    for row in range(rows):
        valid = column < lengths[row]
        copies[row][0].wait()
        copies[row][1].wait()
        for j in range(KV_HEADS):
            lanes = slice(j * HEAD_DIM, (j + 1) * HEAD_DIM)
            own = spread[row, j * group : (j + 1) * group, :].astype(BF16)
            scores = dot_nt(own, k_ref[row, :, lanes])
            scores = jnp.where(valid, scores * (1.0 / math.sqrt(HEAD_DIM)), -1e30)
            top = jnp.max(scores, axis=1, keepdims=True)
            terms = jnp.where(valid, jnp.exp(scores - top), 0.0)
            total = jnp.sum(terms, axis=1, keepdims=True)
            value = dot_nn(terms.astype(BF16), v_ref[row, :, lanes]) / total
            gathered[row, j * group : (j + 1) * group, :] = value
    for h in range(heads):
        flat[:, h * HEAD_DIM : (h + 1) * HEAD_DIM] = gathered[:, h, :]
    width = heads * HEAD_DIM // pieces
    for k in range(pieces):
        start = pl.multiple_of(((where[0] ^ k) if pieces > 1 else 0) * width, width)
        outs[k][...] = flat[:, pl.ds(start, width)].astype(BF16)


def attend(queries, keys_cache, values_cache, lengths, facts, pieces, loads, roomy):
    rows, columns = queries.shape
    heads = columns // HEAD_DIM
    return call(
        functools.partial(attention_kernel, pieces=pieces),
        "attention",
        [in_hbm(a) for a in (queries, lengths, *facts, keys_cache, values_cache)],
        [HBM] * 6,
        [jax.ShapeDtypeStruct((rows, columns // pieces), BF16)] * pieces
        + [jax.ShapeDtypeStruct((facts[0].shape[1], FACT_LANES), BF16)],
        scratch=[
            pltpu.SMEM((rows,), jnp.int32),
            pltpu.VMEM(queries.shape, BF16),
            pltpu.VMEM(facts[0].shape, jnp.int32),
            pltpu.VMEM(facts[1].shape, F32),
            pltpu.VMEM(keys_cache.shape, BF16),
            pltpu.VMEM(values_cache.shape, BF16),
            pltpu.SemaphoreType.DMA((rows + 2, 2)),
            pltpu.VMEM((rows, heads, HEAD_DIM), F32),
            pltpu.VMEM((rows, heads, HEAD_DIM), F32),
            pltpu.VMEM((rows, columns), F32),
        ],
        loads=loads,
        us=4,
        roomy=roomy,
        begins=True,
    )


def route_kernel(table_ref, *refs, sources, experts, top):
    where = position()
    given, (slot_ref, weight_ref, largest_ref, *picks, held) = refs[:sources], refs[sources:]
    pools, pool_rows, lanes = held.shape
    if sources == 1:
        held[...] = given[0][...].astype(F32)
    else:
        for k in range(sources):
            width = given[k].shape[1]
            held[where[3] ^ where[0] ^ k] = given[k][:, width - lanes :].astype(F32)
    rows = pools * pool_rows
    total = table_ref.shape[1]
    groups, _, lanes = slot_ref.shape
    group = lanes // rows
    facts = held[...].reshape(rows, held.shape[2]).T
    shares = facts[top : 2 * top] + facts[2 * top : 3 * top] + facts[3 * top : 4 * top]
    routes = jnp.concatenate([facts[i : i + 1] for i in range(top)], axis=1).astype(jnp.int32)
    ids = lax.broadcasted_iota(jnp.int32, (total, top * rows), 0)
    hot = jnp.where(ids == routes, 1.0, 0.0).astype(BF16)
    table = jnp.broadcast_to(table_ref[...].astype(F32), (8, total)).astype(BF16)
    entry = dot_nn(table, hot)[0:1].astype(jnp.int32)

    first = lax.broadcasted_iota(jnp.int32, (pools, top * rows), 0) * experts
    inside = jnp.where((entry >= first) & (entry < first + experts), 1.0, 0.0)
    loads = jnp.sum(inside, axis=1, keepdims=True)
    largest_ref[...] = jnp.max(loads, axis=0, keepdims=True).astype(jnp.int32)

    lane = lax.broadcasted_iota(jnp.int32, (groups, lanes), 1)
    block = lax.broadcasted_iota(jnp.int32, (groups, lanes), 0)
    wanted = where[3] * experts + block * group + lane // rows
    weight = jnp.zeros((groups, lanes), F32)
    mask = jnp.zeros((groups, lanes), F32)
    for i in range(top):
        named = jnp.concatenate([entry[:, i * rows : (i + 1) * rows]] * group, axis=1)
        value = jnp.concatenate([shares[i : i + 1]] * group, axis=1)
        match = wanted == named
        mask = mask + jnp.where(match, 1.0, 0.0)
        weight = weight + jnp.where(match, value, 0.0)
    earlier = lax.broadcasted_iota(jnp.int32, (lanes, lanes), 0)
    later = lax.broadcasted_iota(jnp.int32, (lanes, lanes), 1)
    before = jnp.where(earlier < later, 1.0, 0.0).astype(BF16)
    rank = dot_nn(mask.astype(BF16), before)
    base = jnp.zeros((1, 1), F32)
    counts = jnp.sum(mask, axis=1, keepdims=True)
    slots = []
    for g in range(groups):
        slots.append(jnp.where(mask[g : g + 1] > 0.0, rank[g : g + 1] + base, -1.0))
        slot_ref[g] = slots[g].astype(jnp.int32)
        weight_ref[g] = weight[g : g + 1]
        base = base + counts[g : g + 1]
    fill_picks(slots, [weight[g : g + 1] for g in range(groups)], *picks)


def fill_picks(slots, weights, pick_ref, spread_ref, slot_weight_ref):
    groups, lanes = len(slots), slots[0].shape[1]
    capacity = pick_ref.shape[0]
    rows = jnp.concatenate(slots + [slots[0]] * (-groups % 8), axis=0).T
    place = lax.broadcasted_iota(jnp.int32, (capacity, lanes), 0).astype(F32)
    along = lax.broadcasted_iota(jnp.int32, (lanes, capacity), 1).astype(F32)
    total = jnp.zeros((capacity, lanes), F32)
    for g in range(groups):
        hit = place == slots[g]
        part = slice(g * lanes, (g + 1) * lanes)
        pick_ref[:, part] = jnp.where(hit, 1.0, 0.0).astype(BF16)
        spread_ref[part, :] = jnp.where(along == rows[:, g : g + 1], 1.0, 0.0).astype(BF16)
        total = total + jnp.where(hit, weights[g], 0.0)
    slot_weight_ref[...] = jnp.sum(total, axis=1, keepdims=True)


def pick_shapes(capacity, pairs):
    return [
        jax.ShapeDtypeStruct((capacity, pairs), BF16),
        jax.ShapeDtypeStruct((pairs, capacity), BF16),
        jax.ShapeDtypeStruct((capacity, 1), F32),
    ]


def route(blocks, expert_table, experts, rows, top, capacity, pools, loads, roomy):
    group = max(1, min(experts, 256 // rows))
    shape = (experts // group, 1, group * rows)
    results, held = call(
        functools.partial(route_kernel, sources=len(blocks), experts=experts, top=top),
        "route",
        [expert_table.reshape(1, -1), *blocks],
        [VMEM] + [VMEM] * len(blocks),
        [
            jax.ShapeDtypeStruct(shape, jnp.int32),
            jax.ShapeDtypeStruct(shape, F32),
            jax.ShapeDtypeStruct((1, 1), jnp.int32),
            *pick_shapes(capacity, experts * rows),
        ],
        scratch=[pltpu.VMEM((pools, rows // pools, FACT_LANES), F32)],
        loads=loads,
        us=6,
        roomy=roomy,
    )
    return results[:3], results[3:], held


def pick_slots(shift, slots, weights, capacity):
    def kernel(shift_ref, *refs):
        slot_ref, weight_ref, *picks = refs
        groups = range(slot_ref.shape[0])
        shifted = [(slot_ref[g] - shift_ref[0]).astype(F32) for g in groups]
        fill_picks(shifted, [weight_ref[g] for g in groups], *picks)

    return call(
        kernel,
        "pick",
        [shift.reshape(1), slots, weights],
        [SMEM, VMEM, VMEM],
        pick_shapes(capacity, slots.shape[0] * slots.shape[2]),
        roomy=True,
    )[0]


def project_kernel(*refs, sources):
    where = position()
    inputs, (own_ref, sent_ref, w_ref) = refs[:sources], refs[sources : sources + 3]
    kept, near, far, held = refs[sources + 3 :]
    own_rows = inputs[0].shape[0]
    count = sources * own_rows
    half = kept.shape[1]
    facts = jnp.where(where[0] == 0, own_ref[...].astype(F32), sent_ref[...].astype(F32))
    facts = facts.astype(BF16)
    held[...] = facts
    stacked = jnp.concatenate([ref[...].astype(F32) for ref in inputs], axis=0).astype(BF16)
    target = lax.broadcasted_iota(jnp.int32, (count, count), 0)
    origin = lax.broadcasted_iota(jnp.int32, (count, count), 1)
    order = (target ^ (where[0] * own_rows)) == origin
    x = dot_nn(jnp.where(order, 1.0, 0.0).astype(BF16), stacked).astype(BF16)
    for k, out in ((1, far), (0, near)):
        start = pl.multiple_of((where[1] ^ k) * half, half)
        value = dot_nn(x, w_ref[:, pl.ds(start, half)])
        out[:, :half] = value.astype(BF16)
        out[:, half:] = facts
        if k == 0:
            kept[...] = value


def project(inputs, facts, out_weight, loads, anchors):
    sources = len(inputs)
    count, half = sources * inputs[0].shape[0], out_weight.shape[1] // 2
    sent = jax.ShapeDtypeStruct((count, half + FACT_LANES), BF16)
    return call(
        functools.partial(project_kernel, sources=sources),
        "project",
        [*inputs, *facts, out_weight],
        [VMEM] * (sources + 3),
        [
            jax.ShapeDtypeStruct((count, half), F32),
            sent,
            sent,
            jax.ShapeDtypeStruct((count, FACT_LANES), BF16),
        ],
        loads=loads,
        anchors=anchors,
    )


def add_kernel(kept, *refs):
    total = kept[...]
    for ref in refs[:-1]:
        total = total + ref[:, : total.shape[1]].astype(F32)
    refs[-1][...] = total.astype(BF16)


def add(kept, others):
    outs = [jax.ShapeDtypeStruct(kept.shape, BF16)]
    return call(add_kernel, "add", [kept, *others], [VMEM] * (1 + len(others)), outs)[0][0]


def gate_up_kernel(*refs, sources, first, index):
    where = position()
    inputs, refs = refs[:sources], refs[sources:]
    pick_ref, g_ref, u_ref, out_ref = refs[:4]
    if first:
        columns_ref, mine_ref, theirs_ref, x, both = refs[4:]
        count = inputs[0].shape[0]
        own_rows = mine_ref.shape[0]
        row = lax.broadcasted_iota(jnp.int32, (own_rows, count), 0)
        place = lax.broadcasted_iota(jnp.int32, (own_rows, count), 1)
        for out, shard in ((mine_ref, where[0]), (theirs_ref, where[0] ^ where[4])):
            chosen = jnp.where(place == row + shard * own_rows, 1.0, 0.0).astype(BF16)
            out[...] = dot_nn(chosen, inputs[0][...]).astype(BF16)
        for k in range(sources):
            start = pl.multiple_of((where[3] ^ k) * count, count) if sources > 1 else 0
            x[pl.ds(start, count), :] = inputs[k][...].astype(F32)
        columns_ref[...] = x[...].T.astype(BF16)
    else:
        (columns_ref,), (both,) = inputs, refs[4:]
    experts, _, depth = g_ref.shape
    rows = columns_ref.shape[1]
    for base, w_ref in ((0, g_ref), (CHUNK, u_ref)):
        units = slice(index * CHUNK, (index + 1) * CHUNK) if w_ref.shape[1] > CHUNK else slice(None)
        value = dot_nn(w_ref[:, units, :].reshape(experts * CHUNK, depth), columns_ref[...]).astype(BF16)
        for e in range(experts):
            both[base : base + CHUNK, e * rows : (e + 1) * rows] = value[
                e * CHUNK : (e + 1) * CHUNK
            ]
    out_ref[...] = dot_nt(pick_ref[...], both[...]).astype(BF16)


def gate_up(xs, pick, w_gate, w_up, index, own_rows, loads, roomy, anchors=()):
    first = index == 0
    experts, _, depth = w_gate.shape
    rows = pick.shape[1] // experts
    outs = [jax.ShapeDtypeStruct((pick.shape[0], 2 * CHUNK), BF16)]
    scratch = [pltpu.VMEM((2 * CHUNK, experts * rows), BF16)]
    if first:
        outs.append(jax.ShapeDtypeStruct((depth, rows), BF16))
        outs += [jax.ShapeDtypeStruct((own_rows, depth), BF16)] * 2
        scratch.insert(0, pltpu.VMEM((rows, depth), F32))
    results, held = call(
        functools.partial(gate_up_kernel, sources=len(xs), first=first, index=index),
        f"gate_up_{index}",
        [*xs, pick, w_gate, w_up],
        [VMEM] * (len(xs) + 3),
        outs,
        scratch=scratch,
        loads=loads,
        anchors=anchors,
        us=4,
        roomy=roomy,
    )
    return results[0], results[1:2] if first else xs, results[2:], held


def down_kernel(own_ref, other_ref, weight_ref, spread_ref, d_ref, *refs, carried, index):
    before, outs = refs[:carried], refs[carried:]
    experts, _, depth = d_ref.shape
    rows = spread_ref.shape[0] // experts
    both = own_ref[...].astype(F32) + other_ref[...].astype(F32)
    gate, up = both[:, :CHUNK], both[:, CHUNK:]
    hidden = (gate / (1.0 + jnp.exp(-gate)) * up * weight_ref[...]).astype(BF16)
    spread = dot_nn(spread_ref[...], hidden).astype(BF16)
    left = jnp.concatenate([spread[e * rows : (e + 1) * rows] for e in range(experts)], axis=1)
    units = slice(index * CHUNK, (index + 1) * CHUNK)
    total = dot_nn(left, d_ref[:, units, :].reshape(experts * CHUNK, depth))
    if carried:
        total = total + before[0][...]
    if len(outs) == 1:
        outs[0][...] = total
    else:
        half = depth // 2
        low, high = total[:, :half], total[:, half:]
        mine = lax.axis_index("sub") == 0
        outs[0][...] = jnp.where(mine, low, high)
        outs[1][...] = jnp.where(mine, high, low)


def down(own, other, slot_weight, spread, w_down, before, index, halved, roomy):
    experts, _, depth = w_down.shape
    rows = spread.shape[0] // experts
    carried = [] if before is None else [before]
    parts = 2 if halved else 1
    return call(
        functools.partial(down_kernel, carried=len(carried), index=index),
        f"down_{index}",
        [own, other, slot_weight, spread, w_down, *carried],
        [VMEM] * (5 + len(carried)),
        [jax.ShapeDtypeStruct((rows, depth // parts), F32)] * parts,
        us=3,
        roomy=roomy,
    )[0]


def load(loads, anchors, name, roomy=False):
    return call(
        lambda: None, name, [], [], [], loads=loads, anchors=anchors, us=2 * len(loads), roomy=roomy
    )[1]


def arrange_kernel(*refs):
    inputs, out_ref = refs[:-1], refs[-1]
    count = inputs[0].shape[0]
    for k, ref in enumerate(inputs):
        start = pl.multiple_of((lax.axis_index("pool") ^ k) * count, count)
        out_ref[pl.ds(start, count), :] = ref[...]


def arrange(blocks):
    shape = (len(blocks) * blocks[0].shape[0], blocks[0].shape[1])
    outs = [jax.ShapeDtypeStruct(shape, BF16)]
    return call(arrange_kernel, "arrange", blocks, [VMEM] * len(blocks), outs, roomy=True)[0][0]


def halves_kernel(value_ref, own_ref, other_ref):
    half = own_ref.shape[1]
    low, high = value_ref[:, :half], value_ref[:, half:]
    mine = lax.axis_index("sub") == 0
    own_ref[...] = jnp.where(mine, low, high)
    other_ref[...] = jnp.where(mine, high, low)


def halves(value):
    outs = [jax.ShapeDtypeStruct((value.shape[0], value.shape[1] // 2), F32)] * 2
    return call(halves_kernel, "halves", [value], [VMEM], outs, roomy=True)[0]


def join_kernel(mine_ref, theirs_ref, out_hbm, out_ref, sem):
    half = mine_ref.shape[1]
    low = lax.axis_index("tp") == 0
    mine, theirs = mine_ref[...].astype(F32), theirs_ref[...].astype(F32)
    out_ref[:, :half] = jnp.where(low, mine, theirs).astype(BF16)
    out_ref[:, half:] = jnp.where(low, theirs, mine).astype(BF16)
    copy = pltpu.make_async_copy(out_ref, out_hbm, sem)
    copy.start()
    copy.wait()


def join(mine, theirs):
    shape = (mine.shape[0], 2 * mine.shape[1])
    return call(
        join_kernel,
        "join",
        [mine, theirs],
        [VMEM, VMEM],
        [jax.ShapeDtypeStruct(shape, BF16)],
        out_specs=[HBM],
        scratch=[pltpu.VMEM(shape, BF16), pltpu.SemaphoreType.DMA],
    )[0][0]


def split_kernel(own_ref, other_ref, *outs):
    count = outs[0].shape[0]
    pool = lax.axis_index("pool")
    for k in range(len(outs)):
        row = pl.ds(pl.multiple_of((pool ^ k) * count, count), count)
        outs[k][...] = (own_ref[row, :] + other_ref[row, :]).astype(outs[k].dtype)


def split(own, other, pieces):
    shape = (own.shape[0] // pieces, own.shape[1])
    return call(
        split_kernel,
        "split",
        [own, other],
        [VMEM, VMEM],
        [jax.ShapeDtypeStruct(shape, F32 if k == 0 else BF16) for k in range(pieces)],
    )[0]


def xor_permute(value, axes, count, k):
    return lax.ppermute(value, axes, [(i, i ^ k) for i in range(count)])


def body(
    queries,
    keys_cache,
    values_cache,
    lengths,
    out_weight,
    routes,
    route_weight,
    expert_table,
    w_gate,
    w_up,
    w_down,
):
    pools, tps, subs = lax.axis_size("pool"), lax.axis_size("tp"), lax.axis_size("sub")
    pool, tp, sub = lax.axis_index("pool"), lax.axis_index("tp"), lax.axis_index("sub")
    shards = tps * subs
    shard = tp * subs + sub
    direct = tps == 2 and subs == 2 and pools == 4
    own_rows = queries.shape[0]
    pool_rows = own_rows * shards
    rows = pool_rows * pools
    experts, hidden_units, half_width = w_gate.shape
    top = routes.shape[1]

    capacity = -(-rows * top * 13 // (8 * pools * 16)) * 16
    gates, ups, downs = [
        [(w, c) for c in range(0, hidden_units, CHUNK)] for w in (w_gate, w_up, w_down)
    ]
    chunks = len(gates)

    if direct:
        axes = ("tp", "sub")
        (*pieces, facts), (out_held,) = attend(
            queries,
            keys_cache,
            values_cache,
            lengths,
            (routes.T, route_weight.T),
            shards,
            [(out_weight, None)],
            False,
        )
        inputs = [pieces[0]] + [xor_permute(pieces[k], axes, shards, k) for k in range(1, shards)]
        pairs = [(i, i ^ (shards * (i % shards))) for i in range(pools * shards) if i % shards]
        other_facts = lax.ppermute(facts, ("pool", "tp", "sub"), pairs)
        (kept, near, far, block), _ = project(inputs, [facts, other_facts], out_held, [], [])
        gate_1, up_1 = gate_2, up_2 = in_vmem(w_gate), in_vmem(w_up)
        gate_0, up_0 = load([gates[0], ups[0]], [near], "load_b")
        blocks = [block]
        for k in range(1, shards):
            blocks.append(xor_permute(near if k < subs else far, axes, shards, k))
        x_sum = add(kept, blocks[1:])
        x_half, gate_0 = lax.optimization_barrier((x_sum, gate_0))
        xs = [x_half] + [xor_permute(x_half, "pool", pools, k) for k in range(1, pools)]
        blocks, _ = lax.optimization_barrier((blocks, x_half))
        (slots, weights, largest), (pick, spread, slot_weight), _ = route(
            blocks,
            expert_table,
            experts,
            rows,
            top,
            capacity,
            pools,
            [],
            False,
        )
        held = [(gate_0, up_0), (gate_1, up_1), (gate_2, up_2)]
        sent, given = [], xs
        for c in range(chunks):
            value, given, rest, _ = gate_up(
                given, pick, *held[c], c, own_rows, [], False, sent[-1:]
            )
            if c == 0:
                mine, theirs = rest
            sent.append(value)
        theirs, _ = lax.optimization_barrier((theirs, sent[-1]))
        theirs = lax.ppermute(theirs, "tp", [(0, 1), (1, 0)])
    else:
        (attention, facts), _ = attend(
            queries,
            keys_cache,
            values_cache,
            lengths,
            (routes.T, route_weight.T),
            1,
            [],
            True,
        )
        blocks = lax.all_gather(facts, "pool", axis=0)
        (slots, weights, largest), (pick, spread, slot_weight), _ = route(
            [blocks], expert_table, experts, rows, top, capacity, pools, [], True
        )
        head_rows = lax.all_to_all(
            attention, ("tp", "sub"), split_axis=1, concat_axis=0, tiled=True
        )
        partial = jnp.dot(head_rows, out_weight, preferred_element_type=F32)
        x_sum = lax.psum_scatter(partial, ("tp", "sub"), scatter_dimension=1, tiled=True)
        x_pool = x_sum.astype(BF16)
        attended = lax.all_to_all(x_pool, ("tp", "sub"), split_axis=0, concat_axis=1, tiled=True)
        x_part = lax.all_gather(x_pool, "pool", axis=0, tiled=True)
        xs = [lax.all_gather(x_part, "sub", axis=1, tiled=True)]
        held = load(gates + ups, [], "load")
        sent, given = [], xs
        for c in range(chunks):
            value, given, *_ = gate_up(
                given, pick, held[c], held[chunks + c], c, own_rows, [], True
            )
            sent.append(value)

    def exchange(value):
        if tps == 2:
            return value, lax.ppermute(value, "tp", [(0, 1), (1, 0)])
        return lax.psum(value.astype(F32), "tp").astype(BF16), jnp.zeros_like(value)

    def combine(halved, extra=None):
        if not direct:
            value = lax.psum_scatter(halved[0], "pool", scatter_dimension=0, tiled=True)
            return lax.psum_scatter(value, "sub", scatter_dimension=1, tiled=True)
        own, other = halved
        received = xor_permute(other, "sub", subs, 1)
        if extra is not None:
            received, extra = lax.optimization_barrier((received, extra))
        pieces = split(own, received, pools)
        total = pieces[0]
        for k in range(1, pools):
            total = total + xor_permute(pieces[k], "pool", pools, k).astype(F32)
        return total if extra is None else total + extra

    def more(state):
        k, total = state
        k, *held_x = lax.optimization_barrier((k, *xs))
        x = arrange(held_x) if direct else held_x[0]
        pick, spread, slot_weight = pick_slots(k * capacity, slots, weights, capacity)
        gate = jnp.einsum("rd,efd->erf", x, w_gate, preferred_element_type=F32)
        up = jnp.einsum("rd,efd->erf", x, w_up, preferred_element_type=F32)
        both = jnp.concatenate([gate, up], axis=2).astype(BF16)
        both = both.reshape(experts * rows, 2 * hidden_units)
        sent = jnp.dot(pick, both, preferred_element_type=F32).astype(BF16)
        if tps == 2:
            both = sent.astype(F32) + lax.ppermute(sent, "tp", [(0, 1), (1, 0)]).astype(F32)
        else:
            both = lax.psum(sent.astype(F32), "tp")
        hidden = jax.nn.silu(both[:, :hidden_units]) * both[:, hidden_units:] * slot_weight
        spread = jnp.dot(spread, hidden.astype(BF16), preferred_element_type=F32).astype(BF16)
        spread = spread.reshape(experts, rows, hidden_units)
        value = jnp.einsum("erf,efd->rd", spread, w_down, preferred_element_type=F32)
        value = halves(value) if direct else [value]
        return k + 1, total + combine(value)

    both = [exchange(value) for value in sent]
    result = [None]
    for c in range(chunks):
        last = direct and c == chunks - 1
        result = down(
            *both[c], slot_weight, spread, in_vmem(w_down), result[0], c, last, not direct
        )
    if direct:
        theirs, largest, *result = lax.optimization_barrier((theirs, largest, *result))
        attended = join(mine, theirs)
    _, extra = lax.while_loop(
        lambda state: state[0] * capacity < largest[0, 0],
        more,
        (jnp.minimum(largest[0, 0], 1), jnp.zeros((pool_rows, half_width // subs), F32)),
    )
    if direct:
        return attended, combine(result, extra).astype(BF16)
    return attended, (combine(result) + extra).astype(BF16)


def solution(mesh):
    in_specs = (
        P(("grp", "pool", "tp", "sub"), None),
        P(("grp", "pool", "tp", "sub"), None, None),
        P(("grp", "pool", "tp", "sub"), None, None),
        P(("grp", "pool", "tp", "sub")),
        P(("tp", "sub"), None),
        P(("grp", "pool"), None),
        P(("grp", "pool"), None),
        P(),
        P("pool", "sub", "tp"),
        P("pool", "sub", "tp"),
        P("pool", "sub", "tp"),
    )
    out_specs = (P(("grp", "pool", "tp", "sub"), None), P(("grp", "pool"), ("tp", "sub")))
    return jax.shard_map(body, mesh=mesh, in_specs=in_specs, out_specs=out_specs, check_vma=False)
```

```python
import functools
import math

import jax
import jax.numpy as jnp
from jax import lax
from jax.experimental import pallas as pl
from jax.experimental.pallas import tpu as pltpu
from jax.sharding import PartitionSpec as P

HEAD_DIM = 128
KV_HEADS = 2
CHUNK = 128
FACT_LANES = 128

F32 = jnp.float32
BF16 = jnp.bfloat16


def dot_nt(a, b):
    return lax.dot_general(a, b, (((1,), (1,)), ((), ())), preferred_element_type=F32)


def dot_tn(a, b):
    return lax.dot_general(a, b, (((0,), (0,)), ((), ())), preferred_element_type=F32)


def dot_nn(a, b):
    return jnp.dot(a, b, preferred_element_type=F32)


def cost(microseconds):
    return pl.CostEstimate(
        flops=0, transcendentals=0, bytes_accessed=int(microseconds * 3_000_000)
    )


VMEM = pl.BlockSpec(memory_space=pltpu.VMEM)
SMEM = pl.BlockSpec(memory_space=pltpu.SMEM)
HBM = pl.BlockSpec(memory_space=pltpu.HBM)
ANY = pl.BlockSpec(memory_space=pl.ANY)


def in_vmem(value):
    return pltpu.with_memory_space_constraint(value, pltpu.VMEM)


def in_hbm(value):
    return pltpu.with_memory_space_constraint(value, pltpu.HBM)


def position():
    tp, sub = lax.axis_index("tp"), lax.axis_index("sub")
    subs = lax.axis_size("sub")
    return tp * subs + sub, tp, sub, lax.axis_index("pool"), subs


def call(kernel, name, inputs, specs, outs, out_specs=None, scratch=(), loads=(), anchors=(), us=2, roomy=False, begins=False):
    count_in, count_out, count_load = len(inputs), len(outs), len(loads)

    def source(ref, first):
        return ref if first is None else ref.at[:, first : first + CHUNK, :]

    def run(*refs):
        refs = list(refs)
        given = [refs.pop(0) for _ in range(count_in)]
        sources = [refs.pop(0) for _ in range(count_load)]
        del refs[: len(anchors)]
        results = [refs.pop(0) for _ in range(count_out)]
        targets = [refs.pop(0) for _ in range(count_load)]
        copies = []
        if loads:
            sems = refs.pop()
            for i, (_, first) in enumerate(loads):
                copies.append(
                    pltpu.make_async_copy(source(sources[i], first), targets[i], sems.at[i])
                )

        def begin():
            if copies:

                @pl.when(lax.axis_index("tp") >= 0)
                def _():
                    for copy in copies:
                        copy.start()

        if begins:
            kernel(begin, *given, *results, *refs)
        else:
            begin()
            kernel(*given, *results, *refs)
        for copy in copies:
            copy.wait()

    def loaded(array, first):
        shape = array.shape if first is None else (array.shape[0], CHUNK, array.shape[2])
        return pltpu.VMEM(shape, array.dtype)

    if not roomy:
        outs = [
            leaf if spec is HBM else pltpu.VMEM(leaf.shape, leaf.dtype)
            for leaf, spec in zip(outs, out_specs or [VMEM] * count_out)
        ]
    scratch = list(scratch) + ([pltpu.SemaphoreType.DMA((count_load,))] if loads else [])
    results = pl.pallas_call(
        run,
        in_specs=list(specs) + [HBM] * count_load + [ANY] * len(anchors),
        out_specs=list(out_specs or [VMEM] * count_out) + [VMEM] * count_load,
        out_shape=list(outs) + [loaded(*leaf) for leaf in loads],
        scratch_shapes=scratch,
        compiler_params=pltpu.CompilerParams(vmem_limit_bytes=(48 if roomy else 12) << 20),
        cost_estimate=cost(us),
        name=name,
    )(*inputs, *[in_hbm(leaf[0]) for leaf in loads], *anchors)
    return list(results[:count_out]), list(results[count_out:])


def attention_kernel(
    begin, q_hbm, lengths_hbm, route_hbm, share_hbm, k_hbm, v_hbm, *refs, pieces
):
    where = position()
    outs, facts_ref = refs[:pieces], refs[pieces]
    lengths, q_ref, route_ref, share_ref, k_ref, v_ref, sems, spread, gathered, flat = refs[
        pieces + 1 :
    ]
    rows, heads, _ = gathered.shape
    positions = k_ref.shape[1]
    group = heads // KV_HEADS
    small = [
        pltpu.make_async_copy(q_hbm, q_ref, sems.at[rows, 0]),
        pltpu.make_async_copy(lengths_hbm, lengths, sems.at[rows, 1]),
        pltpu.make_async_copy(route_hbm, route_ref, sems.at[rows + 1, 0]),
        pltpu.make_async_copy(share_hbm, share_ref, sems.at[rows + 1, 1]),
    ]
    for copy in small:
        copy.start()
    copies = []
    for row in range(rows):
        pair = [
            pltpu.make_async_copy(k_hbm.at[row], k_ref.at[row], sems.at[row, 0]),
            pltpu.make_async_copy(v_hbm.at[row], v_ref.at[row], sems.at[row, 1]),
        ]
        pair[0].start()
        pair[1].start()
        copies.append(pair)
    begin()
    for copy in small:
        copy.wait()
    share = share_ref[...]
    high = share.astype(BF16).astype(F32)
    middle = (share - high).astype(BF16).astype(F32)
    block = jnp.concatenate([route_ref[...].astype(F32), high, middle, share - high - middle], axis=0)
    count, lanes = block.shape[1], facts_ref.shape[1]
    block = jnp.concatenate([block, jnp.zeros((block.shape[0], -count % 128), F32)], axis=1).T
    blank = jnp.zeros((count, lanes - block.shape[1]), F32)
    facts_ref[...] = jnp.concatenate([block[:count], blank], axis=1).astype(BF16)
    queries = q_ref[...].astype(F32)
    for h in range(heads):
        spread[:, h, :] = queries[:, h * HEAD_DIM : (h + 1) * HEAD_DIM]
    column = lax.broadcasted_iota(jnp.int32, (group, positions), 1)
    for pair in copies:
        pair[0].wait()
        pair[1].wait()
    cases = [(row, j) for row in range(rows) for j in range(KV_HEADS)]
    lanes = [slice(j * HEAD_DIM, (j + 1) * HEAD_DIM) for j in range(KV_HEADS)]
    scores, terms, totals = [], [], []
    for row, j in cases:
        own = spread[row, j * group : (j + 1) * group, :].astype(BF16)
        scores.append(dot_nt(own, k_ref[row, :, lanes[j]]))
    for (row, j), score in zip(cases, scores):
        valid = column < lengths[row]
        score = jnp.where(valid, score * (1.0 / math.sqrt(HEAD_DIM)), -1e30)
        top = jnp.max(score, axis=1, keepdims=True)
        terms.append(jnp.where(valid, jnp.exp(score - top), 0.0))
        totals.append(jnp.sum(terms[-1], axis=1, keepdims=True))
    for (row, j), term, total in zip(cases, terms, totals):
        value = dot_nn(term.astype(BF16), v_ref[row, :, lanes[j]]) / total
        gathered[row, j * group : (j + 1) * group, :] = value
    for h in range(heads):
        flat[:, h * HEAD_DIM : (h + 1) * HEAD_DIM] = gathered[:, h, :]
    width = heads * HEAD_DIM // pieces
    for k in range(pieces):
        start = pl.multiple_of(((where[0] ^ k) if pieces > 1 else 0) * width, width)
        outs[k][...] = flat[:, pl.ds(start, width)].astype(BF16)


def attend(queries, keys_cache, values_cache, lengths, facts, pieces, loads, roomy):
    rows, columns = queries.shape
    heads = columns // HEAD_DIM
    return call(
        functools.partial(attention_kernel, pieces=pieces),
        "attention",
        [in_hbm(a) for a in (queries, lengths, *facts, keys_cache, values_cache)],
        [HBM] * 6,
        [jax.ShapeDtypeStruct((rows, columns // pieces), BF16)] * pieces
        + [jax.ShapeDtypeStruct((facts[0].shape[1], FACT_LANES), BF16)],
        scratch=[
            pltpu.SMEM((rows,), jnp.int32),
            pltpu.VMEM(queries.shape, BF16),
            pltpu.VMEM(facts[0].shape, jnp.int32),
            pltpu.VMEM(facts[1].shape, F32),
            pltpu.VMEM(keys_cache.shape, BF16),
            pltpu.VMEM(values_cache.shape, BF16),
            pltpu.SemaphoreType.DMA((rows + 2, 2)),
            pltpu.VMEM((rows, heads, HEAD_DIM), F32),
            pltpu.VMEM((rows, heads, HEAD_DIM), F32),
            pltpu.VMEM((rows, columns), F32),
        ],
        loads=loads,
        us=4,
        roomy=roomy,
        begins=True,
    )


def route_kernel(table_ref, *refs, sources, experts, top):
    where = position()
    given, (slot_ref, weight_ref, largest_ref, *picks, held) = refs[:sources], refs[sources:]
    pools, pool_rows, lanes = held.shape
    if sources == 1:
        held[...] = given[0][...].astype(F32)
    else:
        for k in range(sources):
            width = given[k].shape[1]
            held[where[3] ^ k] = given[k][:, width - lanes :].astype(F32)
    rows = pools * pool_rows
    total = table_ref.shape[1]
    groups, _, lanes = slot_ref.shape
    group = lanes // rows
    facts = held[...].reshape(rows, held.shape[2]).T
    shares = facts[top : 2 * top] + facts[2 * top : 3 * top] + facts[3 * top : 4 * top]
    routes = jnp.concatenate([facts[i : i + 1] for i in range(top)], axis=1).astype(jnp.int32)
    ids = lax.broadcasted_iota(jnp.int32, (total, top * rows), 0)
    hot = jnp.where(ids == routes, 1.0, 0.0).astype(BF16)
    table = jnp.broadcast_to(table_ref[...].astype(F32), (8, total)).astype(BF16)
    entry = dot_nn(table, hot)[0:1].astype(jnp.int32)

    first = lax.broadcasted_iota(jnp.int32, (pools, top * rows), 0) * experts
    inside = jnp.where((entry >= first) & (entry < first + experts), 1.0, 0.0)
    loads = jnp.sum(inside, axis=1, keepdims=True)
    largest_ref[...] = jnp.max(loads, axis=0, keepdims=True).astype(jnp.int32)

    lane = lax.broadcasted_iota(jnp.int32, (groups, lanes), 1)
    block = lax.broadcasted_iota(jnp.int32, (groups, lanes), 0)
    wanted = where[3] * experts + block * group + lane // rows
    weight = jnp.zeros((groups, lanes), F32)
    mask = jnp.zeros((groups, lanes), F32)
    for i in range(top):
        named = jnp.concatenate([entry[:, i * rows : (i + 1) * rows]] * group, axis=1)
        value = jnp.concatenate([shares[i : i + 1]] * group, axis=1)
        match = wanted == named
        mask = mask + jnp.where(match, 1.0, 0.0)
        weight = weight + jnp.where(match, value, 0.0)
    earlier = lax.broadcasted_iota(jnp.int32, (lanes, lanes), 0)
    later = lax.broadcasted_iota(jnp.int32, (lanes, lanes), 1)
    before = jnp.where(earlier < later, 1.0, 0.0).astype(BF16)
    rank = dot_nn(mask.astype(BF16), before)
    base = jnp.zeros((1, 1), F32)
    counts = jnp.sum(mask, axis=1, keepdims=True)
    slots = []
    for g in range(groups):
        slots.append(jnp.where(mask[g : g + 1] > 0.0, rank[g : g + 1] + base, -1.0))
        slot_ref[g] = slots[g].astype(jnp.int32)
        weight_ref[g] = weight[g : g + 1]
        base = base + counts[g : g + 1]
    fill_picks(slots, [weight[g : g + 1] for g in range(groups)], *picks)


def fill_picks(slots, weights, pick_ref, spread_ref, slot_weight_ref):
    groups, lanes = len(slots), slots[0].shape[1]
    capacity = pick_ref.shape[0]
    rows = jnp.concatenate(slots + [slots[0]] * (-groups % 8), axis=0).T
    place = lax.broadcasted_iota(jnp.int32, (capacity, lanes), 0).astype(F32)
    along = lax.broadcasted_iota(jnp.int32, (lanes, capacity), 1).astype(F32)
    total = jnp.zeros((capacity, lanes), F32)
    for g in range(groups):
        hit = place == slots[g]
        part = slice(g * lanes, (g + 1) * lanes)
        pick_ref[:, part] = jnp.where(hit, 1.0, 0.0).astype(BF16)
        spread_ref[part, :] = jnp.where(along == rows[:, g : g + 1], 1.0, 0.0).astype(BF16)
        total = total + jnp.where(hit, weights[g], 0.0)
    slot_weight_ref[...] = jnp.sum(total, axis=1, keepdims=True)


def pick_shapes(capacity, pairs):
    return [
        jax.ShapeDtypeStruct((capacity, pairs), BF16),
        jax.ShapeDtypeStruct((pairs, capacity), BF16),
        jax.ShapeDtypeStruct((capacity, 1), F32),
    ]


def route(blocks, expert_table, experts, rows, top, capacity, pools, loads, roomy):
    group = max(1, min(experts, 256 // rows))
    shape = (experts // group, 1, group * rows)
    results, held = call(
        functools.partial(route_kernel, sources=len(blocks), experts=experts, top=top),
        "route",
        [expert_table.reshape(1, -1), *blocks],
        [VMEM] + [VMEM] * len(blocks),
        [
            jax.ShapeDtypeStruct(shape, jnp.int32),
            jax.ShapeDtypeStruct(shape, F32),
            jax.ShapeDtypeStruct((1, 1), jnp.int32),
            *pick_shapes(capacity, experts * rows),
        ],
        scratch=[pltpu.VMEM((pools, rows // pools, FACT_LANES), F32)],
        loads=loads,
        us=6,
        roomy=roomy,
    )
    return results[:3], results[3:], held


def pick_slots(shift, slots, weights, capacity):
    def kernel(shift_ref, *refs):
        slot_ref, weight_ref, *picks = refs
        groups = range(slot_ref.shape[0])
        shifted = [(slot_ref[g] - shift_ref[0]).astype(F32) for g in groups]
        fill_picks(shifted, [weight_ref[g] for g in groups], *picks)

    return call(
        kernel,
        "pick",
        [shift.reshape(1), slots, weights],
        [SMEM, VMEM, VMEM],
        pick_shapes(capacity, slots.shape[0] * slots.shape[2]),
        roomy=True,
    )[0]


def project_kernel(*refs, sources):
    where = position()
    inputs, (w_ref, kept, near, far) = refs[:sources], refs[sources:]
    own_rows = inputs[0].shape[0]
    count = sources * own_rows
    half = kept.shape[1]
    stacked = jnp.concatenate([ref[...].astype(F32) for ref in inputs], axis=0).astype(BF16)
    target = lax.broadcasted_iota(jnp.int32, (count, count), 0)
    origin = lax.broadcasted_iota(jnp.int32, (count, count), 1)
    order = (target ^ (where[0] * own_rows)) == origin
    x = dot_nn(jnp.where(order, 1.0, 0.0).astype(BF16), stacked).astype(BF16)
    for k, out in ((1, far), (0, near)):
        start = pl.multiple_of((where[1] ^ k) * half, half)
        value = dot_nn(x, w_ref[:, pl.ds(start, half)])
        out[...] = value.astype(BF16)
        if k == 0:
            kept[...] = value


def project(inputs, out_weight):
    sources = len(inputs)
    shape = (sources * inputs[0].shape[0], out_weight.shape[1] // 2)
    return call(
        functools.partial(project_kernel, sources=sources),
        "project",
        [*inputs, out_weight],
        [VMEM] * (sources + 1),
        [jax.ShapeDtypeStruct(shape, kind) for kind in (F32, BF16, BF16)],
    )[0]


def add_kernel(kept, facts, *refs):
    half = kept.shape[1]
    total = kept[...]
    for ref in refs[:-1]:
        total = total + ref[...].astype(F32)
    refs[-1][:, :half] = total.astype(BF16)
    refs[-1][:, half:] = facts[...]


def add(kept, facts, others):
    outs = [jax.ShapeDtypeStruct((kept.shape[0], kept.shape[1] + facts.shape[1]), BF16)]
    return call(add_kernel, "add", [kept, facts, *others], [VMEM] * (2 + len(others)), outs)[0][0]


def gate_up_kernel(*refs, sources, first, index):
    where = position()
    inputs, refs = refs[:sources], refs[sources:]
    pick_ref, g_ref, u_ref, out_ref = refs[:4]
    if first:
        columns_ref, mine_ref, theirs_ref, x, both = refs[4:]
        count = inputs[0].shape[0]
        own_rows = mine_ref.shape[0]
        row = lax.broadcasted_iota(jnp.int32, (own_rows, count), 0)
        place = lax.broadcasted_iota(jnp.int32, (own_rows, count), 1)
        for out, shard in ((mine_ref, where[0]), (theirs_ref, where[0] ^ where[4])):
            chosen = jnp.where(place == row + shard * own_rows, 1.0, 0.0).astype(BF16)
            out[...] = dot_nn(chosen, inputs[0][:, : x.shape[1]]).astype(BF16)
        for k in range(sources):
            start = pl.multiple_of((where[3] ^ k) * count, count) if sources > 1 else 0
            x[pl.ds(start, count), :] = inputs[k][:, : x.shape[1]].astype(F32)
        columns_ref[...] = x[...].T.astype(BF16)
    else:
        (columns_ref,), (both,) = inputs, refs[4:]
    experts, _, depth = g_ref.shape
    rows = columns_ref.shape[1]
    for base, w_ref in ((0, g_ref), (CHUNK, u_ref)):
        units = slice(index * CHUNK, (index + 1) * CHUNK) if w_ref.shape[1] > CHUNK else slice(None)
        value = dot_nn(w_ref[:, units, :].reshape(experts * CHUNK, depth), columns_ref[...]).astype(BF16)
        for e in range(experts):
            both[base : base + CHUNK, e * rows : (e + 1) * rows] = value[
                e * CHUNK : (e + 1) * CHUNK
            ]
    out_ref[...] = dot_nt(pick_ref[...], both[...]).astype(BF16)


def gate_up(xs, pick, w_gate, w_up, index, own_rows, loads, roomy, anchors=()):
    first = index == 0
    experts, _, depth = w_gate.shape
    rows = pick.shape[1] // experts
    outs = [jax.ShapeDtypeStruct((pick.shape[0], 2 * CHUNK), BF16)]
    scratch = [pltpu.VMEM((2 * CHUNK, experts * rows), BF16)]
    if first:
        outs.append(jax.ShapeDtypeStruct((depth, rows), BF16))
        outs += [jax.ShapeDtypeStruct((own_rows, depth), BF16)] * 2
        scratch.insert(0, pltpu.VMEM((rows, depth), F32))
    results, held = call(
        functools.partial(gate_up_kernel, sources=len(xs), first=first, index=index),
        f"gate_up_{index}",
        [*xs, pick, w_gate, w_up],
        [VMEM] * (len(xs) + 3),
        outs,
        scratch=scratch,
        loads=loads,
        anchors=anchors,
        us=4,
        roomy=roomy,
    )
    return results[0], results[1:2] if first else xs, results[2:], held


def down_kernel(own_ref, other_ref, weight_ref, spread_ref, d_ref, *refs, carried, index):
    before, outs = refs[:carried], refs[carried:]
    experts, _, depth = d_ref.shape
    rows = spread_ref.shape[0] // experts
    both = own_ref[...].astype(F32) + other_ref[...].astype(F32)
    gate, up = both[:, :CHUNK], both[:, CHUNK:]
    hidden = (gate / (1.0 + jnp.exp(-gate)) * up * weight_ref[...]).astype(BF16)
    spread = dot_nn(spread_ref[...], hidden).astype(BF16)
    left = jnp.concatenate([spread[e * rows : (e + 1) * rows] for e in range(experts)], axis=1)
    units = slice(index * CHUNK, (index + 1) * CHUNK)
    total = dot_nn(left, d_ref[:, units, :].reshape(experts * CHUNK, depth))
    if carried:
        total = total + before[0][...]
    if len(outs) == 1:
        outs[0][...] = total
    else:
        half = depth // 2
        low, high = total[:, :half], total[:, half:]
        mine = lax.axis_index("sub") == 0
        outs[0][...] = jnp.where(mine, low, high)
        outs[1][...] = jnp.where(mine, high, low)


def down(own, other, slot_weight, spread, w_down, before, index, halved, roomy):
    experts, _, depth = w_down.shape
    rows = spread.shape[0] // experts
    carried = [] if before is None else [before]
    parts = 2 if halved else 1
    return call(
        functools.partial(down_kernel, carried=len(carried), index=index),
        f"down_{index}",
        [own, other, slot_weight, spread, w_down, *carried],
        [VMEM] * (5 + len(carried)),
        [jax.ShapeDtypeStruct((rows, depth // parts), F32)] * parts,
        us=3,
        roomy=roomy,
    )[0]


def load(loads, anchors, name, roomy=False):
    return call(
        lambda: None, name, [], [], [], loads=loads, anchors=anchors, us=2 * len(loads), roomy=roomy
    )[1]


def arrange_kernel(*refs):
    inputs, out_ref = refs[:-1], refs[-1]
    count = inputs[0].shape[0]
    for k, ref in enumerate(inputs):
        start = pl.multiple_of((lax.axis_index("pool") ^ k) * count, count)
        out_ref[pl.ds(start, count), :] = ref[:, : out_ref.shape[1]]


def arrange(blocks, width):
    shape = (len(blocks) * blocks[0].shape[0], width)
    outs = [jax.ShapeDtypeStruct(shape, BF16)]
    return call(arrange_kernel, "arrange", blocks, [VMEM] * len(blocks), outs, roomy=True)[0][0]


def halves_kernel(value_ref, own_ref, other_ref):
    half = own_ref.shape[1]
    low, high = value_ref[:, :half], value_ref[:, half:]
    mine = lax.axis_index("sub") == 0
    own_ref[...] = jnp.where(mine, low, high)
    other_ref[...] = jnp.where(mine, high, low)


def halves(value):
    outs = [jax.ShapeDtypeStruct((value.shape[0], value.shape[1] // 2), F32)] * 2
    return call(halves_kernel, "halves", [value], [VMEM], outs, roomy=True)[0]


def join_kernel(mine_ref, theirs_ref, out_hbm, out_ref, sem):
    half = mine_ref.shape[1]
    low = lax.axis_index("tp") == 0
    mine, theirs = mine_ref[...].astype(F32), theirs_ref[...].astype(F32)
    out_ref[:, :half] = jnp.where(low, mine, theirs).astype(BF16)
    out_ref[:, half:] = jnp.where(low, theirs, mine).astype(BF16)
    copy = pltpu.make_async_copy(out_ref, out_hbm, sem)
    copy.start()
    copy.wait()


def join(mine, theirs):
    shape = (mine.shape[0], 2 * mine.shape[1])
    return call(
        join_kernel,
        "join",
        [mine, theirs],
        [VMEM, VMEM],
        [jax.ShapeDtypeStruct(shape, BF16)],
        out_specs=[HBM],
        scratch=[pltpu.VMEM(shape, BF16), pltpu.SemaphoreType.DMA],
    )[0][0]


def split_kernel(own_ref, other_ref, *outs):
    count = outs[0].shape[0]
    pool = lax.axis_index("pool")
    for k in range(len(outs)):
        row = pl.ds(pl.multiple_of((pool ^ k) * count, count), count)
        outs[k][...] = (own_ref[row, :] + other_ref[row, :]).astype(outs[k].dtype)


def split(own, other, pieces):
    shape = (own.shape[0] // pieces, own.shape[1])
    return call(
        split_kernel,
        "split",
        [own, other],
        [VMEM, VMEM],
        [jax.ShapeDtypeStruct(shape, F32 if k == 0 else BF16) for k in range(pieces)],
    )[0]


def xor_permute(value, axes, count, k):
    return lax.ppermute(value, axes, [(i, i ^ k) for i in range(count)])


def body(
    queries,
    keys_cache,
    values_cache,
    lengths,
    out_weight,
    routes,
    route_weight,
    expert_table,
    w_gate,
    w_up,
    w_down,
):
    pools, tps, subs = lax.axis_size("pool"), lax.axis_size("tp"), lax.axis_size("sub")
    pool, tp, sub = lax.axis_index("pool"), lax.axis_index("tp"), lax.axis_index("sub")
    shards = tps * subs
    shard = tp * subs + sub
    direct = tps == 2 and subs == 2 and pools == 4
    own_rows = queries.shape[0]
    pool_rows = own_rows * shards
    rows = pool_rows * pools
    experts, hidden_units, half_width = w_gate.shape
    top = routes.shape[1]

    capacity = -(-rows * top * 13 // (8 * pools * 16)) * 16
    gates, ups, downs = [
        [(w, c) for c in range(0, hidden_units, CHUNK)] for w in (w_gate, w_up, w_down)
    ]
    chunks = len(gates)

    if direct:
        axes = ("tp", "sub")
        (*pieces, facts), _ = attend(
            queries,
            keys_cache,
            values_cache,
            lengths,
            (routes.T, route_weight.T),
            shards,
            [],
            False,
        )
        inputs = [pieces[0]] + [xor_permute(pieces[k], axes, shards, k) for k in range(1, shards)]
        (out_held,) = load([(out_weight, None)], [pieces[0]], "load_a")
        kept, near, far = project(inputs, out_held)
        gate_1, up_1 = gate_2, up_2 = in_vmem(w_gate), in_vmem(w_up)
        gate_0, up_0 = load([gates[0], ups[0]], [near], "load_b")
        others = [
            xor_permute(near if k < subs else far, axes, shards, k) for k in range(1, shards)
        ]
        x_half, gate_0 = lax.optimization_barrier((add(kept, facts, others), gate_0))
        xs = [x_half] + [xor_permute(x_half, "pool", pools, k) for k in range(1, pools)]
        (slots, weights, largest), (pick, spread, slot_weight), _ = route(
            xs,
            expert_table,
            experts,
            rows,
            top,
            capacity,
            pools,
            [],
            False,
        )
        held = [(gate_0, up_0), (gate_1, up_1), (gate_2, up_2)]
        sent, given = [], xs
        for c in range(chunks):
            value, given, rest, _ = gate_up(
                given, pick, *held[c], c, own_rows, [], False, sent[-1:]
            )
            if c == 0:
                mine, theirs = rest
            sent.append(value)
        theirs, _ = lax.optimization_barrier((theirs, sent[-1]))
        theirs = lax.ppermute(theirs, "tp", [(0, 1), (1, 0)])
    else:
        (attention, facts), _ = attend(
            queries,
            keys_cache,
            values_cache,
            lengths,
            (routes.T, route_weight.T),
            1,
            [],
            True,
        )
        blocks = lax.all_gather(facts, "pool", axis=0)
        (slots, weights, largest), (pick, spread, slot_weight), _ = route(
            [blocks], expert_table, experts, rows, top, capacity, pools, [], True
        )
        head_rows = lax.all_to_all(
            attention, ("tp", "sub"), split_axis=1, concat_axis=0, tiled=True
        )
        partial = jnp.dot(head_rows, out_weight, preferred_element_type=F32)
        x_sum = lax.psum_scatter(partial, ("tp", "sub"), scatter_dimension=1, tiled=True)
        x_pool = x_sum.astype(BF16)
        attended = lax.all_to_all(x_pool, ("tp", "sub"), split_axis=0, concat_axis=1, tiled=True)
        x_part = lax.all_gather(x_pool, "pool", axis=0, tiled=True)
        xs = [lax.all_gather(x_part, "sub", axis=1, tiled=True)]
        held = load(gates + ups, [], "load")
        sent, given = [], xs
        for c in range(chunks):
            value, given, *_ = gate_up(
                given, pick, held[c], held[chunks + c], c, own_rows, [], True
            )
            sent.append(value)

    def exchange(value):
        if tps == 2:
            return value, lax.ppermute(value, "tp", [(0, 1), (1, 0)])
        return lax.psum(value.astype(F32), "tp").astype(BF16), jnp.zeros_like(value)

    def combine(halved, extra=None):
        if not direct:
            value = lax.psum_scatter(halved[0], "pool", scatter_dimension=0, tiled=True)
            return lax.psum_scatter(value, "sub", scatter_dimension=1, tiled=True)
        own, other = halved
        received = xor_permute(other, "sub", subs, 1)
        if extra is not None:
            received, extra = lax.optimization_barrier((received, extra))
        pieces = split(own, received, pools)
        total = pieces[0]
        for k in range(1, pools):
            total = total + xor_permute(pieces[k], "pool", pools, k).astype(F32)
        return total if extra is None else total + extra

    def more(state):
        k, total = state
        k, *held_x = lax.optimization_barrier((k, *xs))
        x = arrange(held_x, half_width) if direct else held_x[0]
        pick, spread, slot_weight = pick_slots(k * capacity, slots, weights, capacity)
        gate = jnp.einsum("rd,efd->erf", x, w_gate, preferred_element_type=F32)
        up = jnp.einsum("rd,efd->erf", x, w_up, preferred_element_type=F32)
        both = jnp.concatenate([gate, up], axis=2).astype(BF16)
        both = both.reshape(experts * rows, 2 * hidden_units)
        sent = jnp.dot(pick, both, preferred_element_type=F32).astype(BF16)
        if tps == 2:
            both = sent.astype(F32) + lax.ppermute(sent, "tp", [(0, 1), (1, 0)]).astype(F32)
        else:
            both = lax.psum(sent.astype(F32), "tp")
        hidden = jax.nn.silu(both[:, :hidden_units]) * both[:, hidden_units:] * slot_weight
        spread = jnp.dot(spread, hidden.astype(BF16), preferred_element_type=F32).astype(BF16)
        spread = spread.reshape(experts, rows, hidden_units)
        value = jnp.einsum("erf,efd->rd", spread, w_down, preferred_element_type=F32)
        value = halves(value) if direct else [value]
        return k + 1, total + combine(value)

    both = [exchange(value) for value in sent]
    result = [None]
    for c in range(chunks):
        last = direct and c == chunks - 1
        result = down(
            *both[c], slot_weight, spread, in_vmem(w_down), result[0], c, last, not direct
        )
    if direct:
        theirs, largest, *result = lax.optimization_barrier((theirs, largest, *result))
        attended = join(mine, theirs)
    _, extra = lax.while_loop(
        lambda state: state[0] * capacity < largest[0, 0],
        more,
        (jnp.minimum(largest[0, 0], 1), jnp.zeros((pool_rows, half_width // subs), F32)),
    )
    if direct:
        return attended, combine(result, extra).astype(BF16)
    return attended, (combine(result) + extra).astype(BF16)


def solution(mesh):
    in_specs = (
        P(("grp", "pool", "tp", "sub"), None),
        P(("grp", "pool", "tp", "sub"), None, None),
        P(("grp", "pool", "tp", "sub"), None, None),
        P(("grp", "pool", "tp", "sub")),
        P(("tp", "sub"), None),
        P(("grp", "pool"), None),
        P(("grp", "pool"), None),
        P(),
        P("pool", "sub", "tp"),
        P("pool", "sub", "tp"),
        P("pool", "sub", "tp"),
    )
    out_specs = (P(("grp", "pool", "tp", "sub"), None), P(("grp", "pool"), ("tp", "sub")))
    return jax.shard_map(body, mesh=mesh, in_specs=in_specs, out_specs=out_specs, check_vma=False)
```

```python
import functools
import math

import jax
import jax.numpy as jnp
from jax import lax
from jax.experimental import pallas as pl
from jax.experimental.pallas import tpu as pltpu
from jax.sharding import PartitionSpec as P

HEAD_DIM = 128
KV_HEADS = 2
CHUNK = 128
FACT_LANES = 128

F32 = jnp.float32
BF16 = jnp.bfloat16


def dot_nt(a, b):
    return lax.dot_general(a, b, (((1,), (1,)), ((), ())), preferred_element_type=F32)


def dot_tn(a, b):
    return lax.dot_general(a, b, (((0,), (0,)), ((), ())), preferred_element_type=F32)


def dot_nn(a, b):
    return jnp.dot(a, b, preferred_element_type=F32)


def cost(microseconds):
    return pl.CostEstimate(
        flops=0, transcendentals=0, bytes_accessed=int(microseconds * 3_000_000)
    )


VMEM = pl.BlockSpec(memory_space=pltpu.VMEM)
SMEM = pl.BlockSpec(memory_space=pltpu.SMEM)
HBM = pl.BlockSpec(memory_space=pltpu.HBM)
ANY = pl.BlockSpec(memory_space=pl.ANY)


def in_vmem(value):
    return pltpu.with_memory_space_constraint(value, pltpu.VMEM)


def in_hbm(value):
    return pltpu.with_memory_space_constraint(value, pltpu.HBM)


def position():
    tp, sub = lax.axis_index("tp"), lax.axis_index("sub")
    subs = lax.axis_size("sub")
    return tp * subs + sub, tp, sub, lax.axis_index("pool"), subs


def far_first(k, count):
    return (count - k) % count


def call(kernel, name, inputs, specs, outs, out_specs=None, scratch=(), loads=(), anchors=(), us=2, roomy=False, begins=False):
    count_in, count_out, count_load = len(inputs), len(outs), len(loads)

    def source(ref, first):
        return ref if first is None else ref.at[:, first : first + CHUNK, :]

    def run(*refs):
        refs = list(refs)
        given = [refs.pop(0) for _ in range(count_in)]
        sources = [refs.pop(0) for _ in range(count_load)]
        del refs[: len(anchors)]
        results = [refs.pop(0) for _ in range(count_out)]
        targets = [refs.pop(0) for _ in range(count_load)]
        copies = []
        if loads:
            sems = refs.pop()
            for i, (_, first) in enumerate(loads):
                copies.append(
                    pltpu.make_async_copy(source(sources[i], first), targets[i], sems.at[i])
                )

        def begin():
            if copies:

                @pl.when(lax.axis_index("tp") >= 0)
                def _():
                    for copy in copies:
                        copy.start()

        if begins:
            kernel(begin, *given, *results, *refs)
        else:
            begin()
            kernel(*given, *results, *refs)
        for copy in copies:
            copy.wait()

    def loaded(array, first):
        shape = array.shape if first is None else (array.shape[0], CHUNK, array.shape[2])
        return pltpu.VMEM(shape, array.dtype)

    if not roomy:
        outs = [
            leaf if spec is HBM else pltpu.VMEM(leaf.shape, leaf.dtype)
            for leaf, spec in zip(outs, out_specs or [VMEM] * count_out)
        ]
    scratch = list(scratch) + ([pltpu.SemaphoreType.DMA((count_load,))] if loads else [])
    results = pl.pallas_call(
        run,
        in_specs=list(specs) + [HBM] * count_load + [ANY] * len(anchors),
        out_specs=list(out_specs or [VMEM] * count_out) + [VMEM] * count_load,
        out_shape=list(outs) + [loaded(*leaf) for leaf in loads],
        scratch_shapes=scratch,
        compiler_params=pltpu.CompilerParams(vmem_limit_bytes=(48 if roomy else 12) << 20),
        cost_estimate=cost(us),
        name=name,
    )(*inputs, *[in_hbm(leaf[0]) for leaf in loads], *anchors)
    return list(results[:count_out]), list(results[count_out:])


def attention_kernel(
    begin, q_hbm, lengths_hbm, route_hbm, share_hbm, k_hbm, v_hbm, *refs, pieces
):
    where = position()
    outs, facts_ref = refs[:pieces], refs[pieces]
    lengths, q_ref, route_ref, share_ref, k_ref, v_ref, sems, spread, gathered, flat = refs[
        pieces + 1 :
    ]
    rows, heads, _ = gathered.shape
    positions = k_ref.shape[1]
    group = heads // KV_HEADS
    small = [
        pltpu.make_async_copy(q_hbm, q_ref, sems.at[rows, 0]),
        pltpu.make_async_copy(lengths_hbm, lengths, sems.at[rows, 1]),
        pltpu.make_async_copy(route_hbm, route_ref, sems.at[rows + 1, 0]),
        pltpu.make_async_copy(share_hbm, share_ref, sems.at[rows + 1, 1]),
    ]
    for copy in small:
        copy.start()
    copies = []
    for row in range(rows):
        pair = [
            pltpu.make_async_copy(k_hbm.at[row], k_ref.at[row], sems.at[row, 0]),
            pltpu.make_async_copy(v_hbm.at[row], v_ref.at[row], sems.at[row, 1]),
        ]
        pair[0].start()
        pair[1].start()
        copies.append(pair)
    begin()
    for copy in small:
        copy.wait()
    share = share_ref[...]
    high = share.astype(BF16).astype(F32)
    middle = (share - high).astype(BF16).astype(F32)
    block = jnp.concatenate([route_ref[...].astype(F32), high, middle, share - high - middle], axis=0)
    count, lanes = block.shape[1], facts_ref.shape[1]
    block = jnp.concatenate([block, jnp.zeros((block.shape[0], -count % 128), F32)], axis=1).T
    blank = jnp.zeros((count, lanes - block.shape[1]), F32)
    facts_ref[...] = jnp.concatenate([block[:count], blank], axis=1).astype(BF16)
    queries = q_ref[...].astype(F32)
    for h in range(heads):
        spread[:, h, :] = queries[:, h * HEAD_DIM : (h + 1) * HEAD_DIM]
    column = lax.broadcasted_iota(jnp.int32, (group, positions), 1)
    for pair in copies:
        pair[0].wait()
        pair[1].wait()
    cases = [(row, j) for row in range(rows) for j in range(KV_HEADS)]
    lanes = [slice(j * HEAD_DIM, (j + 1) * HEAD_DIM) for j in range(KV_HEADS)]
    scores, terms, totals = [], [], []
    for row, j in cases:
        own = spread[row, j * group : (j + 1) * group, :].astype(BF16)
        scores.append(dot_nt(own, k_ref[row, :, lanes[j]]))
    for (row, j), score in zip(cases, scores):
        valid = column < lengths[row]
        score = jnp.where(valid, score * (1.0 / math.sqrt(HEAD_DIM)), -1e30)
        top = jnp.max(score, axis=1, keepdims=True)
        terms.append(jnp.where(valid, jnp.exp(score - top), 0.0))
        totals.append(jnp.sum(terms[-1], axis=1, keepdims=True))
    for (row, j), term, total in zip(cases, terms, totals):
        value = dot_nn(term.astype(BF16), v_ref[row, :, lanes[j]]) / total
        gathered[row, j * group : (j + 1) * group, :] = value
    for h in range(heads):
        flat[:, h * HEAD_DIM : (h + 1) * HEAD_DIM] = gathered[:, h, :]
    width = heads * HEAD_DIM // pieces
    for k in range(pieces):
        start = pl.multiple_of(((where[0] ^ k) if pieces > 1 else 0) * width, width)
        outs[k][...] = flat[:, pl.ds(start, width)].astype(BF16)


def attend(queries, keys_cache, values_cache, lengths, facts, pieces, loads, roomy):
    rows, columns = queries.shape
    heads = columns // HEAD_DIM
    return call(
        functools.partial(attention_kernel, pieces=pieces),
        "attention",
        [in_hbm(a) for a in (queries, lengths, *facts, keys_cache, values_cache)],
        [HBM] * 6,
        [jax.ShapeDtypeStruct((rows, columns // pieces), BF16)] * pieces
        + [jax.ShapeDtypeStruct((facts[0].shape[1], FACT_LANES), BF16)],
        scratch=[
            pltpu.SMEM((rows,), jnp.int32),
            pltpu.VMEM(queries.shape, BF16),
            pltpu.VMEM(facts[0].shape, jnp.int32),
            pltpu.VMEM(facts[1].shape, F32),
            pltpu.VMEM(keys_cache.shape, BF16),
            pltpu.VMEM(values_cache.shape, BF16),
            pltpu.SemaphoreType.DMA((rows + 2, 2)),
            pltpu.VMEM((rows, heads, HEAD_DIM), F32),
            pltpu.VMEM((rows, heads, HEAD_DIM), F32),
            pltpu.VMEM((rows, columns), F32),
        ],
        loads=loads,
        us=4,
        roomy=roomy,
        begins=True,
    )


def route_kernel(table_ref, *refs, sources, experts, top):
    where = position()
    given, (slot_ref, weight_ref, largest_ref, extra_ref, *picks, held) = refs[:sources], refs[sources:]
    pools, pool_rows, lanes = held.shape
    if sources == 1:
        held[...] = given[0][...].astype(F32)
    else:
        for k in range(sources):
            width = given[k].shape[1]
            held[where[3] ^ far_first(k, sources)] = given[k][:, width - lanes :].astype(F32)
    rows = pools * pool_rows
    total = table_ref.shape[1]
    groups, _, lanes = slot_ref.shape
    group = lanes // rows
    facts = held[...].reshape(rows, held.shape[2]).T
    shares = facts[top : 2 * top] + facts[2 * top : 3 * top] + facts[3 * top : 4 * top]
    routes = jnp.concatenate([facts[i : i + 1] for i in range(top)], axis=1).astype(jnp.int32)
    ids = lax.broadcasted_iota(jnp.int32, (total, top * rows), 0)
    hot = jnp.where(ids == routes, 1.0, 0.0).astype(BF16)
    table = jnp.broadcast_to(table_ref[...].astype(F32), (8, total)).astype(BF16)
    entry = dot_nn(table, hot)[0:1].astype(jnp.int32)

    first = lax.broadcasted_iota(jnp.int32, (pools, top * rows), 0) * experts
    inside = jnp.where((entry >= first) & (entry < first + experts), 1.0, 0.0)
    loads = jnp.sum(inside, axis=1, keepdims=True)
    largest_ref[...] = jnp.max(loads, axis=0, keepdims=True).astype(jnp.int32)
    extra_ref[...] = largest_ref[...] - picks[0].shape[0]

    lane = lax.broadcasted_iota(jnp.int32, (groups, lanes), 1)
    block = lax.broadcasted_iota(jnp.int32, (groups, lanes), 0)
    wanted = where[3] * experts + block * group + lane // rows
    weight = jnp.zeros((groups, lanes), F32)
    mask = jnp.zeros((groups, lanes), F32)
    for i in range(top):
        named = jnp.concatenate([entry[:, i * rows : (i + 1) * rows]] * group, axis=1)
        value = jnp.concatenate([shares[i : i + 1]] * group, axis=1)
        match = wanted == named
        mask = mask + jnp.where(match, 1.0, 0.0)
        weight = weight + jnp.where(match, value, 0.0)
    earlier = lax.broadcasted_iota(jnp.int32, (lanes, lanes), 0)
    later = lax.broadcasted_iota(jnp.int32, (lanes, lanes), 1)
    before = jnp.where(earlier < later, 1.0, 0.0).astype(BF16)
    rank = dot_nn(mask.astype(BF16), before)
    base = jnp.zeros((1, 1), F32)
    counts = jnp.sum(mask, axis=1, keepdims=True)
    slots = []
    for g in range(groups):
        slots.append(jnp.where(mask[g : g + 1] > 0.0, rank[g : g + 1] + base, -1.0))
        slot_ref[g] = slots[g].astype(jnp.int32)
        weight_ref[g] = weight[g : g + 1]
        base = base + counts[g : g + 1]
    fill_picks(slots, [weight[g : g + 1] for g in range(groups)], *picks)


def fill_picks(slots, weights, pick_ref, spread_ref, slot_weight_ref):
    groups, lanes = len(slots), slots[0].shape[1]
    capacity = pick_ref.shape[0]
    rows = jnp.concatenate(slots + [slots[0]] * (-groups % 8), axis=0).T
    place = lax.broadcasted_iota(jnp.int32, (capacity, lanes), 0).astype(F32)
    along = lax.broadcasted_iota(jnp.int32, (lanes, capacity), 1).astype(F32)
    total = jnp.zeros((capacity, lanes), F32)
    for g in range(groups):
        hit = place == slots[g]
        part = slice(g * lanes, (g + 1) * lanes)
        pick_ref[:, part] = jnp.where(hit, 1.0, 0.0).astype(BF16)
        spread_ref[part, :] = jnp.where(along == rows[:, g : g + 1], 1.0, 0.0).astype(BF16)
        total = total + jnp.where(hit, weights[g], 0.0)
    slot_weight_ref[...] = jnp.sum(total, axis=1, keepdims=True)


def pick_shapes(capacity, pairs):
    return [
        jax.ShapeDtypeStruct((capacity, pairs), BF16),
        jax.ShapeDtypeStruct((pairs, capacity), BF16),
        jax.ShapeDtypeStruct((capacity, 1), F32),
    ]


def route(blocks, expert_table, experts, rows, top, capacity, pools, loads, roomy):
    group = max(1, min(experts, 256 // rows))
    shape = (experts // group, 1, group * rows)
    results, held = call(
        functools.partial(route_kernel, sources=len(blocks), experts=experts, top=top),
        "route",
        [expert_table.reshape(1, -1), *blocks],
        [VMEM] + [VMEM] * len(blocks),
        [
            jax.ShapeDtypeStruct(shape, jnp.int32),
            jax.ShapeDtypeStruct(shape, F32),
            jax.ShapeDtypeStruct((1, 1), jnp.int32),
            jax.ShapeDtypeStruct((1, 1), jnp.int32),
            *pick_shapes(capacity, experts * rows),
        ],
        scratch=[pltpu.VMEM((pools, rows // pools, FACT_LANES), F32)],
        loads=loads,
        us=6,
        roomy=roomy,
    )
    return results[:4], results[4:], held


def pick_slots(shift, slots, weights, capacity):
    def kernel(shift_ref, *refs):
        slot_ref, weight_ref, *picks = refs
        groups = range(slot_ref.shape[0])
        shifted = [(slot_ref[g] - shift_ref[0]).astype(F32) for g in groups]
        fill_picks(shifted, [weight_ref[g] for g in groups], *picks)

    return call(
        kernel,
        "pick",
        [shift.reshape(1), slots, weights],
        [SMEM, VMEM, VMEM],
        pick_shapes(capacity, slots.shape[0] * slots.shape[2]),
        roomy=True,
    )[0]


def project_kernel(*refs, sources):
    where = position()
    inputs, (w_ref, kept, near, far) = refs[:sources], refs[sources:]
    own_rows = inputs[0].shape[0]
    count = sources * own_rows
    half = kept.shape[1]
    stacked = jnp.concatenate([ref[...].astype(F32) for ref in inputs], axis=0).astype(BF16)
    target = lax.broadcasted_iota(jnp.int32, (count, count), 0)
    origin = lax.broadcasted_iota(jnp.int32, (count, count), 1)
    order = (target ^ (where[0] * own_rows)) == origin
    x = dot_nn(jnp.where(order, 1.0, 0.0).astype(BF16), stacked).astype(BF16)
    for k, out in ((1, far), (0, near)):
        start = pl.multiple_of((where[1] ^ k) * half, half)
        value = dot_nn(x, w_ref[:, pl.ds(start, half)])
        out[...] = value.astype(BF16)
        if k == 0:
            kept[...] = value


def project(inputs, out_weight):
    sources = len(inputs)
    shape = (sources * inputs[0].shape[0], out_weight.shape[1] // 2)
    return call(
        functools.partial(project_kernel, sources=sources),
        "project",
        [*inputs, out_weight],
        [VMEM] * (sources + 1),
        [jax.ShapeDtypeStruct(shape, kind) for kind in (F32, BF16, BF16)],
    )[0]


def add_kernel(kept, facts, *refs):
    half = kept.shape[1]
    total = kept[...]
    for ref in refs[:-1]:
        total = total + ref[...].astype(F32)
    refs[-1][:, :half] = total.astype(BF16)
    refs[-1][:, half:] = facts[...]


def add(kept, facts, others):
    outs = [jax.ShapeDtypeStruct((kept.shape[0], kept.shape[1] + facts.shape[1]), BF16)]
    return call(add_kernel, "add", [kept, facts, *others], [VMEM] * (2 + len(others)), outs)[0][0]


def gate_up_kernel(*refs, sources, first, index):
    where = position()
    inputs, refs = refs[:sources], refs[sources:]
    pick_ref, g_ref, u_ref, out_ref = refs[:4]
    if first:
        columns_ref, mine_ref, theirs_ref, x, both = refs[4:]
        count = inputs[0].shape[0]
        own_rows = mine_ref.shape[0]
        row = lax.broadcasted_iota(jnp.int32, (own_rows, count), 0)
        place = lax.broadcasted_iota(jnp.int32, (own_rows, count), 1)
        for out, shard in ((mine_ref, where[0]), (theirs_ref, where[0] ^ where[4])):
            chosen = jnp.where(place == row + shard * own_rows, 1.0, 0.0).astype(BF16)
            out[...] = dot_nn(chosen, inputs[0][:, : x.shape[1]]).astype(BF16)
        for k in range(sources):
            start = 0
            if sources > 1:
                start = pl.multiple_of((where[3] ^ far_first(k, sources)) * count, count)
            x[pl.ds(start, count), :] = inputs[k][:, : x.shape[1]].astype(F32)
        columns_ref[...] = x[...].T.astype(BF16)
    else:
        (columns_ref,), (both,) = inputs, refs[4:]
    experts, _, depth = g_ref.shape
    rows = columns_ref.shape[1]
    for base, w_ref in ((0, g_ref), (CHUNK, u_ref)):
        units = slice(index * CHUNK, (index + 1) * CHUNK) if w_ref.shape[1] > CHUNK else slice(None)
        value = dot_nn(w_ref[:, units, :].reshape(experts * CHUNK, depth), columns_ref[...]).astype(BF16)
        for e in range(experts):
            both[base : base + CHUNK, e * rows : (e + 1) * rows] = value[
                e * CHUNK : (e + 1) * CHUNK
            ]
    out_ref[...] = dot_nt(pick_ref[...], both[...]).astype(BF16)


def gate_up(xs, pick, w_gate, w_up, index, own_rows, loads, roomy, anchors=()):
    first = index == 0
    experts, _, depth = w_gate.shape
    rows = pick.shape[1] // experts
    outs = [jax.ShapeDtypeStruct((pick.shape[0], 2 * CHUNK), BF16)]
    scratch = [pltpu.VMEM((2 * CHUNK, experts * rows), BF16)]
    if first:
        outs.append(jax.ShapeDtypeStruct((depth, rows), BF16))
        outs += [jax.ShapeDtypeStruct((own_rows, depth), BF16)] * 2
        scratch.insert(0, pltpu.VMEM((rows, depth), F32))
    results, held = call(
        functools.partial(gate_up_kernel, sources=len(xs), first=first, index=index),
        f"gate_up_{index}",
        [*xs, pick, w_gate, w_up],
        [VMEM] * (len(xs) + 3),
        outs,
        scratch=scratch,
        loads=loads,
        anchors=anchors,
        us=4,
        roomy=roomy,
    )
    return results[0], results[1:2] if first else xs, results[2:], held


def down_kernel(own_ref, other_ref, weight_ref, spread_ref, d_ref, *refs, carried, index):
    before, outs = refs[:carried], refs[carried:]
    experts, _, depth = d_ref.shape
    rows = spread_ref.shape[0] // experts
    both = own_ref[...].astype(F32) + other_ref[...].astype(F32)
    gate, up = both[:, :CHUNK], both[:, CHUNK:]
    hidden = (gate / (1.0 + jnp.exp(-gate)) * up * weight_ref[...]).astype(BF16)
    spread = dot_nn(spread_ref[...], hidden).astype(BF16)
    left = jnp.concatenate([spread[e * rows : (e + 1) * rows] for e in range(experts)], axis=1)
    units = slice(index * CHUNK, (index + 1) * CHUNK)
    total = dot_nn(left, d_ref[:, units, :].reshape(experts * CHUNK, depth))
    if carried:
        total = total + before[0][...]
    if len(outs) == 1:
        outs[0][...] = total
    else:
        half = depth // 2
        low, high = total[:, :half], total[:, half:]
        mine = lax.axis_index("sub") == 0
        outs[0][...] = jnp.where(mine, low, high)
        outs[1][...] = jnp.where(mine, high, low)


def down(own, other, slot_weight, spread, w_down, before, index, halved, roomy):
    experts, _, depth = w_down.shape
    rows = spread.shape[0] // experts
    carried = [] if before is None else [before]
    parts = 2 if halved else 1
    return call(
        functools.partial(down_kernel, carried=len(carried), index=index),
        f"down_{index}",
        [own, other, slot_weight, spread, w_down, *carried],
        [VMEM] * (5 + len(carried)),
        [jax.ShapeDtypeStruct((rows, depth // parts), F32)] * parts,
        us=3,
        roomy=roomy,
    )[0]


def load(loads, anchors, name, roomy=False):
    return call(
        lambda: None, name, [], [], [], loads=loads, anchors=anchors, us=2 * len(loads), roomy=roomy
    )[1]


def arrange_kernel(*refs):
    inputs, out_ref = refs[:-1], refs[-1]
    count = inputs[0].shape[0]
    for k, ref in enumerate(inputs):
        start = pl.multiple_of((lax.axis_index("pool") ^ far_first(k, len(inputs))) * count, count)
        out_ref[pl.ds(start, count), :] = ref[:, : out_ref.shape[1]]


def arrange(blocks, width):
    shape = (len(blocks) * blocks[0].shape[0], width)
    outs = [jax.ShapeDtypeStruct(shape, BF16)]
    return call(arrange_kernel, "arrange", blocks, [VMEM] * len(blocks), outs, roomy=True)[0][0]


def halves_kernel(value_ref, own_ref, other_ref):
    half = own_ref.shape[1]
    low, high = value_ref[:, :half], value_ref[:, half:]
    mine = lax.axis_index("sub") == 0
    own_ref[...] = jnp.where(mine, low, high)
    other_ref[...] = jnp.where(mine, high, low)


def halves(value):
    outs = [jax.ShapeDtypeStruct((value.shape[0], value.shape[1] // 2), F32)] * 2
    return call(halves_kernel, "halves", [value], [VMEM], outs, roomy=True)[0]


def join_kernel(mine_ref, theirs_ref, out_hbm, out_ref, sem):
    half = mine_ref.shape[1]
    low = lax.axis_index("tp") == 0
    mine, theirs = mine_ref[...].astype(F32), theirs_ref[...].astype(F32)
    out_ref[:, :half] = jnp.where(low, mine, theirs).astype(BF16)
    out_ref[:, half:] = jnp.where(low, theirs, mine).astype(BF16)
    copy = pltpu.make_async_copy(out_ref, out_hbm, sem)
    copy.start()
    copy.wait()


def join(mine, theirs):
    shape = (mine.shape[0], 2 * mine.shape[1])
    return call(
        join_kernel,
        "join",
        [mine, theirs],
        [VMEM, VMEM],
        [jax.ShapeDtypeStruct(shape, BF16)],
        out_specs=[HBM],
        scratch=[pltpu.VMEM(shape, BF16), pltpu.SemaphoreType.DMA],
    )[0][0]


def split_kernel(own_ref, other_ref, *outs):
    count = outs[0].shape[0]
    pool = lax.axis_index("pool")
    for k in range(len(outs)):
        row = pl.ds(pl.multiple_of((pool ^ k) * count, count), count)
        outs[k][...] = (own_ref[row, :] + other_ref[row, :]).astype(outs[k].dtype)


def split(own, other, pieces):
    shape = (own.shape[0] // pieces, own.shape[1])
    return call(
        split_kernel,
        "split",
        [own, other],
        [VMEM, VMEM],
        [jax.ShapeDtypeStruct(shape, F32 if k == 0 else BF16) for k in range(pieces)],
    )[0]


def xor_permute(value, axes, count, k):
    return lax.ppermute(value, axes, [(i, i ^ k) for i in range(count)])


def body(
    queries,
    keys_cache,
    values_cache,
    lengths,
    out_weight,
    routes,
    route_weight,
    expert_table,
    w_gate,
    w_up,
    w_down,
):
    pools, tps, subs = lax.axis_size("pool"), lax.axis_size("tp"), lax.axis_size("sub")
    pool, tp, sub = lax.axis_index("pool"), lax.axis_index("tp"), lax.axis_index("sub")
    shards = tps * subs
    shard = tp * subs + sub
    direct = tps == 2 and subs == 2 and pools == 4
    own_rows = queries.shape[0]
    pool_rows = own_rows * shards
    rows = pool_rows * pools
    experts, hidden_units, half_width = w_gate.shape
    top = routes.shape[1]

    capacity = -(-rows * top * 13 // (8 * pools * 16)) * 16
    gates, ups, downs = [
        [(w, c) for c in range(0, hidden_units, CHUNK)] for w in (w_gate, w_up, w_down)
    ]
    chunks = len(gates)

    if direct:
        axes = ("tp", "sub")
        (*pieces, facts), _ = attend(
            queries,
            keys_cache,
            values_cache,
            lengths,
            (routes.T, route_weight.T),
            shards,
            [],
            False,
        )
        inputs = [pieces[0]] + [xor_permute(pieces[k], axes, shards, k) for k in range(1, shards)]
        (out_held,) = load([(out_weight, None)], [pieces[0]], "load_a")
        kept, near, far = project(inputs, out_held)
        gate_1, up_1 = gate_2, up_2 = in_vmem(w_gate), in_vmem(w_up)
        gate_0, up_0 = load([gates[0], ups[0]], [near], "load_b")
        others = [
            xor_permute(near if k < subs else far, axes, shards, k) for k in range(1, shards)
        ]
        x_half, gate_0 = lax.optimization_barrier((add(kept, facts, others), gate_0))
        xs = [x_half]
        for k in range(1, pools):
            xs.append(xor_permute(x_half, "pool", pools, far_first(k, pools)))
        (slots, weights, largest, extra_pairs), (pick, spread, slot_weight), _ = route(
            xs,
            expert_table,
            experts,
            rows,
            top,
            capacity,
            pools,
            [],
            False,
        )
        held = [(gate_0, up_0), (gate_1, up_1), (gate_2, up_2)]
        sent, given = [], xs
        for c in range(chunks):
            value, given, rest, _ = gate_up(
                given, pick, *held[c], c, own_rows, [], False, sent[-1:]
            )
            if c == 0:
                mine, theirs = rest
            sent.append(value)
        theirs, _ = lax.optimization_barrier((theirs, sent[-1]))
        theirs = lax.ppermute(theirs, "tp", [(0, 1), (1, 0)])
    else:
        (attention, facts), _ = attend(
            queries,
            keys_cache,
            values_cache,
            lengths,
            (routes.T, route_weight.T),
            1,
            [],
            True,
        )
        blocks = lax.all_gather(facts, "pool", axis=0)
        (slots, weights, largest, extra_pairs), (pick, spread, slot_weight), _ = route(
            [blocks], expert_table, experts, rows, top, capacity, pools, [], True
        )
        head_rows = lax.all_to_all(
            attention, ("tp", "sub"), split_axis=1, concat_axis=0, tiled=True
        )
        partial = jnp.dot(head_rows, out_weight, preferred_element_type=F32)
        x_sum = lax.psum_scatter(partial, ("tp", "sub"), scatter_dimension=1, tiled=True)
        x_pool = x_sum.astype(BF16)
        attended = lax.all_to_all(x_pool, ("tp", "sub"), split_axis=0, concat_axis=1, tiled=True)
        x_part = lax.all_gather(x_pool, "pool", axis=0, tiled=True)
        xs = [lax.all_gather(x_part, "sub", axis=1, tiled=True)]
        held = load(gates + ups, [], "load")
        sent, given = [], xs
        for c in range(chunks):
            value, given, *_ = gate_up(
                given, pick, held[c], held[chunks + c], c, own_rows, [], True
            )
            sent.append(value)

    def exchange(value):
        if tps == 2:
            return value, lax.ppermute(value, "tp", [(0, 1), (1, 0)])
        return lax.psum(value.astype(F32), "tp").astype(BF16), jnp.zeros_like(value)

    def combine(halved, extra=None):
        if not direct:
            value = lax.psum_scatter(halved[0], "pool", scatter_dimension=0, tiled=True)
            return lax.psum_scatter(value, "sub", scatter_dimension=1, tiled=True)
        own, other = halved
        received = xor_permute(other, "sub", subs, 1)
        if extra is not None:
            received, extra = lax.optimization_barrier((received, extra))
        pieces = split(own, received, pools)
        total = pieces[0]
        for k in range(1, pools):
            far = far_first(k, pools)
            total = total + xor_permute(pieces[far], "pool", pools, far).astype(F32)
        return total if extra is None else total + extra

    def more(state):
        left, total = state
        left, *held_x = lax.optimization_barrier((left, *xs))
        x = arrange(held_x, half_width) if direct else held_x[0]
        pick, spread, slot_weight = pick_slots(largest[0, 0] - left, slots, weights, capacity)
        gate = jnp.einsum("rd,efd->erf", x, w_gate, preferred_element_type=F32)
        up = jnp.einsum("rd,efd->erf", x, w_up, preferred_element_type=F32)
        both = jnp.concatenate([gate, up], axis=2).astype(BF16)
        both = both.reshape(experts * rows, 2 * hidden_units)
        sent = jnp.dot(pick, both, preferred_element_type=F32).astype(BF16)
        if tps == 2:
            both = sent.astype(F32) + lax.ppermute(sent, "tp", [(0, 1), (1, 0)]).astype(F32)
        else:
            both = lax.psum(sent.astype(F32), "tp")
        hidden = jax.nn.silu(both[:, :hidden_units]) * both[:, hidden_units:] * slot_weight
        spread = jnp.dot(spread, hidden.astype(BF16), preferred_element_type=F32).astype(BF16)
        spread = spread.reshape(experts, rows, hidden_units)
        value = jnp.einsum("erf,efd->rd", spread, w_down, preferred_element_type=F32)
        value = halves(value) if direct else [value]
        return left - capacity, total + combine(value)

    both = [exchange(value) for value in sent]
    result = [None]
    for c in range(chunks):
        last = direct and c == chunks - 1
        result = down(
            *both[c], slot_weight, spread, in_vmem(w_down), result[0], c, last, not direct
        )
    if direct:
        theirs, extra_pairs, *result = lax.optimization_barrier(
            (theirs, extra_pairs, *result)
        )
        attended = join(mine, theirs)
    _, extra = lax.while_loop(
        lambda state: state[0] > 0,
        more,
        (extra_pairs[0, 0], jnp.zeros((pool_rows, half_width // subs), F32)),
    )
    if direct:
        return attended, combine(result, extra).astype(BF16)
    return attended, (combine(result) + extra).astype(BF16)


def solution(mesh):
    in_specs = (
        P(("grp", "pool", "tp", "sub"), None),
        P(("grp", "pool", "tp", "sub"), None, None),
        P(("grp", "pool", "tp", "sub"), None, None),
        P(("grp", "pool", "tp", "sub")),
        P(("tp", "sub"), None),
        P(("grp", "pool"), None),
        P(("grp", "pool"), None),
        P(),
        P("pool", "sub", "tp"),
        P("pool", "sub", "tp"),
        P("pool", "sub", "tp"),
    )
    out_specs = (P(("grp", "pool", "tp", "sub"), None), P(("grp", "pool"), ("tp", "sub")))
    return jax.shard_map(body, mesh=mesh, in_specs=in_specs, out_specs=out_specs, check_vma=False)
```

```python
import functools
import math

import jax
import jax.numpy as jnp
from jax import lax
from jax.experimental import pallas as pl
from jax.experimental.pallas import tpu as pltpu
from jax.sharding import PartitionSpec as P

HEAD_DIM = 128
KV_HEADS = 2
CHUNK = 128
FACT_LANES = 128

F32 = jnp.float32
BF16 = jnp.bfloat16


def dot_nt(a, b):
    return lax.dot_general(a, b, (((1,), (1,)), ((), ())), preferred_element_type=F32)


def dot_tn(a, b):
    return lax.dot_general(a, b, (((0,), (0,)), ((), ())), preferred_element_type=F32)


def dot_nn(a, b):
    return jnp.dot(a, b, preferred_element_type=F32)


def cost(microseconds):
    return pl.CostEstimate(
        flops=0, transcendentals=0, bytes_accessed=int(microseconds * 3_000_000)
    )


VMEM = pl.BlockSpec(memory_space=pltpu.VMEM)
SMEM = pl.BlockSpec(memory_space=pltpu.SMEM)
HBM = pl.BlockSpec(memory_space=pltpu.HBM)
ANY = pl.BlockSpec(memory_space=pl.ANY)


def in_vmem(value):
    return pltpu.with_memory_space_constraint(value, pltpu.VMEM)


def in_hbm(value):
    return pltpu.with_memory_space_constraint(value, pltpu.HBM)


def position():
    tp, sub = lax.axis_index("tp"), lax.axis_index("sub")
    subs = lax.axis_size("sub")
    return tp * subs + sub, tp, sub, lax.axis_index("pool"), subs


def far_first(k, count):
    return (count - k) % count


def call(kernel, name, inputs, specs, outs, out_specs=None, scratch=(), loads=(), anchors=(), us=2, roomy=False, begins=False):
    count_in, count_out, count_load = len(inputs), len(outs), len(loads)

    def source(ref, first):
        return ref if first is None else ref.at[:, first : first + CHUNK, :]

    def run(*refs):
        refs = list(refs)
        given = [refs.pop(0) for _ in range(count_in)]
        sources = [refs.pop(0) for _ in range(count_load)]
        del refs[: len(anchors)]
        results = [refs.pop(0) for _ in range(count_out)]
        targets = [refs.pop(0) for _ in range(count_load)]
        copies = []
        if loads:
            sems = refs.pop()
            for i, (_, first) in enumerate(loads):
                copies.append(
                    pltpu.make_async_copy(source(sources[i], first), targets[i], sems.at[i])
                )

        def begin():
            if copies:

                @pl.when(lax.axis_index("tp") >= 0)
                def _():
                    for copy in copies:
                        copy.start()

        if begins:
            kernel(begin, *given, *results, *refs)
        else:
            begin()
            kernel(*given, *results, *refs)
        for copy in copies:
            copy.wait()

    def loaded(array, first):
        shape = array.shape if first is None else (array.shape[0], CHUNK, array.shape[2])
        return pltpu.VMEM(shape, array.dtype)

    if not roomy:
        outs = [
            leaf if spec is HBM else pltpu.VMEM(leaf.shape, leaf.dtype)
            for leaf, spec in zip(outs, out_specs or [VMEM] * count_out)
        ]
    scratch = list(scratch) + ([pltpu.SemaphoreType.DMA((count_load,))] if loads else [])
    results = pl.pallas_call(
        run,
        in_specs=list(specs) + [HBM] * count_load + [ANY] * len(anchors),
        out_specs=list(out_specs or [VMEM] * count_out) + [VMEM] * count_load,
        out_shape=list(outs) + [loaded(*leaf) for leaf in loads],
        scratch_shapes=scratch,
        compiler_params=pltpu.CompilerParams(vmem_limit_bytes=(48 if roomy else 12) << 20),
        cost_estimate=cost(us),
        name=name,
    )(*inputs, *[in_hbm(leaf[0]) for leaf in loads], *anchors)
    return list(results[:count_out]), list(results[count_out:])


def attention_kernel(
    begin, q_hbm, lengths_hbm, route_hbm, share_hbm, k_hbm, v_hbm, *refs, pieces
):
    where = position()
    outs, facts_ref = refs[:pieces], refs[pieces]
    lengths, q_ref, route_ref, share_ref, k_ref, v_ref, sems, spread, gathered, flat = refs[
        pieces + 1 :
    ]
    rows, heads, _ = gathered.shape
    positions = k_ref.shape[1]
    group = heads // KV_HEADS
    small = [
        pltpu.make_async_copy(q_hbm, q_ref, sems.at[rows, 0]),
        pltpu.make_async_copy(lengths_hbm, lengths, sems.at[rows, 1]),
        pltpu.make_async_copy(route_hbm, route_ref, sems.at[rows + 1, 0]),
        pltpu.make_async_copy(share_hbm, share_ref, sems.at[rows + 1, 1]),
    ]
    for copy in small:
        copy.start()
    copies = []
    for row in range(rows):
        pair = [
            pltpu.make_async_copy(k_hbm.at[row], k_ref.at[row], sems.at[row, 0]),
            pltpu.make_async_copy(v_hbm.at[row], v_ref.at[row], sems.at[row, 1]),
        ]
        pair[0].start()
        pair[1].start()
        copies.append(pair)
    begin()
    for copy in small:
        copy.wait()
    share = share_ref[...]
    high = share.astype(BF16).astype(F32)
    middle = (share - high).astype(BF16).astype(F32)
    block = jnp.concatenate([route_ref[...].astype(F32), high, middle, share - high - middle], axis=0)
    count, lanes = block.shape[1], facts_ref.shape[1]
    block = jnp.concatenate([block, jnp.zeros((block.shape[0], -count % 128), F32)], axis=1).T
    blank = jnp.zeros((count, lanes - block.shape[1]), F32)
    facts_ref[...] = jnp.concatenate([block[:count], blank], axis=1).astype(BF16)
    queries = q_ref[...].astype(F32)
    for h in range(heads):
        spread[:, h, :] = queries[:, h * HEAD_DIM : (h + 1) * HEAD_DIM]
    column = lax.broadcasted_iota(jnp.int32, (group, positions), 1)
    for pair in copies:
        pair[0].wait()
        pair[1].wait()
    cases = [(row, j) for row in range(rows) for j in range(KV_HEADS)]
    lanes = [slice(j * HEAD_DIM, (j + 1) * HEAD_DIM) for j in range(KV_HEADS)]
    scores, terms, totals = [], [], []
    for row, j in cases:
        own = spread[row, j * group : (j + 1) * group, :].astype(BF16)
        scores.append(dot_nt(own, k_ref[row, :, lanes[j]]))
    for (row, j), score in zip(cases, scores):
        valid = column < lengths[row]
        score = jnp.where(valid, score * (1.0 / math.sqrt(HEAD_DIM)), -1e30)
        top = jnp.max(score, axis=1, keepdims=True)
        terms.append(jnp.where(valid, jnp.exp(score - top), 0.0))
        totals.append(jnp.sum(terms[-1], axis=1, keepdims=True))
    for (row, j), term, total in zip(cases, terms, totals):
        value = dot_nn(term.astype(BF16), v_ref[row, :, lanes[j]]) / total
        gathered[row, j * group : (j + 1) * group, :] = value
    for h in range(heads):
        flat[:, h * HEAD_DIM : (h + 1) * HEAD_DIM] = gathered[:, h, :]
    width = heads * HEAD_DIM // pieces
    for k in range(pieces):
        start = pl.multiple_of(((where[0] ^ k) if pieces > 1 else 0) * width, width)
        outs[k][...] = flat[:, pl.ds(start, width)].astype(BF16)


def attend(queries, keys_cache, values_cache, lengths, facts, pieces, loads, roomy):
    rows, columns = queries.shape
    heads = columns // HEAD_DIM
    return call(
        functools.partial(attention_kernel, pieces=pieces),
        "attention",
        [in_hbm(a) for a in (queries, lengths, *facts, keys_cache, values_cache)],
        [HBM] * 6,
        [jax.ShapeDtypeStruct((rows, columns // pieces), BF16)] * pieces
        + [jax.ShapeDtypeStruct((facts[0].shape[1], FACT_LANES), BF16)],
        scratch=[
            pltpu.SMEM((rows,), jnp.int32),
            pltpu.VMEM(queries.shape, BF16),
            pltpu.VMEM(facts[0].shape, jnp.int32),
            pltpu.VMEM(facts[1].shape, F32),
            pltpu.VMEM(keys_cache.shape, BF16),
            pltpu.VMEM(values_cache.shape, BF16),
            pltpu.SemaphoreType.DMA((rows + 2, 2)),
            pltpu.VMEM((rows, heads, HEAD_DIM), F32),
            pltpu.VMEM((rows, heads, HEAD_DIM), F32),
            pltpu.VMEM((rows, columns), F32),
        ],
        loads=loads,
        us=4,
        roomy=roomy,
        begins=True,
    )


def route_kernel(table_ref, *refs, sources, experts, top):
    where = position()
    given, (slot_ref, weight_ref, largest_ref, extra_ref, *picks, held) = refs[:sources], refs[sources:]
    pools, pool_rows, lanes = held.shape
    if sources == 1:
        held[...] = given[0][...].astype(F32)
    else:
        for k in range(sources):
            width = given[k].shape[1]
            held[where[3] ^ far_first(k, sources)] = given[k][:, width - lanes :].astype(F32)
    rows = pools * pool_rows
    total = table_ref.shape[1]
    groups, _, lanes = slot_ref.shape
    group = lanes // rows
    facts = held[...].reshape(rows, held.shape[2]).T
    shares = facts[top : 2 * top] + facts[2 * top : 3 * top] + facts[3 * top : 4 * top]
    routes = jnp.concatenate([facts[i : i + 1] for i in range(top)], axis=1).astype(jnp.int32)
    ids = lax.broadcasted_iota(jnp.int32, (total, top * rows), 0)
    hot = jnp.where(ids == routes, 1.0, 0.0).astype(BF16)
    table = jnp.broadcast_to(table_ref[...].astype(F32), (8, total)).astype(BF16)
    entry = dot_nn(table, hot)[0:1].astype(jnp.int32)

    first = lax.broadcasted_iota(jnp.int32, (pools, top * rows), 0) * experts
    inside = jnp.where((entry >= first) & (entry < first + experts), 1.0, 0.0)
    loads = jnp.sum(inside, axis=1, keepdims=True)
    largest_ref[...] = jnp.max(loads, axis=0, keepdims=True).astype(jnp.int32)
    extra_ref[...] = largest_ref[...] - picks[0].shape[0]

    lane = lax.broadcasted_iota(jnp.int32, (groups, lanes), 1)
    block = lax.broadcasted_iota(jnp.int32, (groups, lanes), 0)
    wanted = where[3] * experts + block * group + lane // rows
    weight = jnp.zeros((groups, lanes), F32)
    mask = jnp.zeros((groups, lanes), F32)
    for i in range(top):
        named = jnp.concatenate([entry[:, i * rows : (i + 1) * rows]] * group, axis=1)
        value = jnp.concatenate([shares[i : i + 1]] * group, axis=1)
        match = wanted == named
        mask = mask + jnp.where(match, 1.0, 0.0)
        weight = weight + jnp.where(match, value, 0.0)
    earlier = lax.broadcasted_iota(jnp.int32, (lanes, lanes), 0)
    later = lax.broadcasted_iota(jnp.int32, (lanes, lanes), 1)
    before = jnp.where(earlier < later, 1.0, 0.0).astype(BF16)
    rank = dot_nn(mask.astype(BF16), before)
    base = jnp.zeros((1, 1), F32)
    counts = jnp.sum(mask, axis=1, keepdims=True)
    slots = []
    for g in range(groups):
        slots.append(jnp.where(mask[g : g + 1] > 0.0, rank[g : g + 1] + base, -1.0))
        slot_ref[g] = slots[g].astype(jnp.int32)
        weight_ref[g] = weight[g : g + 1]
        base = base + counts[g : g + 1]
    fill_picks(slots, [weight[g : g + 1] for g in range(groups)], *picks)


def fill_picks(slots, weights, pick_ref, spread_ref, slot_weight_ref):
    groups, lanes = len(slots), slots[0].shape[1]
    capacity = pick_ref.shape[0]
    rows = jnp.concatenate(slots + [slots[0]] * (-groups % 8), axis=0).T
    place = lax.broadcasted_iota(jnp.int32, (capacity, lanes), 0).astype(F32)
    along = lax.broadcasted_iota(jnp.int32, (lanes, capacity), 1).astype(F32)
    total = jnp.zeros((capacity, lanes), F32)
    for g in range(groups):
        hit = place == slots[g]
        part = slice(g * lanes, (g + 1) * lanes)
        pick_ref[:, part] = jnp.where(hit, 1.0, 0.0).astype(BF16)
        spread_ref[part, :] = jnp.where(along == rows[:, g : g + 1], 1.0, 0.0).astype(BF16)
        total = total + jnp.where(hit, weights[g], 0.0)
    slot_weight_ref[...] = jnp.sum(total, axis=1, keepdims=True)


def pick_shapes(capacity, pairs):
    return [
        jax.ShapeDtypeStruct((capacity, pairs), BF16),
        jax.ShapeDtypeStruct((pairs, capacity), BF16),
        jax.ShapeDtypeStruct((capacity, 1), F32),
    ]


def route(blocks, expert_table, experts, rows, top, capacity, pools, loads, roomy):
    group = max(1, min(experts, 256 // rows))
    shape = (experts // group, 1, group * rows)
    results, held = call(
        functools.partial(route_kernel, sources=len(blocks), experts=experts, top=top),
        "route",
        [expert_table.reshape(1, -1), *blocks],
        [VMEM] + [VMEM] * len(blocks),
        [
            jax.ShapeDtypeStruct(shape, jnp.int32),
            jax.ShapeDtypeStruct(shape, F32),
            jax.ShapeDtypeStruct((1, 1), jnp.int32),
            jax.ShapeDtypeStruct((1, 1), jnp.int32),
            *pick_shapes(capacity, experts * rows),
        ],
        scratch=[pltpu.VMEM((pools, rows // pools, FACT_LANES), F32)],
        loads=loads,
        us=6,
        roomy=roomy,
    )
    return results[:4], results[4:], held


def pick_slots(shift, slots, weights, capacity):
    def kernel(shift_ref, *refs):
        slot_ref, weight_ref, *picks = refs
        groups = range(slot_ref.shape[0])
        shifted = [(slot_ref[g] - shift_ref[0]).astype(F32) for g in groups]
        fill_picks(shifted, [weight_ref[g] for g in groups], *picks)

    return call(
        kernel,
        "pick",
        [shift.reshape(1), slots, weights],
        [SMEM, VMEM, VMEM],
        pick_shapes(capacity, slots.shape[0] * slots.shape[2]),
        roomy=True,
    )[0]


def project_kernel(*refs, sources):
    where = position()
    inputs, (w_ref, kept, near, far) = refs[:sources], refs[sources:]
    own_rows = inputs[0].shape[0]
    count = sources * own_rows
    half = kept.shape[1]
    stacked = jnp.concatenate([ref[...].astype(F32) for ref in inputs], axis=0).astype(BF16)
    target = lax.broadcasted_iota(jnp.int32, (count, count), 0)
    origin = lax.broadcasted_iota(jnp.int32, (count, count), 1)
    order = (target ^ (where[0] * own_rows)) == origin
    x = dot_nn(jnp.where(order, 1.0, 0.0).astype(BF16), stacked).astype(BF16)
    for k, out in ((1, far), (0, near)):
        start = pl.multiple_of((where[1] ^ k) * half, half)
        value = dot_nn(x, w_ref[:, pl.ds(start, half)])
        out[...] = value.astype(BF16)
        if k == 0:
            kept[...] = value


def project(inputs, out_weight):
    sources = len(inputs)
    shape = (sources * inputs[0].shape[0], out_weight.shape[1] // 2)
    return call(
        functools.partial(project_kernel, sources=sources),
        "project",
        [*inputs, out_weight],
        [VMEM] * (sources + 1),
        [jax.ShapeDtypeStruct(shape, kind) for kind in (F32, BF16, BF16)],
    )[0]


def add_kernel(kept, facts, *refs):
    half = kept.shape[1]
    total = kept[...]
    for ref in refs[:-1]:
        total = total + ref[...].astype(F32)
    refs[-1][:, :half] = total.astype(BF16)
    refs[-1][:, half:] = facts[...]


def add(kept, facts, others):
    outs = [jax.ShapeDtypeStruct((kept.shape[0], kept.shape[1] + facts.shape[1]), BF16)]
    return call(add_kernel, "add", [kept, facts, *others], [VMEM] * (2 + len(others)), outs)[0][0]


def gate_up_kernel(*refs, sources, first, index):
    where = position()
    inputs, refs = refs[:sources], refs[sources:]
    pick_ref, g_ref, u_ref, out_ref = refs[:4]
    if first:
        columns_ref, mine_ref, theirs_ref, x, both = refs[4:]
        count = inputs[0].shape[0]
        own_rows = mine_ref.shape[0]
        row = lax.broadcasted_iota(jnp.int32, (own_rows, count), 0)
        place = lax.broadcasted_iota(jnp.int32, (own_rows, count), 1)
        for out, shard in ((mine_ref, where[0]), (theirs_ref, where[0] ^ where[4])):
            chosen = jnp.where(place == row + shard * own_rows, 1.0, 0.0).astype(BF16)
            out[...] = dot_nn(chosen, inputs[0][:, : x.shape[1]]).astype(BF16)
        for k in range(sources):
            start = 0
            if sources > 1:
                start = pl.multiple_of((where[3] ^ far_first(k, sources)) * count, count)
            x[pl.ds(start, count), :] = inputs[k][:, : x.shape[1]].astype(F32)
        columns_ref[...] = x[...].T.astype(BF16)
    else:
        (columns_ref,), (both,) = inputs, refs[4:]
    experts, _, depth = g_ref.shape
    rows = columns_ref.shape[1]
    for base, w_ref in ((0, g_ref), (CHUNK, u_ref)):
        units = slice(index * CHUNK, (index + 1) * CHUNK) if w_ref.shape[1] > CHUNK else slice(None)
        value = dot_nn(w_ref[:, units, :].reshape(experts * CHUNK, depth), columns_ref[...]).astype(BF16)
        for e in range(experts):
            both[base : base + CHUNK, e * rows : (e + 1) * rows] = value[
                e * CHUNK : (e + 1) * CHUNK
            ]
    out_ref[...] = dot_nt(pick_ref[...], both[...]).astype(BF16)


def gate_up(xs, pick, w_gate, w_up, index, own_rows, loads, roomy, anchors=()):
    first = index == 0
    experts, _, depth = w_gate.shape
    rows = pick.shape[1] // experts
    outs = [jax.ShapeDtypeStruct((pick.shape[0], 2 * CHUNK), BF16)]
    scratch = [pltpu.VMEM((2 * CHUNK, experts * rows), BF16)]
    if first:
        outs.append(jax.ShapeDtypeStruct((depth, rows), BF16))
        outs += [jax.ShapeDtypeStruct((own_rows, depth), BF16)] * 2
        scratch.insert(0, pltpu.VMEM((rows, depth), F32))
    results, held = call(
        functools.partial(gate_up_kernel, sources=len(xs), first=first, index=index),
        f"gate_up_{index}",
        [*xs, pick, w_gate, w_up],
        [VMEM] * (len(xs) + 3),
        outs,
        scratch=scratch,
        loads=loads,
        anchors=anchors,
        us=4,
        roomy=roomy,
    )
    return results[0], results[1:2] if first else xs, results[2:], held


def down_kernel(own_ref, other_ref, weight_ref, spread_ref, d_ref, *refs, carried, index):
    before, outs = refs[:carried], refs[carried:]
    experts, _, depth = d_ref.shape
    rows = spread_ref.shape[0] // experts
    both = own_ref[...].astype(F32) + other_ref[...].astype(F32)
    gate, up = both[:, :CHUNK], both[:, CHUNK:]
    hidden = (gate / (1.0 + jnp.exp(-gate)) * up * weight_ref[...]).astype(BF16)
    spread = dot_nn(spread_ref[...], hidden).astype(BF16)
    left = jnp.concatenate([spread[e * rows : (e + 1) * rows] for e in range(experts)], axis=1)
    units = slice(index * CHUNK, (index + 1) * CHUNK)
    total = dot_nn(left, d_ref[:, units, :].reshape(experts * CHUNK, depth))
    if carried:
        total = total + before[0][...]
    if len(outs) == 1:
        outs[0][...] = total
    else:
        half = depth // 2
        low, high = total[:, :half], total[:, half:]
        mine = lax.axis_index("sub") == 0
        outs[0][...] = jnp.where(mine, low, high)
        outs[1][...] = jnp.where(mine, high, low)


def down(own, other, slot_weight, spread, w_down, before, index, halved, roomy):
    experts, _, depth = w_down.shape
    rows = spread.shape[0] // experts
    carried = [] if before is None else [before]
    parts = 2 if halved else 1
    return call(
        functools.partial(down_kernel, carried=len(carried), index=index),
        f"down_{index}",
        [own, other, slot_weight, spread, w_down, *carried],
        [VMEM] * (5 + len(carried)),
        [jax.ShapeDtypeStruct((rows, depth // parts), F32)] * parts,
        us=3,
        roomy=roomy,
    )[0]


def load(loads, anchors, name, roomy=False):
    return call(
        lambda: None, name, [], [], [], loads=loads, anchors=anchors, us=2 * len(loads), roomy=roomy
    )[1]


def arrange_kernel(*refs):
    inputs, out_ref = refs[:-1], refs[-1]
    count = inputs[0].shape[0]
    for k, ref in enumerate(inputs):
        start = pl.multiple_of((lax.axis_index("pool") ^ far_first(k, len(inputs))) * count, count)
        out_ref[pl.ds(start, count), :] = ref[:, : out_ref.shape[1]]


def arrange(blocks, width):
    shape = (len(blocks) * blocks[0].shape[0], width)
    outs = [jax.ShapeDtypeStruct(shape, BF16)]
    return call(arrange_kernel, "arrange", blocks, [VMEM] * len(blocks), outs, roomy=True)[0][0]


def halves_kernel(value_ref, own_ref, other_ref):
    half = own_ref.shape[1]
    low, high = value_ref[:, :half], value_ref[:, half:]
    mine = lax.axis_index("sub") == 0
    own_ref[...] = jnp.where(mine, low, high)
    other_ref[...] = jnp.where(mine, high, low)


def halves(value):
    outs = [jax.ShapeDtypeStruct((value.shape[0], value.shape[1] // 2), F32)] * 2
    return call(halves_kernel, "halves", [value], [VMEM], outs, roomy=True)[0]


def join_kernel(mine_ref, theirs_ref, out_hbm, out_ref, sem):
    half = mine_ref.shape[1]
    low = lax.axis_index("tp") == 0
    mine, theirs = mine_ref[...].astype(F32), theirs_ref[...].astype(F32)
    out_ref[:, :half] = jnp.where(low, mine, theirs).astype(BF16)
    out_ref[:, half:] = jnp.where(low, theirs, mine).astype(BF16)
    copy = pltpu.make_async_copy(out_ref, out_hbm, sem)
    copy.start()
    copy.wait()


def join(mine, theirs):
    shape = (mine.shape[0], 2 * mine.shape[1])
    return call(
        join_kernel,
        "join",
        [mine, theirs],
        [VMEM, VMEM],
        [jax.ShapeDtypeStruct(shape, BF16)],
        out_specs=[HBM],
        scratch=[pltpu.VMEM(shape, BF16), pltpu.SemaphoreType.DMA],
    )[0][0]


def split_kernel(own_ref, other_ref, *outs):
    count = outs[0].shape[0]
    pool = lax.axis_index("pool")
    for k in range(len(outs)):
        row = pl.ds(pl.multiple_of((pool ^ k) * count, count), count)
        outs[k][...] = (own_ref[row, :] + other_ref[row, :]).astype(outs[k].dtype)


def split(own, other, pieces):
    shape = (own.shape[0] // pieces, own.shape[1])
    return call(
        split_kernel,
        "split",
        [own, other],
        [VMEM, VMEM],
        [jax.ShapeDtypeStruct(shape, F32 if k == 0 else BF16) for k in range(pieces)],
    )[0]


def xor_permute(value, axes, count, k):
    return lax.ppermute(value, axes, [(i, i ^ k) for i in range(count)])


def body(
    queries,
    keys_cache,
    values_cache,
    lengths,
    out_weight,
    routes,
    route_weight,
    expert_table,
    w_gate,
    w_up,
    w_down,
):
    pools, tps, subs = lax.axis_size("pool"), lax.axis_size("tp"), lax.axis_size("sub")
    pool, tp, sub = lax.axis_index("pool"), lax.axis_index("tp"), lax.axis_index("sub")
    shards = tps * subs
    shard = tp * subs + sub
    direct = tps == 2 and subs == 2 and pools == 4
    own_rows = queries.shape[0]
    pool_rows = own_rows * shards
    rows = pool_rows * pools
    experts, hidden_units, half_width = w_gate.shape
    top = routes.shape[1]

    capacity = -(-rows * top * 13 // (8 * pools * 16)) * 16
    gates, ups, downs = [
        [(w, c) for c in range(0, hidden_units, CHUNK)] for w in (w_gate, w_up, w_down)
    ]
    chunks = len(gates)

    if direct:
        axes = ("tp", "sub")
        (*pieces, facts), _ = attend(
            queries,
            keys_cache,
            values_cache,
            lengths,
            (routes.T, route_weight.T),
            shards,
            [],
            False,
        )
        inputs = [pieces[0]] + [xor_permute(pieces[k], axes, shards, k) for k in range(1, shards)]
        (out_held,) = load([(out_weight, None)], [pieces[0]], "load_a")
        kept, near, far = project(inputs, out_held)
        gate_1, up_1 = gate_2, up_2 = in_vmem(w_gate), in_vmem(w_up)
        (gate_0,) = load([gates[0]], [near], "load_b")
        others = [
            xor_permute(near if k < subs else far, axes, shards, k) for k in range(1, shards)
        ]
        x_half, gate_0 = lax.optimization_barrier((add(kept, facts, others), gate_0))
        (up_0,) = load([ups[0]], [x_half], "load_c")
        xs = [x_half]
        for k in range(1, pools):
            xs.append(xor_permute(x_half, "pool", pools, far_first(k, pools)))
        (slots, weights, largest, extra_pairs), (pick, spread, slot_weight), _ = route(
            xs,
            expert_table,
            experts,
            rows,
            top,
            capacity,
            pools,
            [],
            False,
        )
        held = [(gate_0, up_0), (gate_1, up_1), (gate_2, up_2)]
        sent, given = [], xs
        for c in range(chunks):
            value, given, rest, _ = gate_up(
                given, pick, *held[c], c, own_rows, [], False, sent[-1:]
            )
            if c == 0:
                mine, theirs = rest
            sent.append(value)
        theirs, _ = lax.optimization_barrier((theirs, sent[-1]))
        theirs = lax.ppermute(theirs, "tp", [(0, 1), (1, 0)])
    else:
        (attention, facts), _ = attend(
            queries,
            keys_cache,
            values_cache,
            lengths,
            (routes.T, route_weight.T),
            1,
            [],
            True,
        )
        blocks = lax.all_gather(facts, "pool", axis=0)
        (slots, weights, largest, extra_pairs), (pick, spread, slot_weight), _ = route(
            [blocks], expert_table, experts, rows, top, capacity, pools, [], True
        )
        head_rows = lax.all_to_all(
            attention, ("tp", "sub"), split_axis=1, concat_axis=0, tiled=True
        )
        partial = jnp.dot(head_rows, out_weight, preferred_element_type=F32)
        x_sum = lax.psum_scatter(partial, ("tp", "sub"), scatter_dimension=1, tiled=True)
        x_pool = x_sum.astype(BF16)
        attended = lax.all_to_all(x_pool, ("tp", "sub"), split_axis=0, concat_axis=1, tiled=True)
        x_part = lax.all_gather(x_pool, "pool", axis=0, tiled=True)
        xs = [lax.all_gather(x_part, "sub", axis=1, tiled=True)]
        held = load(gates + ups, [], "load")
        sent, given = [], xs
        for c in range(chunks):
            value, given, *_ = gate_up(
                given, pick, held[c], held[chunks + c], c, own_rows, [], True
            )
            sent.append(value)

    def exchange(value):
        if tps == 2:
            return value, lax.ppermute(value, "tp", [(0, 1), (1, 0)])
        return lax.psum(value.astype(F32), "tp").astype(BF16), jnp.zeros_like(value)

    def combine(halved, extra=None):
        if not direct:
            value = lax.psum_scatter(halved[0], "pool", scatter_dimension=0, tiled=True)
            return lax.psum_scatter(value, "sub", scatter_dimension=1, tiled=True)
        own, other = halved
        received = xor_permute(other, "sub", subs, 1)
        if extra is not None:
            received, extra = lax.optimization_barrier((received, extra))
        pieces = split(own, received, pools)
        total = pieces[0]
        for k in range(1, pools):
            far = far_first(k, pools)
            total = total + xor_permute(pieces[far], "pool", pools, far).astype(F32)
        return total if extra is None else total + extra

    def more(state):
        left, total = state
        left, *held_x = lax.optimization_barrier((left, *xs))
        x = arrange(held_x, half_width) if direct else held_x[0]
        pick, spread, slot_weight = pick_slots(largest[0, 0] - left, slots, weights, capacity)
        gate = jnp.einsum("rd,efd->erf", x, w_gate, preferred_element_type=F32)
        up = jnp.einsum("rd,efd->erf", x, w_up, preferred_element_type=F32)
        both = jnp.concatenate([gate, up], axis=2).astype(BF16)
        both = both.reshape(experts * rows, 2 * hidden_units)
        sent = jnp.dot(pick, both, preferred_element_type=F32).astype(BF16)
        if tps == 2:
            both = sent.astype(F32) + lax.ppermute(sent, "tp", [(0, 1), (1, 0)]).astype(F32)
        else:
            both = lax.psum(sent.astype(F32), "tp")
        hidden = jax.nn.silu(both[:, :hidden_units]) * both[:, hidden_units:] * slot_weight
        spread = jnp.dot(spread, hidden.astype(BF16), preferred_element_type=F32).astype(BF16)
        spread = spread.reshape(experts, rows, hidden_units)
        value = jnp.einsum("erf,efd->rd", spread, w_down, preferred_element_type=F32)
        value = halves(value) if direct else [value]
        return left - capacity, total + combine(value)

    both = [exchange(value) for value in sent]
    result = [None]
    for c in range(chunks):
        last = direct and c == chunks - 1
        result = down(
            *both[c], slot_weight, spread, in_vmem(w_down), result[0], c, last, not direct
        )
    if direct:
        theirs, extra_pairs, *result = lax.optimization_barrier(
            (theirs, extra_pairs, *result)
        )
        attended = join(mine, theirs)
    _, extra = lax.while_loop(
        lambda state: state[0] > 0,
        more,
        (extra_pairs[0, 0], jnp.zeros((pool_rows, half_width // subs), F32)),
    )
    if direct:
        return attended, combine(result, extra).astype(BF16)
    return attended, (combine(result) + extra).astype(BF16)


def solution(mesh):
    in_specs = (
        P(("grp", "pool", "tp", "sub"), None),
        P(("grp", "pool", "tp", "sub"), None, None),
        P(("grp", "pool", "tp", "sub"), None, None),
        P(("grp", "pool", "tp", "sub")),
        P(("tp", "sub"), None),
        P(("grp", "pool"), None),
        P(("grp", "pool"), None),
        P(),
        P("pool", "sub", "tp"),
        P("pool", "sub", "tp"),
        P("pool", "sub", "tp"),
    )
    out_specs = (P(("grp", "pool", "tp", "sub"), None), P(("grp", "pool"), ("tp", "sub")))
    return jax.shard_map(body, mesh=mesh, in_specs=in_specs, out_specs=out_specs, check_vma=False)
```
